32 devices in a mesh: rep: 4 (over z), shard: 8 (over y, x, core).
Axes of the slice: x: 2, y: 2, z: 4, core: 2. Of those that a mesh axis runs over, the one named last changes fastest.
Arguments:
- tokens: bfloat16 [8192, 1024], P(('rep', 'shard')), may hold values from -6 to 6
- prefix: int32 [32], P(('rep', 'shard')), may hold values from 25 to 128
- routes: int32 [8192, 8], P(('rep', 'shard')), may hold values from 0 to 31, all different within a row; in each aligned block of 256 rows (0 to 255, 256 to 511, ...) at most 96 rows name the same one
- cotangent: bfloat16 [8192, 1024], P(('rep', 'shard')), may hold values from -6 to 6
- w_query: bfloat16 [1024, 1024], P('shard'), may hold values from -0.625 to 0.625
- key_weight: bfloat16 [1024, 512], P('shard'), may hold values from -0.625 to 0.625
- value_weight: bfloat16 [1024, 512], P('shard'), may hold values from -0.1875 to 0.1875
- w_out: bfloat16 [1024, 1024], P('shard'), may hold values from -6 to 6
- norm_attn: bfloat16 [1024], P('shard'), may hold values from 0.5 to 1.5
- norm_moe: bfloat16 [1024], P('shard'), may hold values from 0.5 to 1.5
- w_router: bfloat16 [1024, 32], P('shard'), may hold values from -0.09375 to 0.09375
- w_gate: bfloat16 [32, 1024, 512], P('shard'), may hold values from -0.1875 to 0.1875
- w_up: bfloat16 [32, 1024, 512], P('shard'), may hold values from -0.1875 to 0.1875
- w_down: bfloat16 [32, 512, 1024], P('shard'), may hold values from -6 to 6
Outputs:
- layer_out: bfloat16 [8192, 1024], P(('rep', 'shard'))
- d_tokens: float32 [8192, 1024], P(('rep', 'shard'))
- d_w_query: float32 [1024, 1024], P('shard')
- d_w_key: float32 [1024, 512], P('shard')
- d_w_value: float32 [1024, 512], P('shard')
- d_w_out: float32 [1024, 1024], P('shard')
- d_norm_attn: float32 [1024], P('shard')
- d_norm_moe: float32 [1024], P('shard')
- d_w_router: float32 [1024, 32], P('shard')
- d_w_gate: float32 [32, 1024, 512], P('shard')
- d_w_up: float32 [32, 1024, 512], P('shard')
- d_w_down: float32 [32, 512, 1024], P('shard')
The draws below stay inside these ranges and needn't reach their ends.
Inputs may be any that keep to these rules, and one draw needn't show every extreme that they name: `routes`: each row names 8 different experts; among the rows of one device no expert is named more than 96 times, and in every draw some device's rows name some expert exactly 96 times.
All inputs are finite; a program needn't handle non-finite values.
Results may differ from the reference program's by a relative error of at most 0.024.
Values may be sent and summed in bfloat16 or wider, within the bound.
A program may use at most 256 MiB of HBM per device.

```python
import math
import jax
import jax.numpy as jnp
import numpy as np
from jax import lax

MODEL_WIDTH = 1024
QUERY_HEADS = 16
KEY_VALUE_HEADS = 8
HEAD_SIZE = 64
EXPERTS = 32
TOP = 8
F = 512
TOKENS_PER_CARD = 256
CAP = 96
SEQS = 32
TOKENS = 8192


def set_ends(values, stream_key, smallest, largest):
    extent = values.shape
    index_at = [jax.random.randint(jax.random.fold_in(stream_key, axis), (), 0, extent[axis]) for axis in range(len(extent))]
    values = values.at[tuple(index_at)].set(smallest)
    longest = extent.index(max(extent))
    index_at[longest] = (index_at[longest] + 1) % extent[longest]
    return values.at[tuple(index_at)].set(largest)


def level_of(key, shape, pieces, low, high):
    gain = 1.0
    for axis_at, blocks in pieces:
        heights = jax.random.uniform(jax.random.fold_in(jax.random.fold_in(key, 6), axis_at), (blocks,), jnp.float32, low / len(pieces), high / len(pieces))
        gain = gain * jnp.repeat(jnp.exp(heights), shape[axis_at] // blocks).reshape((-1,) + (1,) * (len(shape) - 1 - axis_at))
    return gain


def routed_block(stream_key, own, number, rows, count, top, reach, skew):
    sequence = jax.random.permutation(stream_key, count)
    packed, ordinary = portions_of(count, rows * top, reach, skew, True), portions_of(count, rows * top, reach, skew, False)
    places = jnp.arange(count)

    def named(lengths, turn):
        used = int((lengths > 0).sum())
        fixed = max(1, used // 4)
        passed = fixed + (places - fixed + turn * (used - fixed)) % max(1, count - fixed)
        return jnp.zeros((count,), jnp.int32).at[sequence[jnp.where(places < fixed, places, passed)]].set(jnp.asarray(lengths, jnp.int32))

    lengths = jnp.where(number % 4 == 0, named(packed, number // 4), named(ordinary, number - number // 4 - 1))
    mixed = jax.random.permutation(jax.random.fold_in(own, 3), count)
    donor, sink = mixed[0:count // 2 * 2:2], mixed[1:count // 2 * 2:2]
    slack = jnp.minimum(lengths[donor] - 1, reach - lengths[sink]) // 2
    slack = jnp.where((donor == sequence[0]) | (sink == sequence[0]) | (lengths[sink] == 0), 0, jnp.maximum(slack, 0))
    passed = jax.random.randint(jax.random.fold_in(own, 4), (count // 2,), 0, 1 << 20) % (slack + 1)
    lengths = lengths.at[donor].add(-passed).at[sink].add(passed)
    members = jnp.searchsorted(jnp.cumsum(lengths), jnp.arange(rows * top), side="right").astype(jnp.int32)
    table = members.reshape(top, rows).T
    table = table[jax.random.permutation(jax.random.fold_in(own, 1), rows)]
    turn = jax.random.randint(jax.random.fold_in(own, 2), (rows, 1), 0, top)
    return jnp.take_along_axis(table, (jnp.arange(top)[None, :] + turn) % top, axis=1)


def portions_of(number_of, total, reach, lean, full):
    weights = [(1 << 20) // math.isqrt(rank ** lean) + 1 for rank in range(1, number_of + 1)]
    largest = reach if full else min(reach, max(-(-total // number_of), total * weights[0] // sum(weights)))
    least = 1 if total - largest >= number_of - 1 else 0
    given, rest = [largest] + [least] * (number_of - 1), total - largest - least * (number_of - 1)
    while rest > 0:
        movable = [i for i in range(1, number_of) if given[i] < largest] or [i for i in range(1, number_of) if given[i] < reach]
        mass, budget = sum([weights[i] for i in movable]), rest
        for i in movable:
            addition = min(reach - given[i], max(1, budget * weights[i] // mass), rest)
            given[i] = given[i] + addition
            rest = rest - addition
    return np.array(given)


def centred(key, dims, width, limit, cuts=(), kind=jnp.bfloat16):
    entries = width * jax.random.normal(key, dims, jnp.float32)
    if cuts:
        entries = entries * level_of(key, dims, cuts, -0.22, 0.18)
    return jnp.clip(entries, -limit, limit).astype(kind)


def setup_inputs(seed: int = 0) -> dict:
    key_of = jax.random.split(jax.random.key(seed), 15)
    tokens = centred(key_of[0], (TOKENS, MODEL_WIDTH), 1.0, 6.0, ((0, 32),))
    prefix = set_ends(jax.random.randint(key_of[1], (SEQS,), TOKENS_PER_CARD // 10, TOKENS_PER_CARD // 2 + 1), jax.random.fold_in(key_of[1], 1), TOKENS_PER_CARD // 10, (TOKENS_PER_CARD // 2 + 1) - 1).astype(jnp.int32)
    routes_keys = jax.random.split(jax.random.fold_in(key_of[2], 1), TOKENS // TOKENS_PER_CARD)
    routes_turns = jax.random.permutation(jax.random.fold_in(key_of[2], 3), TOKENS // TOKENS_PER_CARD)
    routes = jax.vmap(lambda own, number: routed_block(jax.random.fold_in(key_of[2], 2), own, number, TOKENS_PER_CARD, EXPERTS, TOP, CAP, 1))(routes_keys, routes_turns).reshape((TOKENS, TOP))
    cotangent = centred(key_of[3], (TOKENS, MODEL_WIDTH), 1.0, 6.0, ((0, 32),))
    w_query = centred(key_of[4], (MODEL_WIDTH, QUERY_HEADS * HEAD_SIZE), (MODEL_WIDTH // 12) ** -0.5, 0.625, ((0, 8),))
    key_weight = centred(key_of[5], (MODEL_WIDTH, KEY_VALUE_HEADS * HEAD_SIZE), (MODEL_WIDTH // 12) ** -0.5, 0.625, ((0, 8),))
    value_weight = centred(key_of[6], (MODEL_WIDTH, KEY_VALUE_HEADS * HEAD_SIZE), MODEL_WIDTH ** -0.5, 0.1875, ((0, 8),))
    w_out = centred(key_of[7], (QUERY_HEADS * HEAD_SIZE, MODEL_WIDTH), 0.8, 6.0, ((0, 8),))
    norm_attn = jnp.clip(1.0 + 0.1 * jax.random.normal(key_of[8], (MODEL_WIDTH,), jnp.float32), 0.5, 1.5).astype(jnp.bfloat16)
    norm_moe = jnp.clip(1.0 + 0.1 * jax.random.normal(key_of[9], (MODEL_WIDTH,), jnp.float32), 0.5, 1.5).astype(jnp.bfloat16)
    w_router = centred(key_of[10], (MODEL_WIDTH, EXPERTS), (4 * MODEL_WIDTH) ** -0.5, 0.09375, ((0, 8),))
    w_gate = centred(key_of[11], (EXPERTS, MODEL_WIDTH, F), MODEL_WIDTH ** -0.5, 0.1875, ((0, 8),))
    w_up = centred(key_of[12], (EXPERTS, MODEL_WIDTH, F), MODEL_WIDTH ** -0.5, 0.1875, ((0, 8),))
    w_down = centred(key_of[13], (EXPERTS, F, MODEL_WIDTH), 0.8, 6.0, ((0, 8),))
    return dict(tokens=tokens, prefix=prefix, routes=routes, cotangent=cotangent, w_query=w_query, key_weight=key_weight, value_weight=value_weight, w_out=w_out, norm_attn=norm_attn, norm_moe=norm_moe, w_router=w_router, w_gate=w_gate, w_up=w_up, w_down=w_down)


@jax.custom_vjp
def lower_precision(v):
    return lax.optimization_barrier(v.astype(jnp.bfloat16)).astype(jnp.float32)

@jax.custom_vjp
def lower_backward(v):
    return v

def low_keep(v):
    return (lower_precision(v), None)

def low_pass(kept, grad):
    return (grad,)

def back_keep(v):
    return (v, None)

def back_low(kept, grad):
    return (lower_precision(grad),)
lower_precision.defvjp(low_keep, low_pass)
lower_backward.defvjp(back_keep, back_low)
epsilon = 1e-06
score_scale = 0.015625
branch_scale = 0.22
masked_value = -1e+30

def rms_norm(value_rows, norm_gain):
    return value_rows * lax.rsqrt(lax.optimization_barrier(jnp.mean(value_rows * value_rows, axis=-1, keepdims=True)) + epsilon) * norm_gain

def rotary_tables(positions_count):
    half_size = HEAD_SIZE // 2
    places = jnp.arange(positions_count, dtype=jnp.float32)
    inverse = jnp.exp(jnp.arange(half_size, dtype=jnp.float32) * (-2.0 * math.log(10000.0) / HEAD_SIZE))
    angles = places[:, None] * inverse[None, :]
    return (jnp.cos(angles)[:, None, :], jnp.sin(angles)[:, None, :])

def apply_rotary(value_rows, cosine_table, sine_table):
    half_size = value_rows.shape[-1] // 2
    first_half = value_rows[..., :half_size]
    second_half = value_rows[..., half_size:]
    return jnp.concatenate([first_half * cosine_table - second_half * sine_table, second_half * cosine_table + first_half * sine_table], axis=-1)

def slot_places(route_rows):
    flat_routes = route_rows.reshape(-1)
    expert_ids = jnp.arange(EXPERTS, dtype=jnp.int32)
    matches = (flat_routes[:, None] == expert_ids[None, :]).astype(jnp.int32)
    earlier = jnp.cumsum(matches, axis=0) - matches
    return flat_routes * CAP + lax.optimization_barrier(jnp.sum(earlier * matches, axis=1))

def attend(query_matrix, key_rows, value_rows, prefix_len):
    count_of_rows = query_matrix.shape[0]
    grouped_rows = query_matrix.reshape(count_of_rows, KEY_VALUE_HEADS, QUERY_HEADS // KEY_VALUE_HEADS, HEAD_SIZE)
    raw_scores = lower_backward(jnp.einsum('tngd,snd->ngts', grouped_rows, key_rows, precision=lax.Precision.HIGHEST))
    row_index = jnp.arange(count_of_rows, dtype=jnp.int32)
    visible = (row_index[None, :] <= row_index[:, None]) | (row_index[None, :] < prefix_len)
    scores = jnp.where(visible, raw_scores * score_scale, masked_value)
    probabilities = lower_precision(jax.nn.softmax(scores, axis=-1))
    attended = jnp.einsum('ngts,snd->tngd', probabilities, value_rows, precision=lax.Precision.HIGHEST)
    return attended.reshape(count_of_rows, QUERY_HEADS * HEAD_SIZE)

def gather_rows(table_rows, place_row):
    return table_rows[place_row]

def scatter_rows(place_row, source_rows):
    return jnp.zeros((EXPERTS * CAP, MODEL_WIDTH), jnp.float32).at[place_row].add(source_rows)

def layer_block(arguments, params):
    inputs, prefix_block, route_block = arguments
    w_query, key_weight, value_weight, w_out, norm_attn, norm_moe, w_router, w_gate, w_up, w_down = params
    highest_precision = lax.Precision.HIGHEST
    group_count = prefix_block.shape[0]
    first_normed = lower_precision(rms_norm(inputs, norm_attn))
    cosine_table, sine_table = rotary_tables(TOKENS_PER_CARD)
    query_matrix = lower_backward(jnp.dot(first_normed, w_query, precision=highest_precision)).reshape(group_count, TOKENS_PER_CARD, QUERY_HEADS, HEAD_SIZE)
    query_matrix = lower_precision(apply_rotary(query_matrix, cosine_table, sine_table))
    key_rows = lower_backward(jnp.dot(first_normed, key_weight, precision=highest_precision)).reshape(group_count, TOKENS_PER_CARD, KEY_VALUE_HEADS, HEAD_SIZE)
    key_rows = lower_precision(apply_rotary(key_rows, cosine_table, sine_table))
    value_rows = lower_precision(lower_backward(jnp.dot(first_normed, value_weight, precision=highest_precision))).reshape(group_count, TOKENS_PER_CARD, KEY_VALUE_HEADS, HEAD_SIZE)
    attended = jax.vmap(attend)(query_matrix, key_rows, value_rows, prefix_block).reshape(group_count * TOKENS_PER_CARD, QUERY_HEADS * HEAD_SIZE)
    attended = lower_precision(lower_backward(attended))
    projected = lower_backward(jnp.dot(attended, w_out, precision=highest_precision))
    hidden_one = inputs + branch_scale * projected
    normed_two = lower_precision(rms_norm(hidden_one, norm_moe))
    logits = lower_backward(jnp.dot(normed_two, w_router, precision=highest_precision))
    chosen = jnp.take_along_axis(logits, route_block, axis=1)
    route_gates = jax.nn.softmax(chosen, axis=-1)
    places = jax.vmap(slot_places)(route_block.reshape(group_count, TOKENS_PER_CARD * TOP))
    sources = jnp.repeat(normed_two.reshape(group_count, TOKENS_PER_CARD, MODEL_WIDTH), TOP, axis=1)
    dispatched = jax.vmap(scatter_rows)(places, sources)
    dispatched = lower_backward(dispatched.reshape(group_count, EXPERTS, CAP, MODEL_WIDTH))
    gate_part = lower_backward(jnp.einsum('gecd,edf->gecf', dispatched, w_gate, precision=highest_precision))
    up_part = lower_backward(jnp.einsum('gecd,edf->gecf', dispatched, w_up, precision=highest_precision))
    inner = lower_precision(jax.nn.silu(gate_part) * up_part)
    output = lower_precision(lower_backward(jnp.einsum('gecf,efd->gecd', inner, w_down, precision=highest_precision)))
    routed = jax.vmap(gather_rows)(output.reshape(group_count, EXPERTS * CAP, MODEL_WIDTH), places)
    routed = routed.reshape(group_count * TOKENS_PER_CARD, TOP, MODEL_WIDTH)
    mixture = lax.optimization_barrier(jnp.sum(route_gates[:, :, None] * routed, axis=1))
    return hidden_one + branch_scale * mixture

def reference(tokens, prefix, routes, cotangent, w_query, key_weight, value_weight, w_out, norm_attn, norm_moe, w_router, w_gate, w_up, w_down):
    group_count = math.gcd(SEQS, max(1, 4096 // TOKENS_PER_CARD))
    turn_count = SEQS // group_count
    params = tuple((weight.astype(jnp.float32) for weight in (w_query, key_weight, value_weight, w_out, norm_attn, norm_moe, w_router, w_gate, w_up, w_down)))

    def forward(inputs, weights):

        def one_step(arguments):
            return layer_block(arguments, weights)
        blocks = (inputs.reshape(turn_count, group_count * TOKENS_PER_CARD, MODEL_WIDTH), prefix.reshape(turn_count, group_count), routes.reshape(turn_count, group_count * TOKENS_PER_CARD, TOP))
        return lax.map(jax.checkpoint(one_step), blocks).reshape(TOKENS, MODEL_WIDTH)
    result, pull_back = jax.vjp(forward, tokens.astype(jnp.float32), params)
    d_tokens, d_params = pull_back(cotangent.astype(jnp.float32))
    return (result.astype(jnp.bfloat16), d_tokens, d_params[0], d_params[1], d_params[2], d_params[3], d_params[4], d_params[5], d_params[6], d_params[7], d_params[8], d_params[9])
```

```python
import math

import jax
import jax.numpy as jnp
from jax import lax
from jax.sharding import PartitionSpec as P

QUERY_HEADS = 16
KEY_VALUE_HEADS = 8
HEAD_SIZE = 64
CAP = 96
LANES = 128
MOST_GATHERED = 4

epsilon = 1e-06
score_scale = 0.015625
branch_scale = 0.22
masked_value = -1e30

f32 = jnp.float32
bf16 = jnp.bfloat16


def dot(left, right, contract=((1,), (0,))):
    return lax.dot_general(left, right, (contract, ((), ())), preferred_element_type=f32)


def norm_scale(rows):
    return lax.rsqrt(jnp.mean(rows * rows, axis=-1, keepdims=True) + epsilon)


def norm_backward(rows, scaling, gain, upstream):
    weighted = upstream * gain
    inner_mean = jnp.mean(weighted * rows, axis=-1, keepdims=True)
    gradient = scaling * weighted - rows * (scaling * scaling * scaling) * inner_mean
    return gradient, jnp.sum(upstream * rows * scaling, axis=0, keepdims=True)


def rotary_tables(count):
    half = HEAD_SIZE // 2
    places = jnp.arange(count, dtype=f32)
    inverse = jnp.exp(jnp.arange(half, dtype=f32) * (-2.0 * math.log(10000.0) / HEAD_SIZE))
    angles = places[:, None] * inverse[None, :]
    return jnp.cos(angles)[:, None, :], jnp.sin(angles)[:, None, :]


def apply_rotary(rows, cosine, sine):
    half = HEAD_SIZE // 2
    shaped = rows.reshape(rows.shape[0], -1, HEAD_SIZE)
    first, second = shaped[..., :half], shaped[..., half:]
    turned = jnp.concatenate(
        [first * cosine - second * sine, second * cosine + first * sine], axis=-1
    )
    return turned.reshape(rows.shape)


def attention_scores(query, keys, prefix_len):
    count = query.shape[0]
    raw = jnp.einsum("tngd,snd->ngts", query, keys, preferred_element_type=f32)
    place = jnp.arange(count, dtype=jnp.int32)
    visible = (place[None, :] <= place[:, None]) | (place[None, :] < prefix_len)
    return jnp.where(visible, raw * score_scale, masked_value)


def slots_of(gates, first_expert, local):
    tokens = gates.shape[1]
    mine = lax.dynamic_slice_in_dim(gates, first_expert, local, axis=2)
    named = mine > 0
    place = jnp.arange(tokens)
    earlier = (place[None, :] < place[:, None]).astype(bf16)
    rank = jnp.einsum("ts,bsl->blt", earlier, named.astype(bf16), preferred_element_type=f32)
    slot = jnp.arange(CAP, dtype=f32)
    here = (rank[:, :, None, :] == slot[None, None, :, None]) & named.transpose(0, 2, 1)[:, :, None, :]
    return here, mine


def body(
    tokens, prefix, routes, cotangent, w_query, key_weight, value_weight, w_out,
    norm_attn, norm_moe, w_router, w_gate, w_up, w_down,
):
    inputs = tokens.astype(f32)
    count, width = inputs.shape
    local, _, hidden = w_gate.shape
    shards, reps = lax.axis_size("shard"), lax.axis_size("rep")
    experts = local * shards
    kv_width = key_weight.shape[1]
    me, rep = lax.axis_index("shard"), lax.axis_index("rep")
    group = QUERY_HEADS // KEY_VALUE_HEADS

    small = jnp.concatenate([w_router, norm_attn[:, None], norm_moe[:, None]], axis=1)
    small = jnp.pad(small, ((0, 0), (0, LANES - small.shape[1])))
    packed = jnp.concatenate([w_query, key_weight, value_weight, w_out, small], axis=1)
    packed = lax.all_gather(packed, "shard", axis=0, tiled=True)
    cuts = [width, width + kv_width, width + 2 * kv_width, 2 * width + 2 * kv_width]
    wq, wk, wv, wo, small = jnp.split(packed, cuts, axis=1)
    wr = small[:, :experts]
    gain_one = small[:, experts].astype(f32)[None, :]
    gain_two = small[:, experts + 1].astype(f32)[None, :]
    spread = reps <= MOST_GATHERED
    axes = ("rep", "shard") if spread else "shard"
    all_cot = lax.all_gather(cotangent, axes, axis=0, tiled=True)

    scale_one = norm_scale(inputs)
    normed_one = (inputs * scale_one * gain_one).astype(bf16)
    cosine, sine = rotary_tables(count)
    query = apply_rotary(dot(normed_one, wq), cosine, sine).astype(bf16)
    keys = apply_rotary(dot(normed_one, wk), cosine, sine).astype(bf16)
    values = dot(normed_one, wv).astype(bf16)
    query4 = query.reshape(count, KEY_VALUE_HEADS, group, HEAD_SIZE)
    keys3 = keys.reshape(count, KEY_VALUE_HEADS, HEAD_SIZE)
    values3 = values.reshape(count, KEY_VALUE_HEADS, HEAD_SIZE)
    scores = attention_scores(query4, keys3, prefix[0])
    weights = jnp.exp(scores - jnp.max(scores, axis=-1, keepdims=True))
    probs = weights / jnp.sum(weights, axis=-1, keepdims=True)
    probs_low = probs.astype(bf16)
    attended = jnp.einsum("ngts,snd->tngd", probs_low, values3, preferred_element_type=f32)
    attended = attended.reshape(count, -1).astype(bf16)
    hidden_one = inputs + branch_scale * dot(attended, wo)
    scale_two = norm_scale(hidden_one)
    normed_two = (hidden_one * scale_two * gain_two).astype(bf16)
    logits = dot(normed_two, wr)
    picks = routes[:, :, None] == jnp.arange(experts, dtype=jnp.int32)[None, None, :]
    chosen_mask = jnp.any(picks, axis=1)
    top = jnp.max(jnp.where(chosen_mask, logits, -jnp.inf), axis=1, keepdims=True)
    gates = jnp.where(chosen_mask, jnp.exp(logits - top), 0.0)
    gates = gates / jnp.sum(gates, axis=1, keepdims=True)

    high = gates.astype(bf16)
    low = (gates - high.astype(f32)).astype(bf16)
    pad = jnp.zeros((count, LANES - 2 * experts), bf16)
    sent = jnp.concatenate([normed_two, high, low, pad], axis=1)
    arrived = lax.all_gather(sent, axes, axis=0, tiled=True)
    arrived = arrived.reshape(-1, shards, count, width + LANES)
    all_gates = arrived[..., width : width + experts].astype(f32)
    all_gates = all_gates + arrived[..., width + experts : width + 2 * experts].astype(f32)
    all_cot = all_cot.reshape(-1, shards, count, width)

    def gathered(number):
        rows = lax.dynamic_index_in_dim(arrived, number, 0, keepdims=False)[..., :width]
        cot = lax.dynamic_index_in_dim(all_cot, number, 0, keepdims=False)
        gate_rows = lax.dynamic_index_in_dim(all_gates, number, 0, keepdims=False)
        here, mine = slots_of(gate_rows, me * local, local)
        one_hot = here.astype(bf16)
        slot_gate = jnp.sum(jnp.where(here, mine.transpose(0, 2, 1)[:, :, None, :], 0.0), axis=3)
        xg = jnp.einsum("blst,btd->lbsd", one_hot, rows).reshape(local, -1, width)
        cg = jnp.einsum("blst,btd->lbsd", one_hot, cot).reshape(local, -1, width)
        scale = branch_scale * slot_gate.transpose(1, 0, 2).reshape(local, -1)[:, :, None]
        gate_part = jnp.einsum("lmd,ldf->lmf", xg, w_gate, preferred_element_type=f32)
        up_part = jnp.einsum("lmd,ldf->lmf", xg, w_up, preferred_element_type=f32)
        raw = jnp.einsum("lmd,lfd->lmf", cg, w_down, preferred_element_type=f32)
        sigma = jax.nn.sigmoid(gate_part)
        act = gate_part * sigma
        inner = act * up_part
        d_inner = raw * scale
        d_gate = (d_inner * up_part * sigma * (1.0 + gate_part * (1.0 - sigma))).astype(bf16)
        d_up = (d_inner * act).astype(bf16)
        scaled = (inner * scale).astype(bf16)
        sums = (
            jnp.einsum("lmd,lmf->ldf", xg, d_gate, preferred_element_type=f32),
            jnp.einsum("lmd,lmf->ldf", xg, d_up, preferred_element_type=f32),
            jnp.einsum("lmf,lmd->lfd", scaled, cg, preferred_element_type=f32),
        )
        return sums, (one_hot, inner, raw, d_gate, d_up, scaled)

    sums, (one_hot, inner, raw, d_gate, d_up, scaled) = gathered(rep if spread else 0)
    out_rows = jnp.einsum("lmf,lfd->lmd", scaled, w_down, preferred_element_type=f32).astype(bf16)
    d_rows = jnp.einsum("lmf,ldf->lmd", d_gate, w_gate, preferred_element_type=f32)
    d_rows = (d_rows + jnp.einsum("lmf,ldf->lmd", d_up, w_up, preferred_element_type=f32)).astype(bf16)
    slot_d_gate = branch_scale * jnp.sum(inner * raw, axis=2)
    shape4 = (local, shards, CAP, width)
    mix = jnp.einsum("blst,lbsd->btd", one_hot, out_rows.reshape(shape4), preferred_element_type=f32)
    d_in = jnp.einsum("blst,lbsd->btd", one_hot, d_rows.reshape(shape4), preferred_element_type=f32)
    dg_local = jnp.sum(
        jnp.where(one_hot > 0, slot_d_gate.reshape(local, shards, CAP).transpose(1, 0, 2)[..., None], 0.0), axis=2
    )
    dg = jnp.zeros((shards, count, LANES), f32)
    dg = lax.dynamic_update_slice(dg, dg_local.transpose(0, 2, 1), (0, 0, me * local))
    back = jnp.concatenate([mix, d_in, dg], axis=2).astype(bf16).reshape(shards * count, -1)
    back = lax.psum_scatter(back, "shard", scatter_dimension=0, tiled=True).astype(f32)
    if spread:
        for step in range(1, reps):
            more, _ = gathered(lax.rem(rep + step, reps))
            sums = tuple(a + b for a, b in zip(sums, more))
    else:
        sums = tuple(lax.psum(a.astype(bf16), "rep").astype(f32) for a in sums)
    d_w_gate, d_w_up, d_w_down = sums

    result = (hidden_one + back[:, :width]).astype(bf16)
    cot = cotangent.astype(f32)
    d_gates = back[:, 2 * width : 2 * width + experts]
    d_logits = gates * (d_gates - jnp.sum(gates * d_gates, axis=1, keepdims=True))
    d_logits = d_logits.astype(bf16)
    d_router = dot(normed_two, d_logits, ((0,), (0,)))
    d_normed_two = back[:, width : 2 * width] + dot(d_logits, wr, ((1,), (1,)))
    d_hidden, d_gain_two = norm_backward(hidden_one, scale_two, gain_two, d_normed_two)
    d_hidden = d_hidden + cot
    d_projected = (branch_scale * d_hidden).astype(bf16)
    d_wo = dot(attended, d_projected, ((0,), (0,)))
    d_attended = dot(d_projected, wo, ((1,), (1,))).astype(bf16)
    d_attended = d_attended.reshape(count, KEY_VALUE_HEADS, group, HEAD_SIZE)
    d_values = jnp.einsum("ngts,tngd->snd", probs_low, d_attended, preferred_element_type=f32)
    d_probs = jnp.einsum("tngd,snd->ngts", d_attended, values3, preferred_element_type=f32)
    weighted = jnp.sum(probs * d_probs, axis=-1, keepdims=True)
    d_scores = (probs * (d_probs - weighted) * score_scale).astype(bf16)
    d_query = jnp.einsum("ngts,snd->tngd", d_scores, keys3, preferred_element_type=f32)
    d_keys = jnp.einsum("ngts,tngd->snd", d_scores, query4, preferred_element_type=f32)
    d_query = apply_rotary(d_query.reshape(count, -1), cosine, -sine).astype(bf16)
    d_keys = apply_rotary(d_keys.reshape(count, -1), cosine, -sine).astype(bf16)
    d_values = d_values.reshape(count, -1).astype(bf16)
    d_qkv = jnp.concatenate([d_query, d_keys, d_values], axis=1)
    d_w_qkv = dot(normed_one, d_qkv, ((0,), (0,)))
    d_normed_one = dot(d_qkv, packed[:, : cuts[2]], ((1,), (1,)))
    d_tokens, d_gain_one = norm_backward(inputs, scale_one, gain_one, d_normed_one)
    d_tokens = d_tokens + d_hidden
    small = jnp.concatenate([d_router, d_gain_one.T, d_gain_two.T], axis=1)
    small = jnp.pad(small, ((0, 0), (0, LANES - small.shape[1])))
    shares = jnp.concatenate([d_w_qkv, d_wo, small], axis=1).astype(bf16)
    shares = lax.psum_scatter(shares, "shard", scatter_dimension=0, tiled=True)
    totals = lax.psum(shares, "rep").astype(f32)
    d_wq, d_wk, d_wv, d_wo, small = jnp.split(totals, cuts, axis=1)
    return (
        result, d_tokens, d_wq, d_wk, d_wv, d_wo, small[:, experts], small[:, experts + 1],
        small[:, :experts], d_w_gate, d_w_up, d_w_down,
    )


def solution(mesh):
    rows = P(("rep", "shard"), None)
    one, two, three = P("shard"), P("shard", None), P("shard", None, None)
    return jax.shard_map(
        body,
        mesh=mesh,
        in_specs=(rows, P(("rep", "shard")), rows, rows, two, two, two, two, one, one, two, three, three, three),
        out_specs=(rows, rows, two, two, two, two, one, one, two, three, three, three),
        check_vma=False,
    )
```

```python
import functools
import math

import jax
import jax.numpy as jnp
from jax import lax
from jax.experimental import pallas as pl
from jax.experimental.pallas import tpu as pltpu
from jax.sharding import PartitionSpec as P

QUERY_HEADS = 16
KEY_VALUE_HEADS = 8
HEAD_SIZE = 64
CAP = 96
LANES = 128
MOST_GATHERED = 4

epsilon = 1e-06
score_scale = 0.015625
branch_scale = 0.22
masked_value = -1e30

f32 = jnp.float32
bf16 = jnp.bfloat16
MESH = pl.DeviceIdType.MESH


def dot(left, right, contract=((1,), (0,))):
    return lax.dot_general(left, right, (contract, ((), ())), preferred_element_type=f32)

def slot_ranks(gates):
    tokens = gates.shape[1]
    named = gates > 0
    before = lax.broadcasted_iota(jnp.int32, (tokens, tokens), 0) < lax.broadcasted_iota(jnp.int32, (tokens, tokens), 1)
    rank = dot(named.astype(f32).astype(bf16), before.astype(f32).astype(bf16))
    return jnp.where(named, rank, -1.0)

def pick_row(table, row):
    here = lax.broadcasted_iota(jnp.int32, table.shape, 0) == row
    return jnp.sum(jnp.where(here, table, 0.0), axis=0, keepdims=True)

def slot_one_hot(ranks, first, local):
    tokens = ranks.shape[1]
    slot = lax.broadcasted_iota(jnp.int32, (CAP, tokens), 0).astype(f32)
    return [jnp.where(pick_row(ranks, first + l) == slot, 1.0, 0.0) for l in range(local)]

def gather_block(x, c, gates, first, local, xg_ref, cg_ref, sg_ref, at):
    ranks = slot_ranks(gates)
    parts = slot_one_hot(ranks, first, local)
    table = jnp.concatenate(parts, axis=0).astype(bf16)
    xg = dot(table, x).astype(bf16)
    cg = dot(table, c).astype(bf16)
    for l in range(local):
        rows = slice(l * CAP, (l + 1) * CAP)
        xg_ref[l, pl.ds(at, CAP), :] = xg[rows]
        cg_ref[l, pl.ds(at, CAP), :] = cg[rows]
        gate = jnp.sum(parts[l] * pick_row(gates, first + l), axis=1, keepdims=True)
        sg_ref[l, pl.ds(at, CAP), :] = branch_scale * gate
    return parts

def expert_parts(xg, cg, scale, wg, wu, wd):
    gate_part = dot(xg, wg)
    up_part = dot(xg, wu)
    raw = dot(cg, wd, ((1,), (1,)))
    sigma = 1.0 / (1.0 + jnp.exp(-gate_part))
    act = gate_part * sigma
    inner = act * up_part
    d_inner = raw * scale
    d_gate = (d_inner * up_part * (sigma + act * (1.0 - sigma))).astype(bf16)
    d_up = (d_inner * act).astype(bf16)
    scaled = (inner * scale).astype(bf16)
    return inner, raw, d_gate, d_up, scaled

def sums_kernel(nb, x_hbm, c_hbm, g_ref, wg_hbm, wu_hbm, wd_hbm, og_hbm, ou_hbm, od_hbm,
                xbuf, cbuf, wg, wu, wd, ag, au, ad, xg_ref, cg_ref, sg_ref, sem, wsem):
    local = wg.shape[0]
    blocks = x_hbm.shape[0]
    chunks = blocks // nb
    first = lax.axis_index("shard") * local
    def fetch(i, slot):
        return (pltpu.make_async_copy(x_hbm.at[pl.ds(i * nb, nb)], xbuf.at[slot], sem.at[0, slot]),
                pltpu.make_async_copy(c_hbm.at[pl.ds(i * nb, nb)], cbuf.at[slot], sem.at[1, slot]))
    for cp in fetch(0, 0):
        cp.start()
    weights = [pltpu.make_async_copy(a, b, wsem.at[i]) for i, (a, b) in enumerate(((wg_hbm, wg), (wu_hbm, wu), (wd_hbm, wd)))]
    for cp in weights:
        cp.start()
    ag[...] = jnp.zeros_like(ag)
    au[...] = jnp.zeros_like(au)
    ad[...] = jnp.zeros_like(ad)
    for cp in weights:
        cp.wait()

    def chunk(i, carry):
        slot = lax.rem(i, 2)
        @pl.when(i + 1 < chunks)
        def _():
            for cp in fetch(i + 1, 1 - slot):
                cp.start()
        for cp in fetch(i, slot):
            cp.wait()
        def block(b, carry):
            gather_block(xbuf[slot, b], cbuf[slot, b], g_ref[i * nb + b], first, local, xg_ref, cg_ref, sg_ref,
                         pl.multiple_of(b * CAP, CAP))
            return carry
        lax.fori_loop(0, nb, block, 0)
        def expert(l, carry):
            xg, cg = xg_ref[l], cg_ref[l]
            _, _, d_gate, d_up, scaled = expert_parts(xg, cg, sg_ref[l], wg[l], wu[l], wd[l])
            ag[l] += dot(xg, d_gate, ((0,), (0,)))
            au[l] += dot(xg, d_up, ((0,), (0,)))
            ad[l] += dot(scaled, cg, ((0,), (0,)))
            return carry
        lax.fori_loop(0, local, expert, 0)
        return carry
    lax.fori_loop(0, chunks, chunk, 0)
    outs = [pltpu.make_async_copy(a, b, wsem.at[i]) for i, (a, b) in enumerate(((ag, og_hbm), (au, ou_hbm), (ad, od_hbm)))]
    for cp in outs:
        cp.start()
    for cp in outs:
        cp.wait()

def moe_sums(x, c, gates, wg, wu, wd, nb=4):
    _, tokens, width = x.shape
    local, _, hidden = wg.shape
    any_ = pl.BlockSpec(memory_space=pl.ANY)
    rows = nb * CAP
    return pl.pallas_call(
        functools.partial(sums_kernel, nb),
        out_shape=[jax.ShapeDtypeStruct(w.shape, f32) for w in (wg, wu, wd)],
        in_specs=[any_, any_, pl.BlockSpec(memory_space=pltpu.VMEM), any_, any_, any_],
        out_specs=[any_] * 3,
        scratch_shapes=[
            pltpu.VMEM((2, nb, tokens, width), bf16), pltpu.VMEM((2, nb, tokens, width), bf16),
            pltpu.VMEM(wg.shape, bf16), pltpu.VMEM(wu.shape, bf16), pltpu.VMEM(wd.shape, bf16),
            pltpu.VMEM(wg.shape, f32), pltpu.VMEM(wu.shape, f32), pltpu.VMEM(wd.shape, f32),
            pltpu.VMEM((local, rows, width), bf16), pltpu.VMEM((local, rows, width), bf16), pltpu.VMEM((local, rows, 1), f32),
            pltpu.SemaphoreType.DMA((2, 2)), pltpu.SemaphoreType.DMA((3,)),
        ],
        compiler_params=pltpu.CompilerParams(vmem_limit_bytes=60 << 20),
        name="expert_sums",
    )(x, c, gates, wg, wu, wd)


def norm_scale(rows):
    return lax.rsqrt(jnp.mean(rows * rows, axis=-1, keepdims=True) + epsilon)

def flip(index, bit):
    return index + bit - 2 * bit * ((index // bit) % 2)

def turned(index, core, step, bits):
    return (1 - core) * flip(index, bits[step]) + core * flip(index, bits[-1 - step])

class PlaneGather:
    def __init__(self, buf, send, recv, base=0):
        self.buf, self.send, self.recv, self.base = buf, send, recv, base
        self.rep, self.me = lax.axis_index("rep"), lax.axis_index("shard")
        self.core = self.me % 2
        shards = lax.axis_size("shard")
        self.bits = [1 << i for i in range(1, shards.bit_length() - 1)]
        self.steps = len(self.bits)

    @staticmethod
    def copies(shards):
        return (shards // 2 - 1) + shards // 2

    def owner(self, of, subset):
        for step in range(self.steps):
            if subset >> step & 1:
                of = turned(of, self.core, step, self.bits)
        return of

    def copy(self, number, owner, target):
        return pltpu.make_async_remote_copy(
            src_ref=self.buf.at[owner], dst_ref=self.buf.at[owner],
            send_sem=self.send.at[self.base + number], recv_sem=self.recv.at[self.base + number],
            device_id=(self.rep, target), device_id_type=MESH,
        )

    def chip_copy(self, step, subset):
        return self.copy((1 << step) - 1 + subset, self.owner(self.me, subset), turned(self.me, self.core, step, self.bits))

    def core_copy(self, subset):
        return self.copy((1 << self.steps) - 1 + subset, self.owner(self.me, subset), flip(self.me, 1))

    def start(self):
        for step in range(self.steps):
            self.chip_copy(step, 0).start()
        self.core_copy(0).start()

    def forward(self, step):
        for subset in range(1 << step):
            self.chip_copy(step, subset).wait_recv()
            whole = subset + (1 << step)
            for later in range(step + 1, self.steps):
                self.chip_copy(later, whole).start()
            self.core_copy(whole).start()

    def finish(self):
        for subset in range(1 << self.steps):
            self.core_copy(subset).wait_recv()
        for step in range(self.steps):
            for subset in range(1 << step):
                self.chip_copy(step, subset).wait_send()
        for subset in range(1 << self.steps):
            self.core_copy(subset).wait_send()

def rotate(v, cosine, sine, sign):
    lane = lax.broadcasted_iota(jnp.int32, v.shape, 1) % HEAD_SIZE
    half = HEAD_SIZE // 2
    low = lane < half
    other = jnp.where(low, -pltpu.roll(v, LANES - half, 1), pltpu.roll(v, half, 1))
    return v * cosine + sign * other * sine

def two_heads(v):
    low = lax.broadcasted_iota(jnp.int32, v.shape, 1) < HEAD_SIZE
    zero = jnp.zeros_like(v)
    return jnp.concatenate([jnp.where(low, v, zero), jnp.where(low, zero, v)], axis=0)

def one_head_twice(pair, odd):
    high = lax.broadcasted_iota(jnp.int32, pair.shape, 1) // HEAD_SIZE
    wide = pair.astype(f32)
    return jnp.where(high == odd, wide, pltpu.roll(wide, HEAD_SIZE, 1)).astype(pair.dtype)

def probabilities(query2, keys, prefix_len):
    rows = query2.shape[0] // 2
    raw = dot(query2, keys, ((1,), (1,)))
    row = lax.broadcasted_iota(jnp.int32, raw.shape, 0) % rows
    col = lax.broadcasted_iota(jnp.int32, raw.shape, 1)
    scores = jnp.where((col <= row) | (col < prefix_len), raw * score_scale, masked_value)
    weights = jnp.exp(scores - jnp.max(scores, axis=-1, keepdims=True))
    return weights / jnp.sum(weights, axis=-1, keepdims=True)

def lanes(j, count=1):
    return pl.ds(pl.multiple_of(j * LANES * count, LANES), LANES * count)

def front_kernel(prefix_ref, tok_ref, routes_ref, cos_ref, sin_ref, mine_ref,
                 wall_out, q_out, k_out, v_out, att_out, hid_out, x_out, gates_out, n1_out,
                 wbuf, qkv_ref, send, recv, lsem):
    count, width = tok_ref.shape
    kv_width = k_out.shape[1]
    experts = gates_out.shape[0]
    shards, depth, total = wbuf.shape
    me = lax.axis_index("shard")
    own = pltpu.make_async_copy(mine_ref, wbuf.at[me], lsem.at[0])
    own.start()
    gather = PlaneGather(wbuf, send, recv)
    own.wait()
    gather.start()
    inputs = tok_ref[...].astype(f32)
    scaled = inputs * norm_scale(inputs)
    for step in range(gather.steps):
        gather.forward(step)
    gather.finish()
    keep = pltpu.make_async_copy(wbuf, wall_out, lsem.at[1])
    keep.start()
    cut = [0, width, width + kv_width, width + 2 * kv_width, 2 * width + 2 * kv_width]
    small = wbuf[:, :, cut[4]:].reshape(shards * depth, total - cut[4])
    wide = small.astype(f32).T
    gain_one, gain_two = wide[experts:experts + 1], wide[experts + 1:experts + 2]
    n1_out[...] = (scaled * gain_one).astype(bf16)

    def project(j, carry):
        w = wbuf[:, :, lanes(j, 2)].reshape(shards * depth, 2 * LANES)
        qkv_ref[:, lanes(j, 2)] = dot(n1_out[...], w)
        return carry
    lax.fori_loop(0, cut[3] // (2 * LANES), project, 0)
    cosine, sine = cos_ref[...], sin_ref[...]
    for j in range(width // LANES):
        q_out[:, j * LANES:(j + 1) * LANES] = rotate(qkv_ref[:, j * LANES:(j + 1) * LANES], cosine, sine, 1.0).astype(bf16)
    for j in range(kv_width // LANES):
        at = slice(cut[1] + j * LANES, cut[1] + (j + 1) * LANES)
        k_out[:, j * LANES:(j + 1) * LANES] = rotate(qkv_ref[:, at], cosine, sine, 1.0).astype(bf16)
    v_out[...] = qkv_ref[:, cut[2]:cut[3]].astype(bf16)
    prefix_len = prefix_ref[0]

    def head(j, carry):
        keys = one_head_twice(k_out[:, lanes(j // 2)], j % 2)
        values = one_head_twice(v_out[:, lanes(j // 2)], j % 2)
        prob = probabilities(two_heads(q_out[:, lanes(j)]), keys, prefix_len)
        both = dot(prob.astype(bf16), values)
        low = lax.broadcasted_iota(jnp.int32, (count, LANES), 1) < HEAD_SIZE
        att_out[:, lanes(j)] = jnp.where(low, both[:count], both[count:]).astype(bf16)
        return carry
    lax.fori_loop(0, KEY_VALUE_HEADS, head, 0)

    def project_out(j, carry):
        w = wbuf[:, :, pl.ds(pl.multiple_of(cut[3] + j * 2 * LANES, LANES), 2 * LANES)].reshape(shards * depth, 2 * LANES)
        qkv_ref[:, lanes(j, 2)] = dot(att_out[...], w)
        return carry
    lax.fori_loop(0, width // (2 * LANES), project_out, 0)
    hidden = inputs + branch_scale * qkv_ref[:, :width]
    hid_out[...] = hidden
    x = (hidden * norm_scale(hidden) * gain_two).astype(bf16)
    x_out[...] = x
    logits = dot(x, small).T[:experts]
    expert = lax.broadcasted_iota(jnp.int32, (experts, count), 0)
    named = expert < 0
    for k in range(routes_ref.shape[0]):
        named = named | (routes_ref[k:k + 1, :] == expert)
    top = jnp.max(jnp.where(named, logits, masked_value), axis=0, keepdims=True)
    weights = jnp.where(named, jnp.exp(jnp.where(named, logits - top, 0.0)), 0.0)
    gates_out[...] = weights / jnp.sum(weights, axis=0, keepdims=True)
    keep.wait()

def front(tokens, prefix, routes, mine, cosine, sine, experts, kv_width):
    count, width = tokens.shape
    shards = lax.axis_size("shard")
    depth, total = mine.shape
    v = pl.BlockSpec(memory_space=pltpu.VMEM)
    any_ = pl.BlockSpec(memory_space=pl.ANY)
    sds = jax.ShapeDtypeStruct
    n = PlaneGather.copies(shards)
    return pl.pallas_call(
        front_kernel,
        out_shape=[
            sds((shards, depth, total), bf16), sds((count, width), bf16), sds((count, kv_width), bf16), sds((count, kv_width), bf16),
            sds((count, width), bf16), sds((count, width), f32), sds((count, width), bf16), sds((experts, count), f32), sds((count, width), bf16),
        ],
        in_specs=[pl.BlockSpec(memory_space=pltpu.SMEM), v, v, v, v, any_],
        out_specs=[any_] + [v] * 8,
        scratch_shapes=[
            pltpu.VMEM((shards, depth, total), bf16), pltpu.VMEM((count, width + 2 * kv_width), f32),
            pltpu.SemaphoreType.DMA((n,)), pltpu.SemaphoreType.DMA((n,)), pltpu.SemaphoreType.DMA((2,)),
        ],
        compiler_params=pltpu.CompilerParams(vmem_limit_bytes=60 << 20, has_side_effects=True),
        name="front",
    )(prefix, tokens, routes, cosine, sine, mine)

def rotary_tables(count):
    half = HEAD_SIZE // 2
    places = jnp.arange(count, dtype=f32)
    inverse = jnp.exp(jnp.arange(half, dtype=f32) * (-2.0 * math.log(10000.0) / HEAD_SIZE))
    angles = jnp.tile(places[:, None] * inverse[None, :], (1, LANES // half))
    return jnp.cos(angles), jnp.sin(angles)


def pack(w_query, key_weight, value_weight, w_out, w_router, norm_attn, norm_moe):
    small = jnp.concatenate([w_router, norm_attn[:, None], norm_moe[:, None]], axis=1)
    small = jnp.pad(small, ((0, 0), (0, LANES - small.shape[1])))
    return jnp.concatenate([w_query, key_weight, value_weight, w_out, small], axis=1)


def norm_backward(rows, scaling, gain, upstream):
    weighted = upstream * gain
    inner_mean = jnp.mean(weighted * rows, axis=-1, keepdims=True)
    gradient = scaling * weighted - rows * (scaling * scaling * scaling) * inner_mean
    return gradient, jnp.sum(upstream * rows * scaling, axis=0, keepdims=True)


def turn_back(rows, cosine, sine):
    count = rows.shape[0]
    half = HEAD_SIZE // 2
    shaped = rows.reshape(count, -1, HEAD_SIZE)
    first, second = shaped[..., :half], shaped[..., half:]
    c, s = cosine[:, None, :half], sine[:, None, :half]
    return jnp.concatenate([first * c + second * s, second * c - first * s], axis=-1).reshape(rows.shape)


def own_part(x, c, gates, first, w_gate, w_up, w_down):
    local, width, hidden = w_gate.shape
    shards, count, _ = x.shape
    mine = lax.dynamic_slice_in_dim(gates, first, local, axis=1)
    named = mine > 0
    place = jnp.arange(count)
    earlier = (place[:, None] < place[None, :]).astype(bf16)
    rank = jnp.einsum("bls,st->blt", named.astype(bf16), earlier, preferred_element_type=f32)
    here = (rank[:, :, None, :] == jnp.arange(CAP, dtype=f32)[None, None, :, None]) & named[:, :, None, :]
    one_hot = here.astype(bf16)
    slot_gate = jnp.sum(jnp.where(here, mine[:, :, None, :], 0.0), axis=3)
    xg = jnp.einsum("blst,btd->lbsd", one_hot, x).reshape(local, -1, width)
    cg = jnp.einsum("blst,btd->lbsd", one_hot, c).reshape(local, -1, width)
    scale = branch_scale * slot_gate.transpose(1, 0, 2).reshape(local, -1)[:, :, None]
    gate_part = jnp.einsum("lmd,ldf->lmf", xg, w_gate, preferred_element_type=f32)
    up_part = jnp.einsum("lmd,ldf->lmf", xg, w_up, preferred_element_type=f32)
    raw = jnp.einsum("lmd,lfd->lmf", cg, w_down, preferred_element_type=f32)
    sigma = jax.nn.sigmoid(gate_part)
    act = gate_part * sigma
    inner = act * up_part
    d_inner = raw * scale
    d_gate = (d_inner * up_part * sigma * (1.0 + gate_part * (1.0 - sigma))).astype(bf16)
    d_up = (d_inner * act).astype(bf16)
    scaled = (inner * scale).astype(bf16)
    out_rows = jnp.einsum("lmf,lfd->lmd", scaled, w_down, preferred_element_type=f32).astype(bf16)
    d_rows = jnp.einsum("lmf,ldf->lmd", d_gate, w_gate, preferred_element_type=f32)
    d_rows = (d_rows + jnp.einsum("lmf,ldf->lmd", d_up, w_up, preferred_element_type=f32)).astype(bf16)
    slot_d_gate = branch_scale * jnp.sum(inner * raw, axis=2)
    shape4 = (local, shards, CAP, width)
    mix = jnp.einsum("blst,lbsd->btd", one_hot, out_rows.reshape(shape4), preferred_element_type=f32)
    d_in = jnp.einsum("blst,lbsd->btd", one_hot, d_rows.reshape(shape4), preferred_element_type=f32)
    dg = jnp.sum(jnp.where(here, slot_d_gate.reshape(local, shards, CAP).transpose(1, 0, 2)[..., None], 0.0), axis=2)
    dg_all = jnp.zeros((shards, count, LANES), f32)
    dg_all = lax.dynamic_update_slice(dg_all, dg.transpose(0, 2, 1), (0, 0, first))
    back = jnp.concatenate([mix, d_in, dg_all], axis=2).astype(bf16).reshape(shards * count, -1)
    back = lax.psum_scatter(back, "shard", scatter_dimension=0, tiled=True).astype(f32)
    return back[:, :width], back[:, width:2 * width], back[:, 2 * width:2 * width + gates.shape[1]].T


def body(
    tokens, prefix, routes, cotangent, w_query, key_weight, value_weight, w_out,
    norm_attn, norm_moe, w_router, w_gate, w_up, w_down,
):
    count, width = tokens.shape
    local, _, hidden = w_gate.shape
    shards, reps = lax.axis_size("shard"), lax.axis_size("rep")
    experts = local * shards
    kv_width = key_weight.shape[1]
    me, rep = lax.axis_index("shard"), lax.axis_index("rep")
    group = QUERY_HEADS // KEY_VALUE_HEADS
    spread = reps <= MOST_GATHERED
    axes = ("rep", "shard") if spread else "shard"
    all_cot = lax.all_gather(cotangent, axes, axis=0).reshape(-1, count, width)
    cosine, sine = rotary_tables(count)
    mine = pack(w_query, key_weight, value_weight, w_out, w_router, norm_attn, norm_moe)
    packed, query, keys, values, attended, hidden_one, normed_two, gates, normed_one = front(
        tokens, prefix, routes.T, mine, cosine, sine, experts, kv_width
    )
    packed = packed.reshape(width, -1)
    cuts = [width, width + kv_width, width + 2 * kv_width, 2 * width + 2 * kv_width]
    wo, small = packed[:, cuts[2]:cuts[3]], packed[:, cuts[3]:]
    wr = small[:, :experts]
    gain_one = small[:, experts].astype(f32)[None, :]
    gain_two = small[:, experts + 1].astype(f32)[None, :]
    all_x = lax.all_gather(normed_two, axes, axis=0).reshape(-1, count, width)
    all_gates = lax.all_gather(gates, axes, axis=0).reshape(-1, experts, count)
    own = rep * shards if spread else 0
    rows = lambda a: lax.dynamic_slice_in_dim(a, own, shards, axis=0)
    mix, d_in, d_gates = own_part(rows(all_x), rows(all_cot), rows(all_gates), me * local, w_gate, w_up, w_down)
    sums = moe_sums(all_x, all_cot, all_gates, w_gate, w_up, w_down)
    if not spread:
        sums = [lax.psum(a.astype(bf16), "rep").astype(f32) for a in sums]
    d_w_gate, d_w_up, d_w_down = sums

    inputs = tokens.astype(f32)
    cot = cotangent.astype(f32)
    scale_one, scale_two = norm_scale(inputs), norm_scale(hidden_one)
    result = (hidden_one + mix).astype(bf16)
    d_logits = (gates * (d_gates - jnp.sum(gates * d_gates, axis=0, keepdims=True))).astype(bf16)
    d_router = dot(normed_two, d_logits, ((0,), (1,)))
    d_normed_two = d_in + dot(d_logits, wr, ((0,), (1,)))
    d_hidden, d_gain_two = norm_backward(hidden_one, scale_two, gain_two, d_normed_two)
    d_hidden = d_hidden + cot
    d_projected = (branch_scale * d_hidden).astype(bf16)
    d_wo = dot(attended, d_projected, ((0,), (0,)))
    d_attended = dot(d_projected, wo, ((1,), (1,))).astype(bf16)
    query4 = query.reshape(count, KEY_VALUE_HEADS, group, HEAD_SIZE)
    keys3 = keys.reshape(count, KEY_VALUE_HEADS, HEAD_SIZE)
    values3 = values.reshape(count, KEY_VALUE_HEADS, HEAD_SIZE)
    raw = jnp.einsum("tngd,snd->ngts", query4, keys3, preferred_element_type=f32)
    place = jnp.arange(count, dtype=jnp.int32)
    visible = (place[None, :] <= place[:, None]) | (place[None, :] < prefix[0])
    probs = jax.nn.softmax(jnp.where(visible, raw * score_scale, masked_value), axis=-1)
    d_attended = d_attended.reshape(count, KEY_VALUE_HEADS, group, HEAD_SIZE)
    d_values = jnp.einsum("ngts,tngd->snd", probs.astype(bf16), d_attended, preferred_element_type=f32)
    d_probs = jnp.einsum("tngd,snd->ngts", d_attended, values3, preferred_element_type=f32)
    weighted = jnp.sum(probs * d_probs, axis=-1, keepdims=True)
    d_scores = (probs * (d_probs - weighted) * score_scale).astype(bf16)
    d_query = jnp.einsum("ngts,snd->tngd", d_scores, keys3, preferred_element_type=f32)
    d_keys = jnp.einsum("ngts,tngd->snd", d_scores, query4, preferred_element_type=f32)
    d_query = turn_back(d_query.reshape(count, -1), cosine, sine).astype(bf16)
    d_keys = turn_back(d_keys.reshape(count, -1), cosine, sine).astype(bf16)
    d_values = d_values.reshape(count, -1).astype(bf16)
    d_qkv = jnp.concatenate([d_query, d_keys, d_values], axis=1)
    d_w_qkv = dot(normed_one, d_qkv, ((0,), (0,)))
    d_normed_one = dot(d_qkv, packed[:, :cuts[2]], ((1,), (1,)))
    d_tokens, d_gain_one = norm_backward(inputs, scale_one, gain_one, d_normed_one)
    d_tokens = d_tokens + d_hidden
    small = jnp.concatenate([d_router, d_gain_one.T, d_gain_two.T], axis=1)
    small = jnp.pad(small, ((0, 0), (0, LANES - small.shape[1])))
    shares = jnp.concatenate([d_w_qkv, d_wo, small], axis=1).astype(bf16)
    shares = lax.psum_scatter(shares, "shard", scatter_dimension=0, tiled=True)
    totals = lax.psum(shares, "rep").astype(f32)
    d_wq, d_wk, d_wv, d_wo, small = jnp.split(totals, cuts, axis=1)
    return (
        result, d_tokens, d_wq, d_wk, d_wv, d_wo, small[:, experts], small[:, experts + 1],
        small[:, :experts], d_w_gate, d_w_up, d_w_down,
    )


def solution(mesh):
    rows = P(("rep", "shard"), None)
    one, two, three = P("shard"), P("shard", None), P("shard", None, None)
    return jax.shard_map(
        body,
        mesh=mesh,
        in_specs=(rows, P(("rep", "shard")), rows, rows, two, two, two, two, one, one, two, three, three, three),
        out_specs=(rows, rows, two, two, two, two, one, one, two, three, three, three),
        check_vma=False,
    )
```

```python
import functools
import math

import jax
import jax.numpy as jnp
from jax import lax
from jax.experimental import pallas as pl
from jax.experimental.pallas import tpu as pltpu
from jax.sharding import PartitionSpec as P

QUERY_HEADS = 16
KEY_VALUE_HEADS = 8
HEAD_SIZE = 64
CAP = 96
LANES = 128
MOST_GATHERED = 4

epsilon = 1e-06
score_scale = 0.015625
branch_scale = 0.22
masked_value = -1e30

f32 = jnp.float32
bf16 = jnp.bfloat16
MESH = pl.DeviceIdType.MESH


def dot(left, right, contract=((1,), (0,))):
    return lax.dot_general(left, right, (contract, ((), ())), preferred_element_type=f32)

def slot_ranks(gates):
    tokens = gates.shape[1]
    named = gates > 0
    before = lax.broadcasted_iota(jnp.int32, (tokens, tokens), 0) < lax.broadcasted_iota(jnp.int32, (tokens, tokens), 1)
    rank = dot(named.astype(f32).astype(bf16), before.astype(f32).astype(bf16))
    return jnp.where(named, rank, -1.0)

def pick_row(table, row):
    here = lax.broadcasted_iota(jnp.int32, table.shape, 0) == row
    return jnp.sum(jnp.where(here, table, 0.0), axis=0, keepdims=True)

def slot_one_hot(ranks, first, local):
    tokens = ranks.shape[1]
    slot = lax.broadcasted_iota(jnp.int32, (CAP, tokens), 0).astype(f32)
    return [jnp.where(pick_row(ranks, first + l) == slot, 1.0, 0.0) for l in range(local)]

def gather_block(x, c, gates, first, local, xg_ref, cg_ref, sg_ref, at):
    ranks = slot_ranks(gates)
    parts = slot_one_hot(ranks, first, local)
    table = jnp.concatenate(parts, axis=0).astype(bf16)
    xg = dot(table, x).astype(bf16)
    cg = dot(table, c).astype(bf16)
    for l in range(local):
        rows = slice(l * CAP, (l + 1) * CAP)
        xg_ref[l, pl.ds(at, CAP), :] = xg[rows]
        cg_ref[l, pl.ds(at, CAP), :] = cg[rows]
        gate = jnp.sum(parts[l] * pick_row(gates, first + l), axis=1, keepdims=True)
        sg_ref[l, pl.ds(at, CAP), :] = branch_scale * gate
    return parts

def expert_parts(xg, cg, scale, wg, wu, wd):
    gate_part = dot(xg, wg)
    up_part = dot(xg, wu)
    raw = dot(cg, wd, ((1,), (1,)))
    sigma = 1.0 / (1.0 + jnp.exp(-gate_part))
    act = gate_part * sigma
    inner = act * up_part
    d_inner = raw * scale
    d_gate = (d_inner * up_part * (sigma + act * (1.0 - sigma))).astype(bf16)
    d_up = (d_inner * act).astype(bf16)
    scaled = (inner * scale).astype(bf16)
    return inner, raw, d_gate, d_up, scaled

def sums_kernel(nb, x_hbm, c_hbm, g_ref, wg_hbm, wu_hbm, wd_hbm, og_hbm, ou_hbm, od_hbm,
                xbuf, cbuf, wg, wu, wd, ag, au, ad, xg_ref, cg_ref, sg_ref, sem, wsem):
    local = wg.shape[0]
    blocks = x_hbm.shape[0]
    chunks = blocks // nb
    first = lax.axis_index("shard") * local
    def fetch(i, slot):
        return (pltpu.make_async_copy(x_hbm.at[pl.ds(i * nb, nb)], xbuf.at[slot], sem.at[0, slot]),
                pltpu.make_async_copy(c_hbm.at[pl.ds(i * nb, nb)], cbuf.at[slot], sem.at[1, slot]))
    for cp in fetch(0, 0):
        cp.start()
    weights = [pltpu.make_async_copy(a, b, wsem.at[i]) for i, (a, b) in enumerate(((wg_hbm, wg), (wu_hbm, wu), (wd_hbm, wd)))]
    for cp in weights:
        cp.start()
    ag[...] = jnp.zeros_like(ag)
    au[...] = jnp.zeros_like(au)
    ad[...] = jnp.zeros_like(ad)
    for cp in weights:
        cp.wait()

    def chunk(i, carry):
        slot = lax.rem(i, 2)
        @pl.when(i + 1 < chunks)
        def _():
            for cp in fetch(i + 1, 1 - slot):
                cp.start()
        for cp in fetch(i, slot):
            cp.wait()
        def block(b, carry):
            gather_block(xbuf[slot, b], cbuf[slot, b], g_ref[i * nb + b], first, local, xg_ref, cg_ref, sg_ref,
                         pl.multiple_of(b * CAP, CAP))
            return carry
        lax.fori_loop(0, nb, block, 0)
        def expert(l, carry):
            xg, cg = xg_ref[l], cg_ref[l]
            _, _, d_gate, d_up, scaled = expert_parts(xg, cg, sg_ref[l], wg[l], wu[l], wd[l])
            ag[l] += dot(xg, d_gate, ((0,), (0,)))
            au[l] += dot(xg, d_up, ((0,), (0,)))
            ad[l] += dot(scaled, cg, ((0,), (0,)))
            return carry
        lax.fori_loop(0, local, expert, 0)
        return carry
    lax.fori_loop(0, chunks, chunk, 0)
    outs = [pltpu.make_async_copy(a, b, wsem.at[i]) for i, (a, b) in enumerate(((ag, og_hbm), (au, ou_hbm), (ad, od_hbm)))]
    for cp in outs:
        cp.start()
    for cp in outs:
        cp.wait()

def moe_sums(x, c, gates, wg, wu, wd, nb=4):
    _, tokens, width = x.shape
    local, _, hidden = wg.shape
    any_ = pl.BlockSpec(memory_space=pl.ANY)
    rows = nb * CAP
    return pl.pallas_call(
        functools.partial(sums_kernel, nb),
        out_shape=[jax.ShapeDtypeStruct(w.shape, f32) for w in (wg, wu, wd)],
        in_specs=[any_, any_, pl.BlockSpec(memory_space=pltpu.VMEM), any_, any_, any_],
        out_specs=[any_] * 3,
        scratch_shapes=[
            pltpu.VMEM((2, nb, tokens, width), bf16), pltpu.VMEM((2, nb, tokens, width), bf16),
            pltpu.VMEM(wg.shape, bf16), pltpu.VMEM(wu.shape, bf16), pltpu.VMEM(wd.shape, bf16),
            pltpu.VMEM(wg.shape, f32), pltpu.VMEM(wu.shape, f32), pltpu.VMEM(wd.shape, f32),
            pltpu.VMEM((local, rows, width), bf16), pltpu.VMEM((local, rows, width), bf16), pltpu.VMEM((local, rows, 1), f32),
            pltpu.SemaphoreType.DMA((2, 2)), pltpu.SemaphoreType.DMA((3,)),
        ],
        compiler_params=pltpu.CompilerParams(vmem_limit_bytes=60 << 20),
        name="expert_sums",
    )(x, c, gates, wg, wu, wd)


def norm_scale(rows):
    return lax.rsqrt(jnp.mean(rows * rows, axis=-1, keepdims=True) + epsilon)

def flip(index, bit):
    return index + bit - 2 * bit * ((index // bit) % 2)

def turned(index, core, step, bits):
    return (1 - core) * flip(index, bits[step]) + core * flip(index, bits[-1 - step])

class PlaneGather:
    def __init__(self, buf, own, send, recv, base=0):
        self.buf, self.own, self.send, self.recv, self.base = buf, own, send, recv, base
        self.rep, self.me = lax.axis_index("rep"), lax.axis_index("shard")
        self.core = self.me % 2
        shards = lax.axis_size("shard")
        self.bits = [1 << i for i in range(1, shards.bit_length() - 1)]
        self.steps = len(self.bits)

    @staticmethod
    def copies(shards):
        return (shards // 2 - 1) + shards // 2

    def owner(self, of, subset):
        for step in range(self.steps):
            if subset >> step & 1:
                of = turned(of, self.core, step, self.bits)
        return of

    def copy(self, number, subset, target):
        owner = self.owner(self.me, subset)
        return pltpu.make_async_remote_copy(
            src_ref=self.buf.at[owner] if subset else self.own, dst_ref=self.buf.at[owner],
            send_sem=self.send.at[self.base + number], recv_sem=self.recv.at[self.base + number],
            device_id=(self.rep, target), device_id_type=MESH,
        )

    def chip_copy(self, step, subset):
        return self.copy((1 << step) - 1 + subset, subset, turned(self.me, self.core, step, self.bits))

    def core_copy(self, subset):
        return self.copy((1 << self.steps) - 1 + subset, subset, flip(self.me, 1))

    def start(self):
        for step in range(self.steps):
            self.chip_copy(step, 0).start()
        self.core_copy(0).start()

    def forward(self, step):
        for subset in range(1 << step):
            self.chip_copy(step, subset).wait_recv()
            whole = subset + (1 << step)
            for later in range(step + 1, self.steps):
                self.chip_copy(later, whole).start()
            self.core_copy(whole).start()

    def finish(self):
        for subset in range(1 << self.steps):
            self.core_copy(subset).wait_recv()
        self.sent()

    def sent(self):
        for step in range(self.steps):
            for subset in range(1 << step):
                self.chip_copy(step, subset).wait_send()
        for subset in range(1 << self.steps):
            self.core_copy(subset).wait_send()

class RepSends:
    def __init__(self, buf, own, send, recv, base=0):
        rep, me, reps = lax.axis_index("rep"), lax.axis_index("shard"), lax.axis_size("rep")
        self.copies = [
            pltpu.make_async_remote_copy(
                src_ref=own, dst_ref=buf.at[rep], send_sem=send.at[base + j - 1], recv_sem=recv.at[base + j - 1],
                device_id=((rep + j) % reps, me), device_id_type=MESH,
            )
            for j in range(1, reps)
        ]

    def start(self):
        for copy in self.copies:
            copy.start()

    def finish(self):
        for copy in self.copies:
            copy.wait()


def rotate(v, cosine, sine, sign):
    lane = lax.broadcasted_iota(jnp.int32, v.shape, 1) % HEAD_SIZE
    half = HEAD_SIZE // 2
    low = lane < half
    other = jnp.where(low, -pltpu.roll(v, LANES - half, 1), pltpu.roll(v, half, 1))
    return v * cosine + sign * other * sine

def two_heads(v):
    low = lax.broadcasted_iota(jnp.int32, v.shape, 1) < HEAD_SIZE
    zero = jnp.zeros_like(v)
    return jnp.concatenate([jnp.where(low, v, zero), jnp.where(low, zero, v)], axis=0)

def one_head_twice(pair, odd):
    high = lax.broadcasted_iota(jnp.int32, pair.shape, 1) // HEAD_SIZE
    wide = pair.astype(f32)
    return jnp.where(high == odd, wide, pltpu.roll(wide, HEAD_SIZE, 1)).astype(pair.dtype)

def probabilities(query2, keys, prefix_len):
    rows = query2.shape[0] // 2
    raw = dot(query2, keys, ((1,), (1,)))
    row = lax.broadcasted_iota(jnp.int32, raw.shape, 0) % rows
    col = lax.broadcasted_iota(jnp.int32, raw.shape, 1)
    scores = jnp.where((col <= row) | (col < prefix_len), raw * score_scale, masked_value)
    weights = jnp.exp(scores - jnp.max(scores, axis=-1, keepdims=True))
    return weights / jnp.sum(weights, axis=-1, keepdims=True)

def lanes(j, count=1):
    return pl.ds(pl.multiple_of(j * LANES * count, LANES), LANES * count)

def front_kernel(spread, prefix_ref, tok_ref, routes_ref, cos_ref, sin_ref, mine_ref, cot_ref,
                 wall_out, cown_out, ccol_out, q_out, k_out, v_out, att_out, hid_out, x_out, gates_out, n1_out,
                 wbuf, qkv_ref, send, recv, csend, crecv, zsend, zrecv, lsem):
    count, width = tok_ref.shape
    kv_width = k_out.shape[1]
    experts = gates_out.shape[0]
    shards, depth, total = wbuf.shape
    me = lax.axis_index("shard")
    own = pltpu.make_async_copy(mine_ref, wbuf.at[me], lsem.at[0])
    own.start()
    gather = PlaneGather(wbuf, mine_ref, send, recv)
    gather.start()
    far = RepSends(ccol_out, cot_ref, zsend, zrecv)
    if spread:
        far.start()
    near = PlaneGather(cown_out, cot_ref, csend, crecv)
    own_cot = pltpu.make_async_copy(cot_ref, cown_out.at[me], lsem.at[2])
    own_cot.start()
    own.wait()
    inputs = tok_ref[...].astype(f32)
    scaled = inputs * norm_scale(inputs)
    for step in range(gather.steps):
        gather.forward(step)
    gather.finish()
    near.start()
    keep = pltpu.make_async_copy(wbuf, wall_out, lsem.at[1])
    keep.start()
    cut = [0, width, width + kv_width, width + 2 * kv_width, 2 * width + 2 * kv_width]
    small = wbuf[:, :, cut[4]:].reshape(shards * depth, total - cut[4])
    wide = small.astype(f32).T
    gain_one, gain_two = wide[experts:experts + 1], wide[experts + 1:experts + 2]
    n1_out[...] = (scaled * gain_one).astype(bf16)

    def project(j, carry):
        w = wbuf[:, :, lanes(j, 2)].reshape(shards * depth, 2 * LANES)
        qkv_ref[:, lanes(j, 2)] = dot(n1_out[...], w)
        return carry
    lax.fori_loop(0, cut[3] // (2 * LANES), project, 0)
    cosine, sine = cos_ref[...], sin_ref[...]
    for j in range(width // LANES):
        q_out[:, j * LANES:(j + 1) * LANES] = rotate(qkv_ref[:, j * LANES:(j + 1) * LANES], cosine, sine, 1.0).astype(bf16)
    for j in range(kv_width // LANES):
        at = slice(cut[1] + j * LANES, cut[1] + (j + 1) * LANES)
        k_out[:, j * LANES:(j + 1) * LANES] = rotate(qkv_ref[:, at], cosine, sine, 1.0).astype(bf16)
    v_out[...] = qkv_ref[:, cut[2]:cut[3]].astype(bf16)
    prefix_len = prefix_ref[0]

    near.forward(0)

    def head(j, carry):
        keys = one_head_twice(k_out[:, lanes(j // 2)], j % 2)
        values = one_head_twice(v_out[:, lanes(j // 2)], j % 2)
        prob = probabilities(two_heads(q_out[:, lanes(j)]), keys, prefix_len)
        both = dot(prob.astype(bf16), values)
        low = lax.broadcasted_iota(jnp.int32, (count, LANES), 1) < HEAD_SIZE
        att_out[:, lanes(j)] = jnp.where(low, both[:count], both[count:]).astype(bf16)
        return carry
    lax.fori_loop(0, KEY_VALUE_HEADS, head, 0)
    for step in range(1, near.steps):
        near.forward(step)

    def project_out(j, carry):
        w = wbuf[:, :, pl.ds(pl.multiple_of(cut[3] + j * 2 * LANES, LANES), 2 * LANES)].reshape(shards * depth, 2 * LANES)
        qkv_ref[:, lanes(j, 2)] = dot(att_out[...], w)
        return carry
    lax.fori_loop(0, width // (2 * LANES), project_out, 0)
    hidden = inputs + branch_scale * qkv_ref[:, :width]
    hid_out[...] = hidden
    x = (hidden * norm_scale(hidden) * gain_two).astype(bf16)
    x_out[...] = x
    logits = dot(x, small).T[:experts]
    expert = lax.broadcasted_iota(jnp.int32, (experts, count), 0)
    named = expert < 0
    for k in range(routes_ref.shape[0]):
        named = named | (routes_ref[k:k + 1, :] == expert)
    top = jnp.max(jnp.where(named, logits, masked_value), axis=0, keepdims=True)
    weights = jnp.where(named, jnp.exp(jnp.where(named, logits - top, 0.0)), 0.0)
    gates_out[...] = weights / jnp.sum(weights, axis=0, keepdims=True)
    keep.wait()
    near.finish()
    own_cot.wait()
    if spread:
        far.finish()

def front(tokens, prefix, routes, mine, cot, cosine, sine, experts, kv_width, spread):
    count, width = tokens.shape
    shards, reps = lax.axis_size("shard"), lax.axis_size("rep")
    depth, total = mine.shape
    v = pl.BlockSpec(memory_space=pltpu.VMEM)
    any_ = pl.BlockSpec(memory_space=pl.ANY)
    sds = jax.ShapeDtypeStruct
    n = PlaneGather.copies(shards)
    return pl.pallas_call(
        functools.partial(front_kernel, spread),
        out_shape=[
            sds((shards, depth, total), bf16), sds((shards, count, width), bf16), sds((reps, count, width), bf16), sds((count, width), bf16), sds((count, kv_width), bf16), sds((count, kv_width), bf16),
            sds((count, width), bf16), sds((count, width), f32), sds((count, width), bf16), sds((experts, count), f32), sds((count, width), bf16),
        ],
        in_specs=[pl.BlockSpec(memory_space=pltpu.SMEM), v, v, v, v, any_, any_],
        out_specs=[any_] * 3 + [v] * 8,
        scratch_shapes=[
            pltpu.VMEM((shards, depth, total), bf16), pltpu.VMEM((count, width + 2 * kv_width), f32),
            *[pltpu.SemaphoreType.DMA((k,)) for k in (n, n, n, n, reps, reps, 3)],
        ],
        compiler_params=pltpu.CompilerParams(vmem_limit_bytes=60 << 20, has_side_effects=True),
        name="front",
    )(prefix, tokens, routes, cosine, sine, mine, cot)

def share_order(steps):
    groups = [[u for u in range(1 << steps) if u % (2 << k) == 1 << k] for k in range(steps)]
    return groups + [[0]]


class PlaneReduce:
    def __init__(self, mine, theirs, from_core, from_chip, csend, crecv, send, recv):
        self.mine, self.theirs, self.from_core, self.from_chip = mine, theirs, from_core, from_chip
        self.csend, self.crecv, self.send, self.recv = csend, crecv, send, recv
        self.rep, self.me = lax.axis_index("rep"), lax.axis_index("shard")
        self.core = self.me % 2
        self.bits = [1 << i for i in range(1, lax.axis_size("shard").bit_length() - 1)]
        self.steps = len(self.bits)

    def owner(self, core, u):
        at = flip(self.me, 1) if core else self.me
        of = (1 - self.core) if core else self.core
        for step in range(self.steps):
            if u >> step & 1:
                at = turned(at, of, step, self.bits)
        return at

    def core_copy(self, u):
        return pltpu.make_async_remote_copy(
            src_ref=self.theirs.at[u], dst_ref=self.from_core.at[u], send_sem=self.csend.at[u], recv_sem=self.crecv.at[u],
            device_id=(self.rep, flip(self.me, 1)), device_id_type=MESH,
        )

    def slot(self, step, u):
        return (1 << self.steps) - (1 << (self.steps - step)) + (u >> (step + 1))

    def chip_copy(self, step, u):
        slot = self.slot(step, u)
        return pltpu.make_async_remote_copy(
            src_ref=self.mine.at[u], dst_ref=self.from_chip.at[slot], send_sem=self.send.at[slot], recv_sem=self.recv.at[slot],
            device_id=(self.rep, turned(self.me, self.core, step, self.bits)), device_id_type=MESH,
        )

    def total(self, u, before, rows):
        whole = self.mine[u, rows].astype(f32) + self.from_core[u, rows].astype(f32)
        for step in range(before):
            whole = whole + self.from_chip[self.slot(step, u), rows].astype(f32)
        return whole

    def send_on(self, step, u):
        self.core_copy(u).wait_recv()
        count = self.mine.shape[1]
        piece = 32

        def add(i, carry):
            rows = pl.ds(pl.multiple_of(i * piece, piece), piece)
            self.mine[u, rows] = self.total(u, step, rows).astype(bf16)
            return carry
        lax.fori_loop(0, count // piece, add, 0)
        self.chip_copy(step, u).start()

    def arrive(self, step):
        for u in range(1 << self.steps):
            if u % (2 << step) == 1 << step:
                self.chip_copy(step, u).wait_recv()

    def last(self, out):
        self.core_copy(0).wait_recv()
        count = self.mine.shape[1]
        piece = 32

        def add(i, carry):
            rows = pl.ds(pl.multiple_of(i * piece, piece), piece)
            out[rows] = self.total(0, self.steps, rows)
            return carry
        lax.fori_loop(0, count // piece, add, 0)

    def finish(self):
        for u in range(1 << self.steps):
            self.core_copy(u).wait_send()
        for step in range(self.steps):
            for u in range(1 << self.steps):
                if u % (2 << step) == 1 << step:
                    self.chip_copy(step, u).wait_send()


def own_kernel(spread, nb, x_ref, gates_ref, c_hbm, wg_hbm, wu_hbm, wd_hbm,
               xown_out, xcol_out, gown_out, gcol_out, back_out, dg_out,
               wg, wu, wd, xb, cb, xg_ref, cg_ref, sg_ref, y_ref, ds_ref, mine, theirs, from_core, from_chip,
               gown, gcol, dgs, dgr,
               xs, xr, zxs, zxr, zgs, zgr, gs, gr, dss, dsr, css, csr, hs, hr, wsem, bsem, lsem):
    count, width = x_ref.shape
    local, _, hidden = wg.shape
    rep, me = lax.axis_index("rep"), lax.axis_index("shard")
    shards = lax.axis_size("shard")
    first = me * local
    near = PlaneGather(xown_out, x_ref, xs, xr)
    near.start()
    gown[me] = gates_ref[...]

    def peer(j):
        return (rep, (me + j) % shards)

    gate_sends = [
        pltpu.make_async_remote_copy(
            src_ref=gates_ref, dst_ref=gown.at[me], send_sem=gs.at[j - 1], recv_sem=gr.at[j - 1],
            device_id=peer(j), device_id_type=MESH,
        )
        for j in range(1, shards)
    ]
    for copy in gate_sends:
        copy.start()
    far = [RepSends(xcol_out, x_ref, zxs, zxr), RepSends(gcol, gates_ref, zgs, zgr)] if spread else []
    for sends in far:
        sends.start()
    own_x = pltpu.make_async_copy(x_ref, xown_out.at[me], lsem)
    own_x.start()
    weights = [pltpu.make_async_copy(a, b, wsem.at[i]) for i, (a, b) in enumerate(((wg_hbm, wg), (wu_hbm, wu), (wd_hbm, wd)))]
    for copy in weights:
        copy.start()
    reduce = PlaneReduce(mine, theirs, from_core, from_chip, css, csr, hs, hr)
    for copy in gate_sends:
        copy.wait_recv()
    for step in range(near.steps):
        near.forward(step)
    own_x.wait()
    for subset in range(1 << near.steps):
        near.core_copy(subset).wait_recv()
    for copy in weights:
        copy.wait()

    groups = share_order(reduce.steps)
    order = [u for group in groups for u in group]
    half = nb // 2
    dg_sends = []

    def fetch(at, slot):
        return (pltpu.make_async_copy(xown_out.at[at], xb.at[slot], bsem.at[0, slot]),
                pltpu.make_async_copy(c_hbm.at[at], cb.at[slot], bsem.at[1, slot]))

    plan = []
    for q in range(len(order) // half):
        for u in order[q * half:(q + 1) * half]:
            plan += [(1, u), (0, u)]
    owners = [reduce.owner(core, u) for core, u in plan]
    for copy in fetch(owners[0], 0):
        copy.start()
    for q in range(len(order) // half):
        for b in range(nb):
            n = q * nb + b
            if n + 1 < len(plan):
                for copy in fetch(owners[n + 1], (n + 1) % 2):
                    copy.start()
            for copy in fetch(owners[n], n % 2):
                copy.wait()
            gather_block(xb[n % 2], cb[n % 2], gown[owners[n]], first, local, xg_ref, cg_ref, sg_ref, b * CAP)

        def expert(l, carry):
            inner, raw, d_gate, d_up, scaled = expert_parts(xg_ref[l], cg_ref[l], sg_ref[l], wg[l], wu[l], wd[l])
            ds_ref[l] = branch_scale * jnp.sum(inner * raw, axis=1, keepdims=True)
            rows = pl.ds(pl.multiple_of(l * CAP, CAP), CAP)
            out = dot(scaled, wd[l]).astype(bf16)
            d_in = (dot(d_gate, wg[l], ((1,), (1,))) + dot(d_up, wu[l], ((1,), (1,)))).astype(bf16)
            for b in range(nb):
                y_ref[b, rows, :width] = out[b * CAP:(b + 1) * CAP]
                y_ref[b, rows, width:] = d_in[b * CAP:(b + 1) * CAP]
            return carry
        lax.fori_loop(0, local, expert, 0)
        for b in range(nb):
            core, u = plan[q * nb + b]
            at = owners[q * nb + b]
            parts = slot_one_hot(slot_ranks(gown[at]), first, local)
            table = jnp.concatenate(parts, axis=0).astype(bf16)
            (theirs if core else mine)[u] = dot(table, y_ref[b], ((0,), (0,))).astype(bf16)
            if core:
                reduce.core_copy(u).start()
            dgs[at] = jnp.concatenate(
                [jnp.sum(parts[l] * ds_ref[l, b * CAP:(b + 1) * CAP], axis=0, keepdims=True) for l in range(local)], axis=0
            )
        for step, group in enumerate(groups[:-1]):
            done = order[:(q + 1) * half]
            fresh = order[q * half:(q + 1) * half]
            if group[-1] in fresh:
                if step:
                    reduce.arrive(step - 1)
                for u in group:
                    reduce.send_on(step, u)
    for j in range(1, shards):
        copy = pltpu.make_async_remote_copy(
            src_ref=dgs.at[(me + j) % shards], dst_ref=dgr.at[me], send_sem=dss.at[j - 1], recv_sem=dsr.at[j - 1],
            device_id=peer(j), device_id_type=MESH,
        )
        copy.start()
        dg_sends.append(copy)
    dgr[me] = dgs[me]
    gown_out[...] = gown[...]
    reduce.arrive(reduce.steps - 1)
    reduce.last(back_out)
    for copy in dg_sends:
        copy.wait()
    dg_out[...] = dgr[...]
    reduce.finish()
    near.sent()
    for copy in gate_sends:
        copy.wait_send()
    for sends in far:
        sends.finish()
    if spread:
        gcol_out[...] = gcol[...]


def moe_own(x, gates, c, wg, wu, wd, spread, nb=4):
    count, width = x.shape
    local, _, hidden = wg.shape
    shards, reps = lax.axis_size("shard"), lax.axis_size("rep")
    experts = local * shards
    v = pl.BlockSpec(memory_space=pltpu.VMEM)
    any_ = pl.BlockSpec(memory_space=pl.ANY)
    sds = jax.ShapeDtypeStruct
    n = PlaneGather.copies(shards)
    rows = nb * CAP
    half = shards // 2
    dma = lambda *k: pltpu.SemaphoreType.DMA(k)
    return pl.pallas_call(
        functools.partial(own_kernel, spread, nb),
        out_shape=[
            sds((shards, count, width), bf16), sds((reps, count, width), bf16), sds((shards, experts, count), f32),
            sds((reps, experts, count), f32), sds((count, 2 * width), f32), sds((shards, local, count), f32),
        ],
        in_specs=[v, v, any_, any_, any_, any_],
        out_specs=[any_, any_, v, v, v, v],
        scratch_shapes=[
            pltpu.VMEM(wg.shape, bf16), pltpu.VMEM(wu.shape, bf16), pltpu.VMEM(wd.shape, bf16),
            pltpu.VMEM((2, count, width), bf16), pltpu.VMEM((2, count, width), bf16),
            pltpu.VMEM((local, rows, width), bf16), pltpu.VMEM((local, rows, width), bf16), pltpu.VMEM((local, rows, 1), f32),
            pltpu.VMEM((nb, local * CAP, 2 * width), bf16), pltpu.VMEM((local, rows, 1), f32),
            pltpu.VMEM((half, count, 2 * width), bf16), pltpu.VMEM((half, count, 2 * width), bf16),
            pltpu.VMEM((half, count, 2 * width), bf16), pltpu.VMEM((half - 1, count, 2 * width), bf16),
            pltpu.VMEM((shards, experts, count), f32), pltpu.VMEM((reps, experts, count), f32),
            pltpu.VMEM((shards, local, count), f32), pltpu.VMEM((shards, local, count), f32),
            dma(n), dma(n), dma(reps), dma(reps), dma(reps), dma(reps), dma(shards), dma(shards), dma(shards), dma(shards),
            dma(half), dma(half), dma(half), dma(half), dma(3), dma(2, 2), pltpu.SemaphoreType.DMA,
        ],
        compiler_params=pltpu.CompilerParams(vmem_limit_bytes=60 << 20, has_side_effects=True),
        name="own_experts",
    )(x, gates, c, wg, wu, wd)

def spread_kernel(nb, xown_hbm, cown_hbm, xcol_hbm, ccol_hbm, gown_ref, gcol_ref, wg_hbm, wu_hbm, wd_hbm,
                  xoth_hbm, coth_hbm, og_hbm, ou_hbm, od_hbm,
                  xbuf, cbuf, wg, wu, wd, ag, au, ad, xg_ref, cg_ref, sg_ref, goth, send, recv, bsem, wsem, lsem):
    local = wg.shape[0]
    shards = gown_ref.shape[0]
    rep, me = lax.axis_index("rep"), lax.axis_index("shard")
    reps = lax.axis_size("rep")
    first = me * local
    chunks = shards // nb

    def gathers(j):
        other = (rep + j) % reps
        return [
            PlaneGather(buf.at[j - 1], own.at[other], send.at[j - 1, i], recv.at[j - 1, i])
            for i, (buf, own) in enumerate(((xoth_hbm, xcol_hbm), (coth_hbm, ccol_hbm), (goth, gcol_ref)))
        ]

    def own_copies(j):
        other = (rep + j) % reps
        return (pltpu.make_async_copy(xcol_hbm.at[other], xoth_hbm.at[j - 1, me], lsem.at[0]),
                pltpu.make_async_copy(ccol_hbm.at[other], coth_hbm.at[j - 1, me], lsem.at[1]))

    def begin(j):
        for gather in gathers(j):
            gather.start()
        for copy in own_copies(j):
            copy.start()
        goth[j - 1, me] = gcol_ref[(rep + j) % reps]
        for copy in own_copies(j):
            copy.wait()

    def forward(j):
        for gather in gathers(j):
            gather.forward(0)

    def end(j):
        for gather in gathers(j):
            for step in range(1, gather.steps):
                gather.forward(step)
        for gather in gathers(j):
            gather.finish()

    def fetch(x, c, q, slot):
        return (pltpu.make_async_copy(x.at[pl.ds(q * nb, nb)], xbuf.at[slot], bsem.at[0, slot]),
                pltpu.make_async_copy(c.at[pl.ds(q * nb, nb)], cbuf.at[slot], bsem.at[1, slot]))

    def replica(x, c, g, between):
        for copy in fetch(x, c, 0, 0):
            copy.start()

        def chunk(q, carry):
            slot = lax.rem(q, 2)

            @pl.when(q + 1 < chunks)
            def _():
                for copy in fetch(x, c, q + 1, 1 - slot):
                    copy.start()
            for copy in fetch(x, c, q, slot):
                copy.wait()

            def block(b, carry):
                gather_block(xbuf[slot, b], cbuf[slot, b], g[q * nb + b], first, local, xg_ref, cg_ref, sg_ref,
                             pl.multiple_of(b * CAP, CAP))
                return carry
            lax.fori_loop(0, nb, block, 0)

            def expert(l, carry):
                xg, cg = xg_ref[l], cg_ref[l]
                _, _, d_gate, d_up, scaled = expert_parts(xg, cg, sg_ref[l], wg[l], wu[l], wd[l])
                ag[l] += dot(xg, d_gate, ((0,), (0,)))
                au[l] += dot(xg, d_up, ((0,), (0,)))
                ad[l] += dot(scaled, cg, ((0,), (0,)))
                return carry
            lax.fori_loop(0, local, expert, 0)

            @pl.when(q == 0)
            def _():
                between()
            return carry
        lax.fori_loop(0, chunks, chunk, 0)

    begin(1)
    weights = [pltpu.make_async_copy(a, b, wsem.at[i]) for i, (a, b) in enumerate(((wg_hbm, wg), (wu_hbm, wu), (wd_hbm, wd)))]
    for copy in weights:
        copy.start()
    ag[...] = jnp.zeros_like(ag)
    au[...] = jnp.zeros_like(au)
    ad[...] = jnp.zeros_like(ad)
    for copy in weights:
        copy.wait()

    def next_of(j):
        def between():
            @pl.when(j + 1 < reps)
            def _():
                forward(j + 1)

            @pl.when(j + 2 < reps)
            def _():
                begin(j + 2)
        return between

    replica(xown_hbm, cown_hbm, gown_ref, next_of(0))
    end(1)

    def others(j, carry):
        replica(xoth_hbm.at[j - 1], coth_hbm.at[j - 1], goth.at[j - 1], next_of(j))

        @pl.when(j + 1 < reps)
        def _():
            end(j + 1)
        return carry
    lax.fori_loop(1, reps, others, 0)
    outs = [pltpu.make_async_copy(a, b, wsem.at[i]) for i, (a, b) in enumerate(((ag, og_hbm), (au, ou_hbm), (ad, od_hbm)))]
    for copy in outs:
        copy.start()
    for copy in outs:
        copy.wait()


def moe_spread_sums(xown, cown, xcol, ccol, gown, gcol, wg, wu, wd, nb=4):
    shards, count, width = xown.shape
    reps = xcol.shape[0]
    local, _, hidden = wg.shape
    any_ = pl.BlockSpec(memory_space=pl.ANY)
    v = pl.BlockSpec(memory_space=pltpu.VMEM)
    rows = nb * CAP
    n = PlaneGather.copies(shards)
    slots = reps * shards * local * CAP
    outs = pl.pallas_call(
        functools.partial(spread_kernel, nb),
        out_shape=[jax.ShapeDtypeStruct((reps - 1, shards, count, width), bf16)] * 2
        + [jax.ShapeDtypeStruct(w.shape, f32) for w in (wg, wu, wd)],
        in_specs=[any_, any_, any_, any_, v, v, any_, any_, any_],
        out_specs=[any_] * 5,
        scratch_shapes=[
            pltpu.VMEM((2, nb, count, width), bf16), pltpu.VMEM((2, nb, count, width), bf16),
            pltpu.VMEM(wg.shape, bf16), pltpu.VMEM(wu.shape, bf16), pltpu.VMEM(wd.shape, bf16),
            pltpu.VMEM(wg.shape, f32), pltpu.VMEM(wu.shape, f32), pltpu.VMEM(wd.shape, f32),
            pltpu.VMEM((local, rows, width), bf16), pltpu.VMEM((local, rows, width), bf16), pltpu.VMEM((local, rows, 1), f32),
            pltpu.VMEM((reps - 1, shards, *gown.shape[1:]), f32),
            pltpu.SemaphoreType.DMA((reps - 1, 3, n)), pltpu.SemaphoreType.DMA((reps - 1, 3, n)),
            pltpu.SemaphoreType.DMA((2, 2)), pltpu.SemaphoreType.DMA((3,)), pltpu.SemaphoreType.DMA((2,)),
        ],
        compiler_params=pltpu.CompilerParams(vmem_limit_bytes=60 << 20, has_side_effects=True),
        cost_estimate=pl.CostEstimate(
            flops=12 * slots * width * hidden, transcendentals=slots * hidden, bytes_accessed=4 * reps * shards * count * width
        ),
        name="spread_expert_sums",
    )(xown, cown, xcol, ccol, gown, gcol, wg, wu, wd)
    return outs[2:]

def rotary_tables(count):
    half = HEAD_SIZE // 2
    places = jnp.arange(count, dtype=f32)
    inverse = jnp.exp(jnp.arange(half, dtype=f32) * (-2.0 * math.log(10000.0) / HEAD_SIZE))
    angles = jnp.tile(places[:, None] * inverse[None, :], (1, LANES // half))
    return jnp.cos(angles), jnp.sin(angles)


def pack(w_query, key_weight, value_weight, w_out, w_router, norm_attn, norm_moe):
    small = jnp.concatenate([w_router, norm_attn[:, None], norm_moe[:, None]], axis=1)
    small = jnp.pad(small, ((0, 0), (0, LANES - small.shape[1])))
    return jnp.concatenate([w_query, key_weight, value_weight, w_out, small], axis=1)


def norm_backward(rows, scaling, gain, upstream):
    weighted = upstream * gain
    inner_mean = jnp.mean(weighted * rows, axis=-1, keepdims=True)
    gradient = scaling * weighted - rows * (scaling * scaling * scaling) * inner_mean
    return gradient, jnp.sum(upstream * rows * scaling, axis=0, keepdims=True)


def turn_back(rows, cosine, sine):
    count = rows.shape[0]
    half = HEAD_SIZE // 2
    shaped = rows.reshape(count, -1, HEAD_SIZE)
    first, second = shaped[..., :half], shaped[..., half:]
    c, s = cosine[:, None, :half], sine[:, None, :half]
    return jnp.concatenate([first * c + second * s, second * c - first * s], axis=-1).reshape(rows.shape)


def body(
    tokens, prefix, routes, cotangent, w_query, key_weight, value_weight, w_out,
    norm_attn, norm_moe, w_router, w_gate, w_up, w_down,
):
    count, width = tokens.shape
    local, _, hidden = w_gate.shape
    shards, reps = lax.axis_size("shard"), lax.axis_size("rep")
    experts = local * shards
    kv_width = key_weight.shape[1]
    me, rep = lax.axis_index("shard"), lax.axis_index("rep")
    group = QUERY_HEADS // KEY_VALUE_HEADS
    spread = reps <= MOST_GATHERED
    axes = ("rep", "shard") if spread else "shard"
    cosine, sine = rotary_tables(count)
    mine = pack(w_query, key_weight, value_weight, w_out, w_router, norm_attn, norm_moe)
    packed, cot_own, cot_col, query, keys, values, attended, hidden_one, normed_two, gates, normed_one = front(
        tokens, prefix, routes.T, mine, cotangent, cosine, sine, experts, kv_width, spread
    )
    packed = packed.reshape(width, -1)
    cuts = [width, width + kv_width, width + 2 * kv_width, 2 * width + 2 * kv_width]
    wo, small = packed[:, cuts[2]:cuts[3]], packed[:, cuts[3]:]
    wr = small[:, :experts]
    gain_one = small[:, experts].astype(f32)[None, :]
    gain_two = small[:, experts + 1].astype(f32)[None, :]
    x_own, x_col, gates_own, gates_col, back, d_gates = moe_own(
        normed_two, gates, cot_own, w_gate, w_up, w_down, spread
    )
    mix, d_in = back[:, :width], back[:, width:]
    d_gates = d_gates.reshape(experts, count)
    if spread:
        sums = moe_spread_sums(x_own, cot_own, x_col, cot_col, gates_own, gates_col, w_gate, w_up, w_down)
    else:
        sums = moe_sums(x_own, cot_own, gates_own, w_gate, w_up, w_down)
        sums = [lax.psum(a.astype(bf16), "rep").astype(f32) for a in sums]
    d_w_gate, d_w_up, d_w_down = sums

    inputs = tokens.astype(f32)
    cot = cotangent.astype(f32)
    scale_one, scale_two = norm_scale(inputs), norm_scale(hidden_one)
    result = (hidden_one + mix).astype(bf16)
    d_logits = (gates * (d_gates - jnp.sum(gates * d_gates, axis=0, keepdims=True))).astype(bf16)
    d_router = dot(normed_two, d_logits, ((0,), (1,)))
    d_normed_two = d_in + dot(d_logits, wr, ((0,), (1,)))
    d_hidden, d_gain_two = norm_backward(hidden_one, scale_two, gain_two, d_normed_two)
    d_hidden = d_hidden + cot
    d_projected = (branch_scale * d_hidden).astype(bf16)
    d_wo = dot(attended, d_projected, ((0,), (0,)))
    d_attended = dot(d_projected, wo, ((1,), (1,))).astype(bf16)
    query4 = query.reshape(count, KEY_VALUE_HEADS, group, HEAD_SIZE)
    keys3 = keys.reshape(count, KEY_VALUE_HEADS, HEAD_SIZE)
    values3 = values.reshape(count, KEY_VALUE_HEADS, HEAD_SIZE)
    raw = jnp.einsum("tngd,snd->ngts", query4, keys3, preferred_element_type=f32)
    place = jnp.arange(count, dtype=jnp.int32)
    visible = (place[None, :] <= place[:, None]) | (place[None, :] < prefix[0])
    probs = jax.nn.softmax(jnp.where(visible, raw * score_scale, masked_value), axis=-1)
    d_attended = d_attended.reshape(count, KEY_VALUE_HEADS, group, HEAD_SIZE)
    d_values = jnp.einsum("ngts,tngd->snd", probs.astype(bf16), d_attended, preferred_element_type=f32)
    d_probs = jnp.einsum("tngd,snd->ngts", d_attended, values3, preferred_element_type=f32)
    weighted = jnp.sum(probs * d_probs, axis=-1, keepdims=True)
    d_scores = (probs * (d_probs - weighted) * score_scale).astype(bf16)
    d_query = jnp.einsum("ngts,snd->tngd", d_scores, keys3, preferred_element_type=f32)
    d_keys = jnp.einsum("ngts,tngd->snd", d_scores, query4, preferred_element_type=f32)
    d_query = turn_back(d_query.reshape(count, -1), cosine, sine).astype(bf16)
    d_keys = turn_back(d_keys.reshape(count, -1), cosine, sine).astype(bf16)
    d_values = d_values.reshape(count, -1).astype(bf16)
    d_qkv = jnp.concatenate([d_query, d_keys, d_values], axis=1)
    d_w_qkv = dot(normed_one, d_qkv, ((0,), (0,)))
    d_normed_one = dot(d_qkv, packed[:, :cuts[2]], ((1,), (1,)))
    d_tokens, d_gain_one = norm_backward(inputs, scale_one, gain_one, d_normed_one)
    d_tokens = d_tokens + d_hidden
    small = jnp.concatenate([d_router, d_gain_one.T, d_gain_two.T], axis=1)
    small = jnp.pad(small, ((0, 0), (0, LANES - small.shape[1])))
    shares = jnp.concatenate([d_w_qkv, d_wo, small], axis=1).astype(bf16)
    shares = lax.psum_scatter(shares, "shard", scatter_dimension=0, tiled=True)
    totals = lax.psum(shares, "rep").astype(f32)
    d_wq, d_wk, d_wv, d_wo, small = jnp.split(totals, cuts, axis=1)
    return (
        result, d_tokens, d_wq, d_wk, d_wv, d_wo, small[:, experts], small[:, experts + 1],
        small[:, :experts], d_w_gate, d_w_up, d_w_down,
    )


def solution(mesh):
    rows = P(("rep", "shard"), None)
    one, two, three = P("shard"), P("shard", None), P("shard", None, None)
    return jax.shard_map(
        body,
        mesh=mesh,
        in_specs=(rows, P(("rep", "shard")), rows, rows, two, two, two, two, one, one, two, three, three, three),
        out_specs=(rows, rows, two, two, two, two, one, one, two, three, three, three),
        check_vma=False,
    )
```

```python
import functools
import math

import jax
import jax.numpy as jnp
import numpy as np
from jax import lax
from jax.experimental import pallas as pl
from jax.experimental.pallas import tpu as pltpu
from jax.sharding import PartitionSpec as P

QUERY_HEADS = 16
KEY_VALUE_HEADS = 8
HEAD_SIZE = 64
CAP = 96
LANES = 128
MOST_GATHERED = 4

epsilon = 1e-06
score_scale = 0.015625
branch_scale = 0.22
masked_value = -1e30

f32 = jnp.float32
bf16 = jnp.bfloat16
MESH = pl.DeviceIdType.MESH


def dot(left, right, contract=((1,), (0,))):
    return lax.dot_general(left, right, (contract, ((), ())), preferred_element_type=f32)

def slot_ranks(gates):
    tokens = gates.shape[1]
    named = gates > 0
    before = lax.broadcasted_iota(jnp.int32, (tokens, tokens), 0) < lax.broadcasted_iota(jnp.int32, (tokens, tokens), 1)
    rank = dot(named.astype(f32).astype(bf16), before.astype(f32).astype(bf16))
    return jnp.where(named, rank, -1.0)

def pick_row(table, row):
    here = lax.broadcasted_iota(jnp.int32, table.shape, 0) == row
    return jnp.sum(jnp.where(here, table, 0.0), axis=0, keepdims=True)

def slot_one_hot(ranks, first, local):
    tokens = ranks.shape[1]
    slot = lax.broadcasted_iota(jnp.int32, (CAP, tokens), 0).astype(f32)
    return [jnp.where(pick_row(ranks, first + l) == slot, 1.0, 0.0) for l in range(local)]

def gather_block(x, c, gates, first, local, xg_ref, cg_ref, sg_ref, at):
    ranks = slot_ranks(gates)
    parts = slot_one_hot(ranks, first, local)
    table = jnp.concatenate(parts, axis=0).astype(bf16)
    xg = dot(table, x).astype(bf16)
    cg = dot(table, c).astype(bf16)
    for l in range(local):
        rows = slice(l * CAP, (l + 1) * CAP)
        xg_ref[l, pl.ds(at, CAP), :] = xg[rows]
        cg_ref[l, pl.ds(at, CAP), :] = cg[rows]
        gate = jnp.sum(parts[l] * pick_row(gates, first + l), axis=1, keepdims=True)
        sg_ref[l, pl.ds(at, CAP), :] = branch_scale * gate
    return parts

def expert_parts(xg, cg, scale, wg, wu, wd):
    gate_part = dot(xg, wg)
    up_part = dot(xg, wu)
    raw = dot(cg, wd, ((1,), (1,)))
    sigma = 1.0 / (1.0 + jnp.exp(-gate_part))
    act = gate_part * sigma
    inner = act * up_part
    d_inner = raw * scale
    d_gate = (d_inner * up_part * (sigma + act * (1.0 - sigma))).astype(bf16)
    d_up = (d_inner * act).astype(bf16)
    scaled = (inner * scale).astype(bf16)
    return inner, raw, d_gate, d_up, scaled

def add_expert(l, xg_ref, cg_ref, sg_ref, wg, wu, wd, ag, au, ad):
    xg, cg = xg_ref[l], cg_ref[l]
    _, _, d_gate, d_up, scaled = expert_parts(xg, cg, sg_ref[l], wg[l], wu[l], wd[l])
    ag[l] += dot(xg, d_gate, ((0,), (0,)))
    au[l] += dot(xg, d_up, ((0,), (0,)))
    ad[l] += dot(scaled, cg, ((0,), (0,)))

def sums_kernel(nb, more, x_hbm, c_hbm, g_ref, wg_hbm, wu_hbm, wd_hbm, *rest):
    if len(x_hbm.shape) == 4:
        x_hbm, c_hbm = x_hbm.at[x_hbm.shape[0] - 1], c_hbm.at[c_hbm.shape[0] - 1]
    starts, (og_hbm, ou_hbm, od_hbm, *scratch) = rest[:3 * more], rest[3 * more:]
    sums_body(nb, starts, x_hbm, c_hbm, g_ref, wg_hbm, wu_hbm, wd_hbm, og_hbm, ou_hbm, od_hbm, *scratch)

def sums_body(nb, starts, x_hbm, c_hbm, g_ref, wg_hbm, wu_hbm, wd_hbm, og_hbm, ou_hbm, od_hbm,
                xbuf, cbuf, wg, wu, wd, ag, au, ad, xg_ref, cg_ref, sg_ref, sem, wsem, asem):
    local = wg.shape[0]
    blocks = x_hbm.shape[0]
    chunks = blocks // nb
    first = lax.axis_index("shard") * local
    def fetch(i, slot):
        return (pltpu.make_async_copy(x_hbm.at[pl.ds(i * nb, nb)], xbuf.at[slot], sem.at[0, slot]),
                pltpu.make_async_copy(c_hbm.at[pl.ds(i * nb, nb)], cbuf.at[slot], sem.at[1, slot]))
    for cp in fetch(0, 0):
        cp.start()
    weights = [pltpu.make_async_copy(a, b, wsem.at[i]) for i, (a, b) in enumerate(((wg_hbm, wg), (wu_hbm, wu), (wd_hbm, wd)))]
    for cp in weights:
        cp.start()
    loads = [
        pltpu.make_async_copy(a.at[l], b.at[l], asem.at[i, l])
        for l in range(local) for i, (a, b) in enumerate(zip(starts, (ag, au, ad)))
    ]
    for cp in loads:
        cp.start()
    if not starts:
        ag[...] = jnp.zeros_like(ag)
        au[...] = jnp.zeros_like(au)
        ad[...] = jnp.zeros_like(ad)
    for cp in weights:
        cp.wait()

    def chunk(i, carry):
        slot = lax.rem(i, 2)
        @pl.when(i + 1 < chunks)
        def _():
            for cp in fetch(i + 1, 1 - slot):
                cp.start()
        for cp in fetch(i, slot):
            cp.wait()
        def block(b, carry):
            gather_block(xbuf[slot, b], cbuf[slot, b], g_ref[i * nb + b], first, local, xg_ref, cg_ref, sg_ref,
                         pl.multiple_of(b * CAP, CAP))
            return carry
        lax.fori_loop(0, nb, block, 0)
        def expert(l, carry):
            if starts:
                @pl.when(i == 0)
                def _():
                    for k, (a, b) in enumerate(zip(starts, (ag, au, ad))):
                        pltpu.make_async_copy(a.at[l], b.at[l], asem.at[k, l]).wait()
            add_expert(l, xg_ref, cg_ref, sg_ref, wg, wu, wd, ag, au, ad)

            @pl.when(i == chunks - 1)
            def _():
                for k, (a, b) in enumerate(((ag, og_hbm), (au, ou_hbm), (ad, od_hbm))):
                    pltpu.make_async_copy(a.at[l], b.at[l], asem.at[k, l]).start()
            return carry
        lax.fori_loop(0, local, expert, 0)
        return carry
    lax.fori_loop(0, chunks, chunk, 0)
    for l in range(local):
        for k, (a, b) in enumerate(((ag, og_hbm), (au, ou_hbm), (ad, od_hbm))):
            pltpu.make_async_copy(a.at[l], b.at[l], asem.at[k, l]).wait()

def moe_sums(x, c, gates, wg, wu, wd, starts=(), nb=4):
    blocks, tokens, width = x.shape[-3:]
    local, _, hidden = wg.shape
    any_ = pl.BlockSpec(memory_space=pl.ANY)
    rows = nb * CAP
    return pl.pallas_call(
        functools.partial(sums_kernel, nb, bool(starts)),
        out_shape=[jax.ShapeDtypeStruct(w.shape, f32) for w in (wg, wu, wd)],
        in_specs=[any_, any_, pl.BlockSpec(memory_space=pltpu.VMEM), any_, any_, any_] + [any_] * len(starts),
        out_specs=[any_] * 3,
        scratch_shapes=[
            pltpu.VMEM((2, nb, tokens, width), bf16), pltpu.VMEM((2, nb, tokens, width), bf16),
            pltpu.VMEM(wg.shape, bf16), pltpu.VMEM(wu.shape, bf16), pltpu.VMEM(wd.shape, bf16),
            pltpu.VMEM(wg.shape, f32), pltpu.VMEM(wu.shape, f32), pltpu.VMEM(wd.shape, f32),
            pltpu.VMEM((local, rows, width), bf16), pltpu.VMEM((local, rows, width), bf16), pltpu.VMEM((local, rows, 1), f32),
            pltpu.SemaphoreType.DMA((2, 2)), pltpu.SemaphoreType.DMA((3,)), pltpu.SemaphoreType.DMA((3, local)),
        ],
        compiler_params=pltpu.CompilerParams(vmem_limit_bytes=60 << 20),
        cost_estimate=pl.CostEstimate(
            flops=12 * blocks * local * CAP * width * hidden, transcendentals=blocks * local * CAP * hidden,
            bytes_accessed=4 * blocks * tokens * width + 24 * wg.size,
        ),
        name="expert_sums",
    )(x, c, gates, wg, wu, wd, *starts)


def norm_scale(rows):
    return lax.rsqrt(jnp.mean(rows * rows, axis=-1, keepdims=True) + epsilon)

def flip(index, bit):
    return index + bit - 2 * bit * ((index // bit) % 2)

def turned(index, core, step, bits):
    return (1 - core) * flip(index, bits[step]) + core * flip(index, bits[-1 - step])

def greet(spread):
    rep, me = lax.axis_index("rep"), lax.axis_index("shard")
    shards, reps = lax.axis_size("shard"), lax.axis_size("rep")
    peers = [(rep, (me + j) % shards) for j in range(1, shards)]
    if spread:
        peers += [((rep + j) % reps, me) for j in range(1, reps)]
    barrier = pltpu.get_barrier_semaphore()
    for peer in peers:
        pl.semaphore_signal(barrier, inc=1, device_id=peer, device_id_type=MESH)
    pl.semaphore_wait(barrier, len(peers))


class PlaneGather:
    def __init__(self, buf, own, send, recv, base=0):
        self.buf, self.own, self.send, self.recv, self.base = buf, own, send, recv, base
        self.rep, self.me = lax.axis_index("rep"), lax.axis_index("shard")
        self.core = self.me % 2
        shards = lax.axis_size("shard")
        self.bits = [1 << i for i in range(1, shards.bit_length() - 1)]
        self.steps = len(self.bits)

    @staticmethod
    def copies(shards):
        return (shards // 2 - 1) + shards // 2

    def owner(self, of, subset):
        for step in range(self.steps):
            if subset >> step & 1:
                of = turned(of, self.core, step, self.bits)
        return of

    def copy(self, number, subset, target):
        owner = self.owner(self.me, subset)
        return pltpu.make_async_remote_copy(
            src_ref=self.buf.at[owner] if subset else self.own, dst_ref=self.buf.at[owner],
            send_sem=self.send.at[self.base + number], recv_sem=self.recv.at[self.base + number],
            device_id=(self.rep, target), device_id_type=MESH,
        )

    def chip_copy(self, step, subset):
        return self.copy((1 << step) - 1 + subset, subset, turned(self.me, self.core, step, self.bits))

    def core_copy(self, subset):
        return self.copy((1 << self.steps) - 1 + subset, subset, flip(self.me, 1))

    def start(self):
        for step in range(self.steps):
            self.chip_copy(step, 0).start()
        self.core_copy(0).start()

    def forward(self, step):
        for subset in range(1 << step):
            self.chip_copy(step, subset).wait_recv()
            whole = subset + (1 << step)
            for later in range(step + 1, self.steps):
                self.chip_copy(later, whole).start()
            self.core_copy(whole).start()

    def finish(self):
        for subset in range(1 << self.steps):
            self.core_copy(subset).wait_recv()
        self.sent()

    def sent(self):
        for step in range(self.steps):
            for subset in range(1 << step):
                self.chip_copy(step, subset).wait_send()
        for subset in range(1 << self.steps):
            self.core_copy(subset).wait_send()

class RepSends:
    def __init__(self, buf, own, send, recv, base=0):
        rep, me, reps = lax.axis_index("rep"), lax.axis_index("shard"), lax.axis_size("rep")
        self.copies = [
            pltpu.make_async_remote_copy(
                src_ref=own, dst_ref=buf.at[rep], send_sem=send.at[base + j - 1], recv_sem=recv.at[base + j - 1],
                device_id=((rep + j) % reps, me), device_id_type=MESH,
            )
            for j in range(1, reps)
        ]

    def start(self):
        for copy in self.copies:
            copy.start()

    def finish(self):
        for copy in self.copies:
            copy.wait()


def rotate(v, cosine, sine, sign):
    lane = lax.broadcasted_iota(jnp.int32, v.shape, 1) % HEAD_SIZE
    half = HEAD_SIZE // 2
    low = lane < half
    other = jnp.where(low, -pltpu.roll(v, LANES - half, 1), pltpu.roll(v, half, 1))
    return v * cosine + sign * other * sine

def two_heads(v):
    low = lax.broadcasted_iota(jnp.int32, v.shape, 1) < HEAD_SIZE
    zero = jnp.zeros_like(v)
    return jnp.concatenate([jnp.where(low, v, zero), jnp.where(low, zero, v)], axis=0)

def one_head_twice(pair, odd):
    high = lax.broadcasted_iota(jnp.int32, pair.shape, 1) // HEAD_SIZE
    wide = pair.astype(f32)
    return jnp.where(high == odd, wide, pltpu.roll(wide, HEAD_SIZE, 1)).astype(pair.dtype)

def probabilities(query2, keys, prefix_len):
    rows = query2.shape[0] // 2
    raw = dot(query2, keys, ((1,), (1,)))
    row = lax.broadcasted_iota(jnp.int32, raw.shape, 0) % rows
    col = lax.broadcasted_iota(jnp.int32, raw.shape, 1)
    scores = jnp.where((col <= row) | (col < prefix_len), raw * score_scale, masked_value)
    weights = jnp.exp(scores - jnp.max(scores, axis=-1, keepdims=True))
    return weights / jnp.sum(weights, axis=-1, keepdims=True)

def lanes(j, count=1):
    return pl.ds(pl.multiple_of(j * LANES * count, LANES), LANES * count)

def front_kernel(spread, prefix_ref, tok_ref, routes_ref, cos_ref, sin_ref, wq_hbm, wk_hbm, wv_hbm, wo_hbm, ws_hbm, cot_ref,
                 wall_out, cown_out, ccol_out, q_out, k_out, v_out, att_out, hid_out, x_out, gates_out, n1_out,
                 wbuf, qkv_ref, send, recv, csend, crecv, zsend, zrecv, lsem, osem):
    count, width = tok_ref.shape
    kv_width = k_out.shape[1]
    experts = gates_out.shape[0]
    shards, depth, total = wbuf.shape
    me = lax.axis_index("shard")
    own, at = [], 0
    for i, part in enumerate((wq_hbm, wk_hbm, wv_hbm, wo_hbm, ws_hbm)):
        own.append(pltpu.make_async_copy(part, wbuf.at[me, :, at:at + part.shape[1]], osem.at[i]))
        own[-1].start()
        at += part.shape[1]
    greet(spread)
    gather = PlaneGather(wbuf, wbuf.at[me], send, recv)
    for copy in own:
        copy.wait()
    gather.start()
    far = RepSends(ccol_out, cot_ref, zsend, zrecv)
    if spread:
        far.start()
    near = PlaneGather(cown_out, cot_ref, csend, crecv)
    own_cot = pltpu.make_async_copy(cot_ref, cown_out.at[me], lsem.at[2])
    own_cot.start()
    inputs = tok_ref[...].astype(f32)
    scaled = inputs * norm_scale(inputs)
    for step in range(gather.steps):
        gather.forward(step)
    gather.finish()
    near.start()
    keep = pltpu.make_async_copy(wbuf, wall_out, lsem.at[1])
    keep.start()
    cut = [0, width, width + kv_width, width + 2 * kv_width, 2 * width + 2 * kv_width]
    small = wbuf[:, :, cut[4]:].reshape(shards * depth, total - cut[4])
    wide = small.astype(f32).T
    gain_one, gain_two = wide[experts:experts + 1], wide[experts + 1:experts + 2]
    n1_out[...] = (scaled * gain_one).astype(bf16)

    def project(j, carry):
        w = wbuf[:, :, lanes(j, 2)].reshape(shards * depth, 2 * LANES)
        qkv_ref[:, lanes(j, 2)] = dot(n1_out[...], w)
        return carry
    lax.fori_loop(0, cut[3] // (2 * LANES), project, 0)
    cosine, sine = cos_ref[...], sin_ref[...]
    for j in range(width // LANES):
        q_out[:, j * LANES:(j + 1) * LANES] = rotate(qkv_ref[:, j * LANES:(j + 1) * LANES], cosine, sine, 1.0).astype(bf16)
    for j in range(kv_width // LANES):
        at = slice(cut[1] + j * LANES, cut[1] + (j + 1) * LANES)
        k_out[:, j * LANES:(j + 1) * LANES] = rotate(qkv_ref[:, at], cosine, sine, 1.0).astype(bf16)
    v_out[...] = qkv_ref[:, cut[2]:cut[3]].astype(bf16)
    prefix_len = prefix_ref[0]

    near.forward(0)

    def head(j, carry):
        keys = one_head_twice(k_out[:, lanes(j // 2)], j % 2)
        values = one_head_twice(v_out[:, lanes(j // 2)], j % 2)
        prob = probabilities(two_heads(q_out[:, lanes(j)]), keys, prefix_len)
        both = dot(prob.astype(bf16), values)
        low = lax.broadcasted_iota(jnp.int32, (count, LANES), 1) < HEAD_SIZE
        att_out[:, lanes(j)] = jnp.where(low, both[:count], both[count:]).astype(bf16)
        return carry
    lax.fori_loop(0, KEY_VALUE_HEADS, head, 0)
    for step in range(1, near.steps):
        near.forward(step)

    def project_out(j, carry):
        w = wbuf[:, :, pl.ds(pl.multiple_of(cut[3] + j * 2 * LANES, LANES), 2 * LANES)].reshape(shards * depth, 2 * LANES)
        qkv_ref[:, lanes(j, 2)] = dot(att_out[...], w)
        return carry
    lax.fori_loop(0, width // (2 * LANES), project_out, 0)
    hidden = inputs + branch_scale * qkv_ref[:, :width]
    hid_out[...] = hidden
    x = (hidden * norm_scale(hidden) * gain_two).astype(bf16)
    x_out[...] = x
    logits = dot(x, small).T[:experts]
    expert = lax.broadcasted_iota(jnp.int32, (experts, count), 0)
    named = expert < 0
    for k in range(routes_ref.shape[0]):
        named = named | (routes_ref[k:k + 1, :] == expert)
    top = jnp.max(jnp.where(named, logits, masked_value), axis=0, keepdims=True)
    weights = jnp.where(named, jnp.exp(jnp.where(named, logits - top, 0.0)), 0.0)
    gates_out[...] = weights / jnp.sum(weights, axis=0, keepdims=True)
    keep.wait()
    near.finish()
    own_cot.wait()
    if spread:
        far.finish()

def front(tokens, prefix, routes, mine, cot, cosine, sine, experts, kv_width, spread):
    count, width = tokens.shape
    shards, reps = lax.axis_size("shard"), lax.axis_size("rep")
    depth, total = tokens.shape[1] // shards, sum(part.shape[1] for part in mine)
    v = pl.BlockSpec(memory_space=pltpu.VMEM)
    any_ = pl.BlockSpec(memory_space=pl.ANY)
    sds = jax.ShapeDtypeStruct
    n = PlaneGather.copies(shards)
    return pl.pallas_call(
        functools.partial(front_kernel, spread),
        out_shape=[
            sds((shards, depth, total), bf16), sds((shards, count, width), bf16), sds((reps, count, width), bf16), sds((count, width), bf16), sds((count, kv_width), bf16), sds((count, kv_width), bf16),
            sds((count, width), bf16), sds((count, width), f32), sds((count, width), bf16), sds((experts, count), f32), sds((count, width), bf16),
        ],
        in_specs=[pl.BlockSpec(memory_space=pltpu.SMEM), v, v, v, v] + [any_] * 6,
        out_specs=[any_] * 3 + [v] * 8,
        scratch_shapes=[
            pltpu.VMEM((shards, depth, total), bf16), pltpu.VMEM((count, width + 2 * kv_width), f32),
            *[pltpu.SemaphoreType.DMA((k,)) for k in (n, n, n, n, reps, reps, 3, 5)],
        ],
        compiler_params=pltpu.CompilerParams(vmem_limit_bytes=60 << 20, has_side_effects=True, collective_id=1),
        name="front",
    )(prefix, tokens, routes, cosine, sine, *mine, cot)

def share_order(steps):
    groups = [[u for u in range(1 << steps) if u % (2 << k) == 1 << k] for k in range(steps)]
    return groups + [[0]]


class PlaneReduce:
    def __init__(self, mine, theirs, from_core, from_chip, csend, crecv, send, recv):
        self.mine, self.theirs, self.from_core, self.from_chip = mine, theirs, from_core, from_chip
        self.csend, self.crecv, self.send, self.recv = csend, crecv, send, recv
        self.rep, self.me = lax.axis_index("rep"), lax.axis_index("shard")
        self.core = self.me % 2
        self.bits = [1 << i for i in range(1, lax.axis_size("shard").bit_length() - 1)]
        self.steps = len(self.bits)

    def owner(self, core, u):
        at = flip(self.me, 1) if core else self.me
        of = (1 - self.core) if core else self.core
        for step in range(self.steps):
            if u >> step & 1:
                at = turned(at, of, step, self.bits)
        return at

    def core_copy(self, u):
        return pltpu.make_async_remote_copy(
            src_ref=self.theirs.at[u], dst_ref=self.from_core.at[u], send_sem=self.csend.at[u], recv_sem=self.crecv.at[u],
            device_id=(self.rep, flip(self.me, 1)), device_id_type=MESH,
        )

    def slot(self, step, u):
        return (1 << self.steps) - (1 << (self.steps - step)) + (u >> (step + 1))

    def chip_copy(self, step, u):
        slot = self.slot(step, u)
        return pltpu.make_async_remote_copy(
            src_ref=self.mine.at[u], dst_ref=self.from_chip.at[slot], send_sem=self.send.at[slot], recv_sem=self.recv.at[slot],
            device_id=(self.rep, turned(self.me, self.core, step, self.bits)), device_id_type=MESH,
        )

    def total(self, u, before, rows):
        whole = self.mine[u, rows].astype(f32) + self.from_core[u, rows].astype(f32)
        for step in range(before):
            whole = whole + self.from_chip[self.slot(step, u), rows].astype(f32)
        return whole

    def send_on(self, step, u):
        self.core_copy(u).wait_recv()
        count = self.mine.shape[1]
        piece = 32

        def add(i, carry):
            rows = pl.ds(pl.multiple_of(i * piece, piece), piece)
            self.mine[u, rows] = self.total(u, step, rows).astype(bf16)
            return carry
        lax.fori_loop(0, count // piece, add, 0)
        self.chip_copy(step, u).start()

    def arrive(self, step):
        for u in range(1 << self.steps):
            if u % (2 << step) == 1 << step:
                self.chip_copy(step, u).wait_recv()

    def last(self, out):
        self.core_copy(0).wait_recv()
        count = self.mine.shape[1]
        piece = 32

        def add(i, carry):
            rows = pl.ds(pl.multiple_of(i * piece, piece), piece)
            out[rows] = self.total(0, self.steps, rows)
            return carry
        lax.fori_loop(0, count // piece, add, 0)

    def finish(self):
        for u in range(1 << self.steps):
            self.core_copy(u).wait_send()
        for step in range(self.steps):
            for u in range(1 << self.steps):
                if u % (2 << step) == 1 << step:
                    self.chip_copy(step, u).wait_send()


def own_kernel(spread, nb, x_ref, gates_ref, c_hbm, wg_hbm, wu_hbm, wd_hbm,
               xown_out, xcol_out, gown_out, gcol_out, back_out, dg_out,
               wg, wu, wd, xb, cb, xg_ref, cg_ref, sg_ref, y_ref, ds_ref, mine, theirs, from_core, from_chip,
               gown, gcol, dgs, dgr,
               xs, xr, zxs, zxr, zgs, zgr, gs, gr, dss, dsr, css, csr, hs, hr, wsem, bsem, lsem):
    count, width = x_ref.shape
    local, _, hidden = wg.shape
    rep, me = lax.axis_index("rep"), lax.axis_index("shard")
    shards = lax.axis_size("shard")
    first = me * local
    greet(spread)
    near = PlaneGather(xown_out, x_ref, xs, xr)
    near.start()
    gown[me] = gates_ref[...]

    def peer(j):
        return (rep, (me + j) % shards)

    gate_sends = [
        pltpu.make_async_remote_copy(
            src_ref=gates_ref, dst_ref=gown.at[me], send_sem=gs.at[j - 1], recv_sem=gr.at[j - 1],
            device_id=peer(j), device_id_type=MESH,
        )
        for j in range(1, shards)
    ]
    for copy in gate_sends:
        copy.start()
    far = [RepSends(xcol_out, x_ref, zxs, zxr), RepSends(gcol, gates_ref, zgs, zgr)] if spread else []
    for sends in far:
        sends.start()
    own_x = pltpu.make_async_copy(x_ref, xown_out.at[me], lsem)
    own_x.start()
    weights = [pltpu.make_async_copy(a, b, wsem.at[i]) for i, (a, b) in enumerate(((wg_hbm, wg), (wu_hbm, wu), (wd_hbm, wd)))]
    for copy in weights:
        copy.start()
    reduce = PlaneReduce(mine, theirs, from_core, from_chip, css, csr, hs, hr)
    for copy in gate_sends:
        copy.wait_recv()
    for step in range(near.steps):
        near.forward(step)
    own_x.wait()
    for subset in range(1 << near.steps):
        near.core_copy(subset).wait_recv()
    for copy in weights:
        copy.wait()

    groups = share_order(reduce.steps)
    order = [u for group in groups for u in group]
    half = nb // 2
    dg_sends = []

    def fetch(at, slot):
        return (pltpu.make_async_copy(xown_out.at[at], xb.at[slot], bsem.at[0, slot]),
                pltpu.make_async_copy(c_hbm.at[at], cb.at[slot], bsem.at[1, slot]))

    plan = []
    for q in range(len(order) // half):
        for u in order[q * half:(q + 1) * half]:
            plan += [(1, u), (0, u)]
    owners = [reduce.owner(core, u) for core, u in plan]
    for copy in fetch(owners[0], 0):
        copy.start()
    for q in range(len(order) // half):
        for b in range(nb):
            n = q * nb + b
            if n + 1 < len(plan):
                for copy in fetch(owners[n + 1], (n + 1) % 2):
                    copy.start()
            for copy in fetch(owners[n], n % 2):
                copy.wait()
            gather_block(xb[n % 2], cb[n % 2], gown[owners[n]], first, local, xg_ref, cg_ref, sg_ref, b * CAP)

        def expert(l, carry):
            inner, raw, d_gate, d_up, scaled = expert_parts(xg_ref[l], cg_ref[l], sg_ref[l], wg[l], wu[l], wd[l])
            ds_ref[l] = branch_scale * jnp.sum(inner * raw, axis=1, keepdims=True)
            rows = pl.ds(pl.multiple_of(l * CAP, CAP), CAP)
            out = dot(scaled, wd[l]).astype(bf16)
            d_in = (dot(d_gate, wg[l], ((1,), (1,))) + dot(d_up, wu[l], ((1,), (1,)))).astype(bf16)
            for b in range(nb):
                y_ref[b, rows, :width] = out[b * CAP:(b + 1) * CAP]
                y_ref[b, rows, width:] = d_in[b * CAP:(b + 1) * CAP]
            return carry
        lax.fori_loop(0, local, expert, 0)
        for b in range(nb):
            core, u = plan[q * nb + b]
            at = owners[q * nb + b]
            parts = slot_one_hot(slot_ranks(gown[at]), first, local)
            table = jnp.concatenate(parts, axis=0).astype(bf16)
            (theirs if core else mine)[u] = dot(table, y_ref[b], ((0,), (0,))).astype(bf16)
            if core:
                reduce.core_copy(u).start()
            dgs[at] = jnp.concatenate(
                [jnp.sum(parts[l] * ds_ref[l, b * CAP:(b + 1) * CAP], axis=0, keepdims=True) for l in range(local)], axis=0
            )
        for step, group in enumerate(groups[:-1]):
            done = order[:(q + 1) * half]
            fresh = order[q * half:(q + 1) * half]
            if group[-1] in fresh:
                if step:
                    reduce.arrive(step - 1)
                for u in group:
                    reduce.send_on(step, u)
    for j in range(1, shards):
        copy = pltpu.make_async_remote_copy(
            src_ref=dgs.at[(me + j) % shards], dst_ref=dgr.at[me], send_sem=dss.at[j - 1], recv_sem=dsr.at[j - 1],
            device_id=peer(j), device_id_type=MESH,
        )
        copy.start()
        dg_sends.append(copy)
    dgr[me] = dgs[me]
    gown_out[...] = gown[...]
    reduce.arrive(reduce.steps - 1)
    reduce.last(back_out)
    for copy in dg_sends:
        copy.wait()
    dg_out[...] = dgr[...]
    reduce.finish()
    near.sent()
    for copy in gate_sends:
        copy.wait_send()
    for sends in far:
        sends.finish()
    if spread:
        gcol_out[...] = gcol[...]


def moe_own(x, gates, c, wg, wu, wd, spread, nb=4):
    count, width = x.shape
    local, _, hidden = wg.shape
    shards, reps = lax.axis_size("shard"), lax.axis_size("rep")
    experts = local * shards
    v = pl.BlockSpec(memory_space=pltpu.VMEM)
    any_ = pl.BlockSpec(memory_space=pl.ANY)
    sds = jax.ShapeDtypeStruct
    n = PlaneGather.copies(shards)
    rows = nb * CAP
    half = shards // 2
    dma = lambda *k: pltpu.SemaphoreType.DMA(k)
    return pl.pallas_call(
        functools.partial(own_kernel, spread, nb),
        out_shape=[
            sds((shards, count, width), bf16), sds((reps, count, width), bf16), sds((shards, experts, count), f32),
            sds((reps, experts, count), f32), sds((count, 2 * width), f32), sds((shards, local, count), f32),
        ],
        in_specs=[v, v, any_, any_, any_, any_],
        out_specs=[any_, any_, v, v, v, v],
        scratch_shapes=[
            pltpu.VMEM(wg.shape, bf16), pltpu.VMEM(wu.shape, bf16), pltpu.VMEM(wd.shape, bf16),
            pltpu.VMEM((2, count, width), bf16), pltpu.VMEM((2, count, width), bf16),
            pltpu.VMEM((local, rows, width), bf16), pltpu.VMEM((local, rows, width), bf16), pltpu.VMEM((local, rows, 1), f32),
            pltpu.VMEM((nb, local * CAP, 2 * width), bf16), pltpu.VMEM((local, rows, 1), f32),
            pltpu.VMEM((half, count, 2 * width), bf16), pltpu.VMEM((half, count, 2 * width), bf16),
            pltpu.VMEM((half, count, 2 * width), bf16), pltpu.VMEM((half - 1, count, 2 * width), bf16),
            pltpu.VMEM((shards, experts, count), f32), pltpu.VMEM((reps, experts, count), f32),
            pltpu.VMEM((shards, local, count), f32), pltpu.VMEM((shards, local, count), f32),
            dma(n), dma(n), dma(reps), dma(reps), dma(reps), dma(reps), dma(shards), dma(shards), dma(shards), dma(shards),
            dma(half), dma(half), dma(half), dma(half), dma(3), dma(2, 2), pltpu.SemaphoreType.DMA,
        ],
        compiler_params=pltpu.CompilerParams(vmem_limit_bytes=60 << 20, has_side_effects=True, collective_id=2),
        name="own_experts",
    )(x, gates, c, wg, wu, wd)

def norm_backward(rows, scaling, gain, upstream):
    weighted = upstream * gain
    inner_mean = jnp.mean(weighted * rows, axis=-1, keepdims=True)
    gradient = scaling * weighted - rows * (scaling * scaling * scaling) * inner_mean
    return gradient, jnp.sum(upstream * rows * scaling, axis=0, keepdims=True)


def back_kernel(prefix_ref, tok_ref, cot_ref, cos_ref, sin_ref, w_ref, q_ref, k_ref, v_ref, att_ref, n1_ref, x_ref,
                hid_ref, gates_ref, dg_ref, back_ref, res_out, dtok_out, shares_out, dqkv_ref, datt_ref, dproj_ref):
    count, width = tok_ref.shape
    kv_width = k_ref.shape[1]
    experts = gates_ref.shape[0]
    shards, depth, total = w_ref.shape
    rows = shards * depth
    cut = [0, width, width + kv_width, width + 2 * kv_width, 2 * width + 2 * kv_width]
    small = w_ref[:, :, cut[4]:].reshape(rows, total - cut[4])
    wide = small.astype(f32).T
    gain_one, gain_two = wide[experts:experts + 1], wide[experts + 1:experts + 2]
    hidden = hid_ref[...]
    res_out[...] = (hidden + back_ref[:, :width]).astype(bf16)
    gates, d_gates = gates_ref[...], dg_ref[...]
    d_logits = gates * (d_gates - jnp.sum(gates * d_gates, axis=0, keepdims=True))
    none = jnp.zeros((LANES - experts, count), f32)
    d_logits = jnp.concatenate([d_logits, none], axis=0).T.astype(bf16)
    d_normed_two = back_ref[:, width:] + dot(d_logits, small, ((1,), (1,)))
    d_hidden, d_gain_two = norm_backward(hidden, norm_scale(hidden), gain_two, d_normed_two)
    d_hidden = d_hidden + cot_ref[...].astype(f32)
    dtok_out[...] = d_hidden
    dproj_ref[...] = (branch_scale * d_hidden).astype(bf16)
    tile = 2 * LANES

    def out_tile(j, carry):
        grad = dot(att_ref[...], dproj_ref[:, lanes(j, 2)], ((0,), (0,))).astype(bf16)
        at = pl.ds(pl.multiple_of(cut[3] + j * tile, LANES), tile)
        shares_out[:, :, at] = grad.reshape(shards, depth, tile)
        return carry
    lax.fori_loop(0, width // tile, out_tile, 0)
    datt_ref[...] = dot(dproj_ref[...], w_ref[:, :, cut[3]:cut[4]].reshape(rows, width), ((1,), (1,))).astype(bf16)
    cosine, sine = cos_ref[...], sin_ref[...]
    prefix_len = prefix_ref[0]
    low = lax.broadcasted_iota(jnp.int32, (count, LANES), 1) < HEAD_SIZE

    def pair(p, carry):
        at_k = pl.ds(pl.multiple_of(cut[1] + p * LANES, LANES), LANES)
        at_v = pl.ds(pl.multiple_of(cut[2] + p * LANES, LANES), LANES)
        d_keys, d_values = [], []
        for odd in range(2):
            j = 2 * p + odd
            keys = one_head_twice(k_ref[:, lanes(p)], odd)
            values = one_head_twice(v_ref[:, lanes(p)], odd)
            query2, d_att2 = two_heads(q_ref[:, lanes(j)]), two_heads(datt_ref[:, lanes(j)])
            prob = probabilities(query2, keys, prefix_len)
            d_value = dot(prob.astype(bf16), d_att2, ((0,), (0,)))
            d_prob = dot(d_att2, values, ((1,), (1,)))
            weighted = jnp.sum(prob * d_prob, axis=-1, keepdims=True)
            d_score = (prob * (d_prob - weighted) * score_scale).astype(bf16)
            d_query = dot(d_score, keys)
            d_query = jnp.where(low, d_query[:count], d_query[count:])
            dqkv_ref[:, lanes(j)] = rotate(d_query, cosine, sine, -1.0).astype(bf16)
            d_key = dot(d_score, query2, ((0,), (0,)))
            d_keys.append(d_key + pltpu.roll(d_key, HEAD_SIZE, 1))
            d_values.append(d_value + pltpu.roll(d_value, HEAD_SIZE, 1))
        dqkv_ref[:, at_k] = rotate(jnp.where(low, *d_keys), cosine, sine, -1.0).astype(bf16)
        dqkv_ref[:, at_v] = jnp.where(low, *d_values).astype(bf16)
        return carry
    lax.fori_loop(0, KEY_VALUE_HEADS // 2, pair, 0)

    def in_tile(j, carry):
        grad = dot(n1_ref[...], dqkv_ref[:, lanes(j, 2)], ((0,), (0,))).astype(bf16)
        shares_out[:, :, lanes(j, 2)] = grad.reshape(shards, depth, tile)
        return carry
    lax.fori_loop(0, cut[3] // tile, in_tile, 0)
    d_normed_one = dot(dqkv_ref[...], w_ref[:, :, :cut[3]].reshape(rows, cut[3]), ((1,), (1,)))
    inputs = tok_ref[...].astype(f32)
    d_inputs, d_gain_one = norm_backward(inputs, norm_scale(inputs), gain_one, d_normed_one)
    dtok_out[...] += d_inputs
    row = lax.broadcasted_iota(jnp.int32, (LANES, rows), 0)
    gains = jnp.where(row == experts, d_gain_one, jnp.where(row == experts + 1, d_gain_two, 0.0)).T
    d_small = (dot(x_ref[...], d_logits, ((0,), (0,))) + gains).astype(bf16)
    shares_out[:, :, cut[4]:] = d_small.reshape(shards, depth, total - cut[4])


def attention_back(prefix, tokens, cot, cosine, sine, packed, query, keys, values, attended, n1, x, hidden, gates, d_gates, back):
    count, width = tokens.shape
    v = pl.BlockSpec(memory_space=pltpu.VMEM)
    sds = jax.ShapeDtypeStruct
    return pl.pallas_call(
        back_kernel,
        out_shape=[sds((count, width), bf16), sds((count, width), f32), sds(packed.shape, bf16)],
        in_specs=[pl.BlockSpec(memory_space=pltpu.SMEM)] + [v] * 15,
        out_specs=[v] * 3,
        scratch_shapes=[
            pltpu.VMEM((count, width + 2 * keys.shape[1]), bf16), pltpu.VMEM((count, width), bf16), pltpu.VMEM((count, width), bf16),
        ],
        compiler_params=pltpu.CompilerParams(vmem_limit_bytes=60 << 20),
        name="attention_back",
    )(prefix, tokens, cot, cosine, sine, packed, query, keys, values, attended, n1, x, hidden, gates, d_gates, back)

def spread_kernel(nb, xown_hbm, cown_hbm, xcol_hbm, ccol_hbm, gown_ref, gcol_ref, wg_hbm, wu_hbm, wd_hbm,
                  xoth_hbm, coth_hbm, og_hbm, ou_hbm, od_hbm, glast_ref,
                  xbuf, cbuf, wg, wu, wd, ag, au, ad, xg_ref, cg_ref, sg_ref, goth, send, recv, bsem, wsem, lsem):
    local = wg.shape[0]
    shards = gown_ref.shape[0]
    rep, me = lax.axis_index("rep"), lax.axis_index("shard")
    reps = lax.axis_size("rep")
    first = me * local
    chunks = shards // nb

    def gathers(j):
        other = (rep + j) % reps
        return [
            PlaneGather(buf.at[j - 1], own.at[other], send.at[j - 1, i], recv.at[j - 1, i])
            for i, (buf, own) in enumerate(((xoth_hbm, xcol_hbm), (coth_hbm, ccol_hbm), (goth, gcol_ref)))
        ]

    def own_copies(j):
        other = (rep + j) % reps
        return (pltpu.make_async_copy(xcol_hbm.at[other], xoth_hbm.at[j - 1, me], lsem.at[0]),
                pltpu.make_async_copy(ccol_hbm.at[other], coth_hbm.at[j - 1, me], lsem.at[1]))

    def begin(j):
        for gather in gathers(j):
            gather.start()
        for copy in own_copies(j):
            copy.start()
        goth[j - 1, me] = gcol_ref[(rep + j) % reps]

    def forward(j):
        for gather in gathers(j):
            gather.forward(0)

    def end(j):
        for gather in gathers(j):
            for step in range(1, gather.steps):
                gather.forward(step)
        for gather in gathers(j):
            gather.finish()
        for copy in own_copies(j):
            copy.wait()

    def fetch(x, c, q, slot):
        return (pltpu.make_async_copy(x.at[pl.ds(q * nb, nb)], xbuf.at[slot], bsem.at[0, slot]),
                pltpu.make_async_copy(c.at[pl.ds(q * nb, nb)], cbuf.at[slot], bsem.at[1, slot]))

    def replica(x, c, g, midway, last):
        for copy in fetch(x, c, 0, 0):
            copy.start()

        def chunk(q, carry):
            slot = lax.rem(q, 2)

            @pl.when(q + 1 < chunks)
            def _():
                for copy in fetch(x, c, q + 1, 1 - slot):
                    copy.start()
            for copy in fetch(x, c, q, slot):
                copy.wait()

            def block(b, carry):
                gather_block(xbuf[slot, b], cbuf[slot, b], g[q * nb + b], first, local, xg_ref, cg_ref, sg_ref,
                             pl.multiple_of(b * CAP, CAP))
                return carry
            lax.fori_loop(0, nb, block, 0)

            def expert(l, carry):
                add_expert(l, xg_ref, cg_ref, sg_ref, wg, wu, wd, ag, au, ad)

                @pl.when((q == chunks // 2) & (l == 0))
                def _():
                    midway()
                return carry
            lax.fori_loop(0, local, expert, 0)
            return carry
        lax.fori_loop(0, chunks, chunk, 0)
        last()

    greet(False)
    begin(1)
    weights = [pltpu.make_async_copy(a, b, wsem.at[i]) for i, (a, b) in enumerate(((wg_hbm, wg), (wu_hbm, wu), (wd_hbm, wd)))]
    for copy in weights:
        copy.start()
    ag[...] = jnp.zeros_like(ag)
    au[...] = jnp.zeros_like(au)
    ad[...] = jnp.zeros_like(ad)
    for copy in weights:
        copy.wait()

    def midway(j):
        def run():
            @pl.when(j + 1 < reps)
            def _():
                forward(j + 1)
        return run

    def last(j):
        def run():
            @pl.when(j + 1 < reps)
            def _():
                end(j + 1)

            @pl.when(j + 2 < reps)
            def _():
                begin(j + 2)
        return run

    replica(xown_hbm, cown_hbm, gown_ref, midway(0), last(0))

    def others(j, carry):
        replica(xoth_hbm.at[j - 1], coth_hbm.at[j - 1], goth.at[j - 1], midway(j), last(j))
        return carry
    lax.fori_loop(1, reps - 1, others, 0)
    glast_ref[...] = goth[reps - 2]
    outs = [pltpu.make_async_copy(a, b, wsem.at[i]) for i, (a, b) in enumerate(((ag, og_hbm), (au, ou_hbm), (ad, od_hbm)))]
    for copy in outs:
        copy.start()
    for copy in outs:
        copy.wait()


def moe_spread_sums(xown, cown, xcol, ccol, gown, gcol, wg, wu, wd, nb=4):
    shards, count, width = xown.shape
    reps = xcol.shape[0]
    local, _, hidden = wg.shape
    any_ = pl.BlockSpec(memory_space=pl.ANY)
    v = pl.BlockSpec(memory_space=pltpu.VMEM)
    rows = nb * CAP
    n = PlaneGather.copies(shards)
    slots = reps * shards * local * CAP
    outs = pl.pallas_call(
        functools.partial(spread_kernel, nb),
        out_shape=[jax.ShapeDtypeStruct((reps - 1, shards, count, width), bf16)] * 2
        + [jax.ShapeDtypeStruct(w.shape, f32) for w in (wg, wu, wd)] + [jax.ShapeDtypeStruct(gown.shape, f32)],
        in_specs=[any_, any_, any_, any_, v, v, any_, any_, any_],
        out_specs=[any_] * 5 + [v],
        scratch_shapes=[
            pltpu.VMEM((2, nb, count, width), bf16), pltpu.VMEM((2, nb, count, width), bf16),
            pltpu.VMEM(wg.shape, bf16), pltpu.VMEM(wu.shape, bf16), pltpu.VMEM(wd.shape, bf16),
            pltpu.VMEM(wg.shape, f32), pltpu.VMEM(wu.shape, f32), pltpu.VMEM(wd.shape, f32),
            pltpu.VMEM((local, rows, width), bf16), pltpu.VMEM((local, rows, width), bf16), pltpu.VMEM((local, rows, 1), f32),
            pltpu.VMEM((reps - 1, shards, *gown.shape[1:]), f32),
            pltpu.SemaphoreType.DMA((reps - 1, 3, n)), pltpu.SemaphoreType.DMA((reps - 1, 3, n)),
            pltpu.SemaphoreType.DMA((2, 2)), pltpu.SemaphoreType.DMA((3,)), pltpu.SemaphoreType.DMA((2,)),
        ],
        compiler_params=pltpu.CompilerParams(vmem_limit_bytes=60 << 20, has_side_effects=True, collective_id=3),
        cost_estimate=pl.CostEstimate(
            flops=12 * slots * width * hidden, transcendentals=slots * hidden, bytes_accessed=4 * reps * shards * count * width
        ),
        name="spread_expert_sums",
    )(xown, cown, xcol, ccol, gown, gcol, wg, wu, wd)
    return outs[0], outs[1], outs[5], outs[2:5]

def rotary_tables(count):
    half = HEAD_SIZE // 2
    inverse = np.exp(np.arange(half) * (-2.0 * math.log(10000.0) / HEAD_SIZE))
    angles = np.tile(np.arange(count)[:, None] * inverse[None, :], (1, LANES // half))
    return np.cos(angles).astype(np.float32), np.sin(angles).astype(np.float32)


def pack_small(w_router, norm_attn, norm_moe):
    small = jnp.concatenate([w_router, norm_attn[:, None], norm_moe[:, None]], axis=1)
    return jnp.pad(small, ((0, 0), (0, LANES - small.shape[1])))


def body(
    tokens, prefix, routes, cotangent, w_query, key_weight, value_weight, w_out,
    norm_attn, norm_moe, w_router, w_gate, w_up, w_down,
):
    count, width = tokens.shape
    local = w_gate.shape[0]
    shards, reps = lax.axis_size("shard"), lax.axis_size("rep")
    experts = local * shards
    kv_width = key_weight.shape[1]
    spread = reps <= MOST_GATHERED
    cosine, sine = rotary_tables(count)
    mine = (w_query, key_weight, value_weight, w_out, pack_small(w_router, norm_attn, norm_moe))
    packed, cot_own, cot_col, query, keys, values, attended, hidden_one, normed_two, gates, normed_one = front(
        tokens, prefix, routes.T, mine, cotangent, cosine, sine, experts, kv_width, spread
    )
    x_own, x_col, gates_own, gates_col, back, d_gates = moe_own(
        normed_two, gates, cot_own, w_gate, w_up, w_down, spread
    )
    result, d_tokens, shares = attention_back(
        prefix, tokens, cotangent, cosine, sine, packed, query, keys, values, attended, normed_one, normed_two, hidden_one,
        gates, d_gates.reshape(experts, count), back,
    )
    shares = shares.reshape(width, -1)
    if spread:
        x_own, shares = lax.optimization_barrier((x_own, shares))
        x_oth, cot_oth, gates_oth, sums = moe_spread_sums(
            x_own, cot_own, x_col, cot_col, gates_own, gates_col, w_gate, w_up, w_down
        )
        shares = lax.psum_scatter(shares, "shard", scatter_dimension=0, tiled=True)
        shares, gates_oth = lax.optimization_barrier((shares, gates_oth))
        sums = moe_sums(x_oth, cot_oth, gates_oth, w_gate, w_up, w_down, sums)
    else:
        sums = moe_sums(x_own, cot_own, gates_own, w_gate, w_up, w_down)
        sums = [lax.psum(a.astype(bf16), "rep").astype(f32) for a in sums]
        shares = lax.psum_scatter(shares, "shard", scatter_dimension=0, tiled=True)
    d_w_gate, d_w_up, d_w_down = sums
    totals = lax.psum(shares, "rep").astype(f32)
    cuts = [width, width + kv_width, width + 2 * kv_width, 2 * width + 2 * kv_width]
    d_wq, d_wk, d_wv, d_wo, small = jnp.split(totals, cuts, axis=1)
    return (
        result, d_tokens, d_wq, d_wk, d_wv, d_wo, small[:, experts], small[:, experts + 1],
        small[:, :experts], d_w_gate, d_w_up, d_w_down,
    )


def solution(mesh):
    rows = P(("rep", "shard"), None)
    one, two, three = P("shard"), P("shard", None), P("shard", None, None)
    return jax.shard_map(
        body,
        mesh=mesh,
        in_specs=(rows, P(("rep", "shard")), rows, rows, two, two, two, two, one, one, two, three, three, three),
        out_specs=(rows, rows, two, two, two, two, one, one, two, three, three, three),
        check_vma=False,
    )
```

```python
import functools
import math

import jax
import jax.numpy as jnp
import numpy as np
from jax import lax
from jax.experimental import pallas as pl
from jax.experimental.pallas import tpu as pltpu
from jax.sharding import PartitionSpec as P

QUERY_HEADS = 16
KEY_VALUE_HEADS = 8
HEAD_SIZE = 64
CAP = 96
LANES = 128
GATHERED_REPLICAS = 4

epsilon = 1e-06
score_scale = 0.015625
branch_scale = 0.22
masked_value = -1e30

f32 = jnp.float32
bf16 = jnp.bfloat16
MESH = pl.DeviceIdType.MESH


def dot(left, right, contract=((1,), (0,))):
    return lax.dot_general(left, right, (contract, ((), ())), preferred_element_type=f32)

def slot_ranks(gates):
    tokens = gates.shape[1]
    named = gates > 0
    before = lax.broadcasted_iota(jnp.int32, (tokens, tokens), 0) < lax.broadcasted_iota(jnp.int32, (tokens, tokens), 1)
    rank = dot(named.astype(f32).astype(bf16), before.astype(f32).astype(bf16))
    return jnp.where(named, rank, -1.0)

def pick_row(table, row):
    here = lax.broadcasted_iota(jnp.int32, table.shape, 0) == row
    return jnp.sum(jnp.where(here, table, 0.0), axis=0, keepdims=True)

def slot_one_hot(ranks, first, local):
    tokens = ranks.shape[1]
    slot = lax.broadcasted_iota(jnp.int32, (CAP, tokens), 0).astype(f32)
    return [jnp.where(pick_row(ranks, first + l) == slot, 1.0, 0.0) for l in range(local)]

def gather_block(x, c, gates, first, local, xg_ref, cg_ref, sg_ref, at):
    ranks = slot_ranks(gates)
    parts = slot_one_hot(ranks, first, local)
    table = jnp.concatenate(parts, axis=0).astype(bf16)
    xg = dot(table, x).astype(bf16)
    cg = dot(table, c).astype(bf16)
    for l in range(local):
        rows = slice(l * CAP, (l + 1) * CAP)
        xg_ref[l, pl.ds(at, CAP), :] = xg[rows]
        cg_ref[l, pl.ds(at, CAP), :] = cg[rows]
        gate = jnp.sum(parts[l] * pick_row(gates, first + l), axis=1, keepdims=True)
        sg_ref[l, pl.ds(at, CAP), :] = branch_scale * gate
    return parts

def expert_parts(xg, cg, scale, wg, wu, wd):
    gate_part = dot(xg, wg)
    up_part = dot(xg, wu)
    raw = dot(cg, wd, ((1,), (1,)))
    sigma = 1.0 / (1.0 + jnp.exp(-gate_part))
    act = gate_part * sigma
    inner = act * up_part
    d_inner = raw * scale
    d_gate = (d_inner * up_part * (sigma + act * (1.0 - sigma))).astype(bf16)
    d_up = (d_inner * act).astype(bf16)
    scaled = (inner * scale).astype(bf16)
    return inner, raw, d_gate, d_up, scaled

def add_expert(l, xg_ref, cg_ref, sg_ref, wg, wu, wd, ag, au, ad):
    xg, cg = xg_ref[l], cg_ref[l]
    _, _, d_gate, d_up, scaled = expert_parts(xg, cg, sg_ref[l], wg[l], wu[l], wd[l])
    ag[l] += dot(xg, d_gate, ((0,), (0,)))
    au[l] += dot(xg, d_up, ((0,), (0,)))
    ad[l] += dot(scaled, cg, ((0,), (0,)))

def late_places(rep, reps):
    later = (rep + reps - 1) // reps
    return later * (reps - 2), (1 - later) * (reps - 2)

def sums_kernel(nb, more, x_hbm, c_hbm, g_ref, wg_hbm, wu_hbm, wd_hbm, *rest):
    if len(x_hbm.shape) == 4:
        _, left = late_places(lax.axis_index("rep"), lax.axis_size("rep"))
        x_hbm, c_hbm = x_hbm.at[left], c_hbm.at[left]
    starts, (og_hbm, ou_hbm, od_hbm, *scratch) = rest[:3 * more], rest[3 * more:]
    sums_body(nb, starts, x_hbm, c_hbm, g_ref, wg_hbm, wu_hbm, wd_hbm, og_hbm, ou_hbm, od_hbm, *scratch)

def sums_body(nb, starts, x_hbm, c_hbm, g_ref, wg_hbm, wu_hbm, wd_hbm, og_hbm, ou_hbm, od_hbm,
                xbuf, cbuf, wg, wu, wd, ag, au, ad, xg_ref, cg_ref, sg_ref, sem, wsem, asem):
    local = wg.shape[0]
    blocks = x_hbm.shape[0]
    chunks = blocks // nb
    first = lax.axis_index("shard") * local
    def fetch(i, slot):
        return (pltpu.make_async_copy(x_hbm.at[pl.ds(i * nb, nb)], xbuf.at[slot], sem.at[0, slot]),
                pltpu.make_async_copy(c_hbm.at[pl.ds(i * nb, nb)], cbuf.at[slot], sem.at[1, slot]))
    for cp in fetch(0, 0):
        cp.start()
    weights = [pltpu.make_async_copy(a, b, wsem.at[i]) for i, (a, b) in enumerate(((wg_hbm, wg), (wu_hbm, wu), (wd_hbm, wd)))]
    for cp in weights:
        cp.start()
    loads = [
        pltpu.make_async_copy(a.at[l], b.at[l], asem.at[i, l])
        for l in range(local) for i, (a, b) in enumerate(zip(starts, (ag, au, ad)))
    ]
    for cp in loads:
        cp.start()
    if not starts:
        ag[...] = jnp.zeros_like(ag)
        au[...] = jnp.zeros_like(au)
        ad[...] = jnp.zeros_like(ad)
    for cp in weights:
        cp.wait()

    def chunk(i, carry):
        slot = lax.rem(i, 2)
        @pl.when(i + 1 < chunks)
        def _():
            for cp in fetch(i + 1, 1 - slot):
                cp.start()
        for cp in fetch(i, slot):
            cp.wait()
        def block(b, carry):
            gather_block(xbuf[slot, b], cbuf[slot, b], g_ref[i * nb + b], first, local, xg_ref, cg_ref, sg_ref,
                         pl.multiple_of(b * CAP, CAP))
            return carry
        lax.fori_loop(0, nb, block, 0)
        def expert(l, carry):
            if starts:
                @pl.when(i == 0)
                def _():
                    for k, (a, b) in enumerate(zip(starts, (ag, au, ad))):
                        pltpu.make_async_copy(a.at[l], b.at[l], asem.at[k, l]).wait()
            add_expert(l, xg_ref, cg_ref, sg_ref, wg, wu, wd, ag, au, ad)

            @pl.when(i == chunks - 1)
            def _():
                for k, (a, b) in enumerate(((ag, og_hbm), (au, ou_hbm), (ad, od_hbm))):
                    pltpu.make_async_copy(a.at[l], b.at[l], asem.at[k, l]).start()
            return carry
        lax.fori_loop(0, local, expert, 0)
        return carry
    lax.fori_loop(0, chunks, chunk, 0)
    for l in range(local):
        for k, (a, b) in enumerate(((ag, og_hbm), (au, ou_hbm), (ad, od_hbm))):
            pltpu.make_async_copy(a.at[l], b.at[l], asem.at[k, l]).wait()

def moe_sums(x, c, gates, wg, wu, wd, starts=(), nb=4):
    blocks, tokens, width = x.shape[-3:]
    local, _, hidden = wg.shape
    any_ = pl.BlockSpec(memory_space=pl.ANY)
    rows = nb * CAP
    return pl.pallas_call(
        functools.partial(sums_kernel, nb, bool(starts)),
        out_shape=[jax.ShapeDtypeStruct(w.shape, f32) for w in (wg, wu, wd)],
        in_specs=[any_, any_, pl.BlockSpec(memory_space=pltpu.VMEM), any_, any_, any_] + [any_] * len(starts),
        out_specs=[any_] * 3,
        scratch_shapes=[
            pltpu.VMEM((2, nb, tokens, width), bf16), pltpu.VMEM((2, nb, tokens, width), bf16),
            pltpu.VMEM(wg.shape, bf16), pltpu.VMEM(wu.shape, bf16), pltpu.VMEM(wd.shape, bf16),
            pltpu.VMEM(wg.shape, f32), pltpu.VMEM(wu.shape, f32), pltpu.VMEM(wd.shape, f32),
            pltpu.VMEM((local, rows, width), bf16), pltpu.VMEM((local, rows, width), bf16), pltpu.VMEM((local, rows, 1), f32),
            pltpu.SemaphoreType.DMA((2, 2)), pltpu.SemaphoreType.DMA((3,)), pltpu.SemaphoreType.DMA((3, local)),
        ],
        compiler_params=pltpu.CompilerParams(vmem_limit_bytes=60 << 20),
        cost_estimate=pl.CostEstimate(
            flops=12 * blocks * local * CAP * width * hidden, transcendentals=blocks * local * CAP * hidden,
            bytes_accessed=4 * blocks * tokens * width + 24 * wg.size,
        ),
        name="expert_sums",
    )(x, c, gates, wg, wu, wd, *starts)


def norm_scale(rows):
    return lax.rsqrt(jnp.mean(rows * rows, axis=-1, keepdims=True) + epsilon)

def flip(index, bit):
    return index + bit - 2 * bit * ((index // bit) % 2)

def turned(index, core, step, bits):
    return (1 - core) * flip(index, bits[step]) + core * flip(index, bits[-1 - step])

def greet(spread):
    rep, me = lax.axis_index("rep"), lax.axis_index("shard")
    shards, reps = lax.axis_size("shard"), lax.axis_size("rep")
    peers = [(rep, (me + j) % shards) for j in range(1, shards)]
    if spread:
        peers += [((rep + j) % reps, me) for j in range(1, reps)]
    barrier = pltpu.get_barrier_semaphore()
    for peer in peers:
        pl.semaphore_signal(barrier, inc=1, device_id=peer, device_id_type=MESH)
    pl.semaphore_wait(barrier, len(peers))


class PlaneGather:
    def __init__(self, buf, own, send, recv, base=0):
        self.buf, self.own, self.send, self.recv, self.base = buf, own, send, recv, base
        self.rep, self.me = lax.axis_index("rep"), lax.axis_index("shard")
        self.core = self.me % 2
        shards = lax.axis_size("shard")
        self.bits = [1 << i for i in range(1, shards.bit_length() - 1)]
        self.steps = len(self.bits)

    @staticmethod
    def copies(shards):
        return (shards // 2 - 1) + shards // 2

    def owner(self, of, subset):
        for step in range(self.steps):
            if subset >> step & 1:
                of = turned(of, self.core, step, self.bits)
        return of

    def copy(self, number, subset, target):
        owner = self.owner(self.me, subset)
        return pltpu.make_async_remote_copy(
            src_ref=self.buf.at[owner] if subset else self.own, dst_ref=self.buf.at[owner],
            send_sem=self.send.at[self.base + number], recv_sem=self.recv.at[self.base + number],
            device_id=(self.rep, target), device_id_type=MESH,
        )

    def chip_copy(self, step, subset):
        return self.copy((1 << step) - 1 + subset, subset, turned(self.me, self.core, step, self.bits))

    def core_copy(self, subset):
        return self.copy((1 << self.steps) - 1 + subset, subset, flip(self.me, 1))

    def start(self):
        for step in range(self.steps):
            self.chip_copy(step, 0).start()
        self.core_copy(0).start()

    def forward(self, step):
        for subset in range(1 << step):
            self.chip_copy(step, subset).wait_recv()
            whole = subset + (1 << step)
            for later in range(step + 1, self.steps):
                self.chip_copy(later, whole).start()
            self.core_copy(whole).start()

    def finish(self):
        for subset in range(1 << self.steps):
            self.core_copy(subset).wait_recv()
        self.sent()

    def sent(self):
        for step in range(self.steps):
            for subset in range(1 << step):
                self.chip_copy(step, subset).wait_send()
        for subset in range(1 << self.steps):
            self.core_copy(subset).wait_send()

class RepSends:
    def __init__(self, buf, own, send, recv, neighbours):
        rep, me, reps = lax.axis_index("rep"), lax.axis_index("shard"), lax.axis_size("rep")
        self.rep, self.reps, self.neighbours = rep, reps, neighbours
        self.copies = [
            pltpu.make_async_remote_copy(
                src_ref=own, dst_ref=buf.at[rep], send_sem=send.at[j - 1], recv_sem=recv.at[j - 1],
                device_id=((rep + j) % reps, me), device_id_type=MESH,
            )
            for j in range(1, reps)
        ]

    def each(self, sent, act):
        for j, copy in enumerate(self.copies, 1):
            if self.neighbours or j not in (1, self.reps - 1):
                act(copy)
            else:
                end = self.reps - 1 if (j == 1) == sent else 0

                @pl.when(self.rep == end)
                def _(copy=copy):
                    act(copy)

    def start(self):
        self.each(True, lambda copy: copy.start())

    def finish(self):
        self.each(True, lambda copy: copy.wait_send())
        self.each(False, lambda copy: copy.wait_recv())


def on_ends(low, high):
    pl.when(lax.axis_index("rep") == 0)(low)
    pl.when(lax.axis_index("rep") == lax.axis_size("rep") - 1)(high)


class Spread:
    def __init__(self, oth, col, own, send, recv, psend, precv, asend, arecv, lsem):
        self.oth, self.col, self.own, self.send, self.recv = oth, col, own, send, recv
        self.psend, self.precv, self.asend, self.arecv, self.lsem = psend, precv, asend, arecv, lsem
        self.rep, self.me, self.reps = lax.axis_index("rep"), lax.axis_index("shard"), lax.axis_size("rep")
        self.core = self.me % 2
        self.blocks = range(lax.axis_size("shard") // 2)

    @staticmethod
    def semaphores(shards, reps):
        n = PlaneGather.copies(shards)
        dma = lambda *k: pltpu.SemaphoreType.DMA(k)
        return [dma(reps - 1, n), dma(reps - 1, n), *[dma(2, shards // 2)] * 4, dma(reps - 1)]

    def gather(self, j):
        return PlaneGather(self.oth.at[j - 1], self.col.at[(self.rep + j) % self.reps], self.send.at[j - 1], self.recv.at[j - 1])

    def own_copy(self, j):
        return pltpu.make_async_copy(self.col.at[(self.rep + j) % self.reps], self.oth.at[j - 1, self.me], self.lsem.at[j - 1])

    def begin(self, j):
        self.gather(j).start()
        self.own_copy(j).start()

    def forward(self, j):
        self.gather(j).forward(0)

    def end(self, j):
        gather = self.gather(j)
        for step in range(1, gather.steps):
            gather.forward(step)
        gather.finish()
        self.own_copy(j).wait()

    def straight(self, up, b):
        at, way = 2 * b + self.core, self.reps - 2 if up else 0
        return pltpu.make_async_remote_copy(
            src_ref=self.own.at[at], dst_ref=self.oth.at[way, at], send_sem=self.psend.at[up, b], recv_sem=self.precv.at[up, b],
            device_id=((self.rep + (1 if up else self.reps - 1)) % self.reps, self.me), device_id_type=MESH,
        )

    def across(self, up, b):
        at, way = 2 * b + self.core, self.reps - 2 if up else 0
        return pltpu.make_async_remote_copy(
            src_ref=self.oth.at[way, at], dst_ref=self.oth.at[way, at], send_sem=self.asend.at[up, b], recv_sem=self.arecv.at[up, b],
            device_id=(self.rep, flip(self.me, 1)), device_id_type=MESH,
        )

    def sends(self, up):
        return self.rep < self.reps - 1 if up else self.rep > 0

    def gets(self, up):
        return self.rep > 0 if up else self.rep < self.reps - 1

    def start_straight(self):
        for up in (0, 1):
            @pl.when(self.sends(up))
            def _(up=up):
                for b in self.blocks:
                    self.straight(up, b).start()

    def sent_straight(self):
        for up in (0, 1):
            @pl.when(self.sends(up))
            def _(up=up):
                for b in self.blocks:
                    self.straight(up, b).wait_send()

    def got_straight(self, up):
        @pl.when(self.gets(up))
        def _():
            for b in self.blocks:
                self.straight(up, b).wait_recv()

    def start_across(self, up):
        @pl.when(self.gets(up))
        def _():
            for b in self.blocks:
                self.across(up, b).start()

    def end_across(self, up):
        @pl.when(self.gets(up))
        def _():
            for b in self.blocks:
                self.across(up, b).wait()


def rotate(v, cosine, sine, sign):
    lane = lax.broadcasted_iota(jnp.int32, v.shape, 1) % HEAD_SIZE
    half = HEAD_SIZE // 2
    low = lane < half
    other = jnp.where(low, -pltpu.roll(v, LANES - half, 1), pltpu.roll(v, half, 1))
    return v * cosine + sign * other * sine

def two_heads(v):
    low = lax.broadcasted_iota(jnp.int32, v.shape, 1) < HEAD_SIZE
    zero = jnp.zeros_like(v)
    return jnp.concatenate([jnp.where(low, v, zero), jnp.where(low, zero, v)], axis=0)

def one_head_twice(pair, odd):
    high = lax.broadcasted_iota(jnp.int32, pair.shape, 1) // HEAD_SIZE
    wide = pair.astype(f32)
    return jnp.where(high == odd, wide, pltpu.roll(wide, HEAD_SIZE, 1)).astype(pair.dtype)

def probabilities(query2, keys, prefix_len):
    rows = query2.shape[0] // 2
    raw = dot(query2, keys, ((1,), (1,)))
    row = lax.broadcasted_iota(jnp.int32, raw.shape, 0) % rows
    col = lax.broadcasted_iota(jnp.int32, raw.shape, 1)
    scores = jnp.where((col <= row) | (col < prefix_len), raw * score_scale, masked_value)
    weights = jnp.exp(scores - jnp.max(scores, axis=-1, keepdims=True))
    return weights / jnp.sum(weights, axis=-1, keepdims=True)

def lanes(j, count=1):
    return pl.ds(pl.multiple_of(j * LANES * count, LANES), LANES * count)

def front_kernel(spread, prefix_ref, tok_ref, routes_ref, cos_ref, sin_ref, wq_hbm, wk_hbm, wv_hbm, wo_hbm, ws_hbm, cot_ref,
                 wall_out, cown_out, ccol_out, q_out, k_out, v_out, att_out, hid_out, x_out, gates_out, n1_out,
                 wbuf, qkv_ref, send, recv, csend, crecv, zsend, zrecv, lsem, osem):
    count, width = tok_ref.shape
    kv_width = k_out.shape[1]
    experts = gates_out.shape[0]
    shards, depth, total = wbuf.shape
    me = lax.axis_index("shard")
    own, at = [], 0
    for i, part in enumerate((wq_hbm, wk_hbm, wv_hbm, wo_hbm, ws_hbm)):
        own.append(pltpu.make_async_copy(part, wbuf.at[me, :, at:at + part.shape[1]], osem.at[i]))
        own[-1].start()
        at += part.shape[1]
    greet(spread)
    gather = PlaneGather(wbuf, wbuf.at[me], send, recv)
    for copy in own:
        copy.wait()
    gather.start()
    far = RepSends(ccol_out, cot_ref, zsend, zrecv, False)
    if spread:
        far.start()
    near = PlaneGather(cown_out, cot_ref, csend, crecv)
    own_cot = pltpu.make_async_copy(cot_ref, cown_out.at[me], lsem.at[2])
    own_cot.start()
    inputs = tok_ref[...].astype(f32)
    scaled = inputs * norm_scale(inputs)
    for step in range(gather.steps):
        gather.forward(step)
    gather.finish()
    near.start()
    keep = pltpu.make_async_copy(wbuf, wall_out, lsem.at[1])
    keep.start()
    cut = [0, width, width + kv_width, width + 2 * kv_width, 2 * width + 2 * kv_width]
    small = wbuf[:, :, cut[4]:].reshape(shards * depth, total - cut[4])
    wide = small.astype(f32).T
    gain_one, gain_two = wide[experts:experts + 1], wide[experts + 1:experts + 2]
    n1_out[...] = (scaled * gain_one).astype(bf16)

    def project(j, carry):
        w = wbuf[:, :, lanes(j, 2)].reshape(shards * depth, 2 * LANES)
        qkv_ref[:, lanes(j, 2)] = dot(n1_out[...], w)
        return carry
    lax.fori_loop(0, cut[3] // (2 * LANES), project, 0)
    cosine, sine = cos_ref[...], sin_ref[...]
    for j in range(width // LANES):
        q_out[:, j * LANES:(j + 1) * LANES] = rotate(qkv_ref[:, j * LANES:(j + 1) * LANES], cosine, sine, 1.0).astype(bf16)
    for j in range(kv_width // LANES):
        at = slice(cut[1] + j * LANES, cut[1] + (j + 1) * LANES)
        k_out[:, j * LANES:(j + 1) * LANES] = rotate(qkv_ref[:, at], cosine, sine, 1.0).astype(bf16)
    v_out[...] = qkv_ref[:, cut[2]:cut[3]].astype(bf16)
    prefix_len = prefix_ref[0]

    near.forward(0)

    def head(j, carry):
        keys = one_head_twice(k_out[:, lanes(j // 2)], j % 2)
        values = one_head_twice(v_out[:, lanes(j // 2)], j % 2)
        prob = probabilities(two_heads(q_out[:, lanes(j)]), keys, prefix_len)
        both = dot(prob.astype(bf16), values)
        low = lax.broadcasted_iota(jnp.int32, (count, LANES), 1) < HEAD_SIZE
        att_out[:, lanes(j)] = jnp.where(low, both[:count], both[count:]).astype(bf16)
        return carry
    lax.fori_loop(0, KEY_VALUE_HEADS, head, 0)
    for step in range(1, near.steps):
        near.forward(step)

    def project_out(j, carry):
        w = wbuf[:, :, pl.ds(pl.multiple_of(cut[3] + j * 2 * LANES, LANES), 2 * LANES)].reshape(shards * depth, 2 * LANES)
        qkv_ref[:, lanes(j, 2)] = dot(att_out[...], w)
        return carry
    lax.fori_loop(0, width // (2 * LANES), project_out, 0)
    hidden = inputs + branch_scale * qkv_ref[:, :width]
    hid_out[...] = hidden
    x = (hidden * norm_scale(hidden) * gain_two).astype(bf16)
    x_out[...] = x
    logits = dot(x, small).T[:experts]
    expert = lax.broadcasted_iota(jnp.int32, (experts, count), 0)
    named = expert < 0
    for k in range(routes_ref.shape[0]):
        named = named | (routes_ref[k:k + 1, :] == expert)
    top = jnp.max(jnp.where(named, logits, masked_value), axis=0, keepdims=True)
    weights = jnp.where(named, jnp.exp(jnp.where(named, logits - top, 0.0)), 0.0)
    gates_out[...] = weights / jnp.sum(weights, axis=0, keepdims=True)
    keep.wait()
    near.finish()
    own_cot.wait()
    if spread:
        far.finish()

def front(tokens, prefix, routes, mine, cot, cosine, sine, experts, kv_width, spread):
    count, width = tokens.shape
    shards, reps = lax.axis_size("shard"), lax.axis_size("rep")
    depth, total = tokens.shape[1] // shards, sum(part.shape[1] for part in mine)
    v = pl.BlockSpec(memory_space=pltpu.VMEM)
    any_ = pl.BlockSpec(memory_space=pl.ANY)
    sds = jax.ShapeDtypeStruct
    n = PlaneGather.copies(shards)
    return pl.pallas_call(
        functools.partial(front_kernel, spread),
        out_shape=[
            sds((shards, depth, total), bf16), sds((shards, count, width), bf16), sds((reps, count, width), bf16), sds((count, width), bf16), sds((count, kv_width), bf16), sds((count, kv_width), bf16),
            sds((count, width), bf16), sds((count, width), f32), sds((count, width), bf16), sds((experts, count), f32), sds((count, width), bf16),
        ],
        in_specs=[pl.BlockSpec(memory_space=pltpu.SMEM), v, v, v, v] + [any_] * 6,
        out_specs=[any_] * 3 + [v] * 8,
        scratch_shapes=[
            pltpu.VMEM((shards, depth, total), bf16), pltpu.VMEM((count, width + 2 * kv_width), f32),
            *[pltpu.SemaphoreType.DMA((k,)) for k in (n, n, n, n, reps, reps, 3, 5)],
        ],
        compiler_params=pltpu.CompilerParams(vmem_limit_bytes=60 << 20, has_side_effects=True, collective_id=1),
        name="front",
    )(prefix, tokens, routes, cosine, sine, *mine, cot)

class PlaneReduce:
    def __init__(self, mine, theirs, from_core, from_chip, csend, crecv, send, recv):
        self.mine, self.theirs, self.from_core, self.from_chip = mine, theirs, from_core, from_chip
        self.csend, self.crecv, self.send, self.recv = csend, crecv, send, recv
        self.rep, self.me = lax.axis_index("rep"), lax.axis_index("shard")
        self.core = self.me % 2
        self.bits = [1 << i for i in range(1, lax.axis_size("shard").bit_length() - 1)]
        self.steps = len(self.bits)

    def owner(self, core, u):
        at = flip(self.me, 1) if core else self.me
        of = (1 - self.core) if core else self.core
        for step in range(self.steps):
            if u >> step & 1:
                at = turned(at, of, step, self.bits)
        return at

    def core_copy(self, u):
        return pltpu.make_async_remote_copy(
            src_ref=self.theirs.at[u], dst_ref=self.from_core.at[u], send_sem=self.csend.at[u], recv_sem=self.crecv.at[u],
            device_id=(self.rep, flip(self.me, 1)), device_id_type=MESH,
        )

    def slot(self, step, u):
        return (1 << self.steps) - (1 << (self.steps - step)) + (u >> (step + 1))

    def chip_copy(self, step, u):
        slot = self.slot(step, u)
        return pltpu.make_async_remote_copy(
            src_ref=self.mine.at[u], dst_ref=self.from_chip.at[slot], send_sem=self.send.at[slot], recv_sem=self.recv.at[slot],
            device_id=(self.rep, turned(self.me, self.core, step, self.bits)), device_id_type=MESH,
        )

    def total(self, u, before, rows):
        whole = self.mine[u, rows].astype(f32) + self.from_core[u, rows].astype(f32)
        for step in range(before):
            whole = whole + self.from_chip[self.slot(step, u), rows].astype(f32)
        return whole

    def send_on(self, step, u):
        self.core_copy(u).wait_recv()
        count = self.mine.shape[1]
        piece = 32

        def add(i, carry):
            rows = pl.ds(pl.multiple_of(i * piece, piece), piece)
            self.mine[u, rows] = self.total(u, step, rows).astype(bf16)
            return carry
        lax.fori_loop(0, count // piece, add, 0)
        self.chip_copy(step, u).start()

    def group(self, step):
        return [u for u in range(1 << self.steps) if u % (2 << step) == 1 << step]

    def arrive(self, step):
        for u in self.group(step):
            self.chip_copy(step, u).wait_recv()

    def advance(self, step):
        if step < self.steps:
            if step:
                self.arrive(step - 1)
            for u in self.group(step):
                self.send_on(step, u)

    def last(self, out, plus=None):
        self.arrive(self.steps - 1)
        self.core_copy(0).wait_recv()
        count = self.mine.shape[1]
        piece = 32

        def add(i, carry):
            rows = pl.ds(pl.multiple_of(i * piece, piece), piece)
            whole = self.total(0, self.steps, rows)
            out[rows] = (whole if plus is None else whole + plus[rows]).astype(out.dtype)
            return carry
        lax.fori_loop(0, count // piece, add, 0)

    def finish(self):
        for u in range(1 << self.steps):
            self.core_copy(u).wait_send()
        for step in range(self.steps):
            for u in self.group(step):
                self.chip_copy(step, u).wait_send()


def own_kernel(spread, nb, x_ref, gates_ref, c_hbm, ccol_hbm, wg_hbm, wu_hbm, wd_hbm,
               xown_out, xcol_out, gown_out, gcol_out, back_out, dg_out, mix_out, coth_out,
               wg, wu, wd, xb, cb, xg_ref, cg_ref, sg_ref, y_ref, ds_ref, mine, theirs, mix, from_core, from_chip,
               gown, gcol, dgs, dgr,
               xs, xr, zxs, zxr, zgs, zgr, gs, gr, dss, dsr, css, csr, hs, hr, wsem, bsem, lsem, msem, *csems):
    count, width = x_ref.shape
    local, _, hidden = wg.shape
    rep, me = lax.axis_index("rep"), lax.axis_index("shard")
    shards = lax.axis_size("shard")
    first = me * local
    greet(spread)
    near = PlaneGather(xown_out, x_ref, xs, xr)
    near.start()
    gown[me] = gates_ref[...]

    def peer(j):
        return (rep, (me + j) % shards)

    gate_sends = [
        pltpu.make_async_remote_copy(
            src_ref=gates_ref, dst_ref=gown.at[me], send_sem=gs.at[j - 1], recv_sem=gr.at[j - 1],
            device_id=peer(j), device_id_type=MESH,
        )
        for j in range(1, shards)
    ]
    for copy in gate_sends:
        copy.start()
    far = [RepSends(xcol_out, x_ref, zxs, zxr, False), RepSends(gcol, gates_ref, zgs, zgr, True)] if spread else []
    for sends in far:
        sends.start()
    cots = Spread(coth_out, ccol_hbm, c_hbm, *csems)
    reps = lax.axis_size("rep")
    if spread:
        cots.start_straight()
    own_x = pltpu.make_async_copy(x_ref, xown_out.at[me], lsem)
    own_x.start()
    weights = [pltpu.make_async_copy(a, b, wsem.at[i]) for i, (a, b) in enumerate(((wg_hbm, wg), (wu_hbm, wu), (wd_hbm, wd)))]
    for copy in weights:
        copy.start()
    reduce = PlaneReduce(mine, theirs, from_core, from_chip, css, csr, hs, hr)
    for copy in gate_sends:
        copy.wait_recv()
    order = list(range(1 << reduce.steps))
    half = nb // 2
    dg_sends, mixes = [], []

    def fetch(at, slot):
        return (pltpu.make_async_copy(xown_out.at[at], xb.at[slot], bsem.at[0, slot]),
                pltpu.make_async_copy(c_hbm.at[at], cb.at[slot], bsem.at[1, slot]))

    chunks = [order[q:q + half] for q in range(0, len(order), half)]
    forwarded = 0
    for q, chunk in enumerate(chunks):
        plan = [(core, u) for u in chunk for core in (0, 1)]
        owners = [reduce.owner(core, u) for core, u in plan]
        while forwarded < chunk[-1].bit_length():
            near.forward(forwarded)
            forwarded += 1
        if not q:
            own_x.wait()
        for u in chunk:
            near.core_copy(u).wait_recv()
        for copy in fetch(owners[0], 0):
            copy.start()
        for b in range(nb):
            if b + 1 < nb:
                for copy in fetch(owners[b + 1], (b + 1) % 2):
                    copy.start()
            for copy in fetch(owners[b], b % 2):
                copy.wait()
            gather_block(xb[b % 2], cb[b % 2], gown[owners[b]], first, local, xg_ref, cg_ref, sg_ref, b * CAP)
        if not q:
            for copy in weights:
                copy.wait()

        def expert(l, carry):
            inner, raw, d_gate, d_up, scaled = expert_parts(xg_ref[l], cg_ref[l], sg_ref[l], wg[l], wu[l], wd[l])
            ds_ref[l] = branch_scale * jnp.sum(inner * raw, axis=1, keepdims=True)
            rows = pl.ds(pl.multiple_of(l * CAP, CAP), CAP)
            out = dot(scaled, wd[l]).astype(bf16)
            d_in = (dot(d_gate, wg[l], ((1,), (1,))) + dot(d_up, wu[l], ((1,), (1,)))).astype(bf16)
            for b in range(nb):
                y_ref[b, rows, :width] = out[b * CAP:(b + 1) * CAP]
                y_ref[b, rows, width:] = d_in[b * CAP:(b + 1) * CAP]
            return carry
        lax.fori_loop(0, local, expert, 0)
        if q + 1 < len(chunks):
            while forwarded < chunks[q + 1][-1].bit_length():
                near.forward(forwarded)
                forwarded += 1
        if spread:
            if not q:
                cots.begin(2)
            else:
                cots.forward(2)
        for b in range(nb):
            core, u = plan[b]
            parts = slot_one_hot(slot_ranks(gown[owners[b]]), first, local)
            table = jnp.concatenate(parts, axis=0).astype(bf16)
            both = dot(table, y_ref[b], ((0,), (0,))).astype(bf16)
            mix[core, u] = both[:, :width]
            mixes.append(pltpu.make_async_copy(mix.at[core, u], mix_out.at[owners[b]], msem.at[core, u]))
            mixes[-1].start()
            (theirs if core else mine)[u] = both[:, width:]
            if core:
                reduce.core_copy(u).start()
            dgs[owners[b]] = jnp.concatenate(
                [jnp.sum(parts[l] * ds_ref[l, b * CAP:(b + 1) * CAP], axis=0, keepdims=True) for l in range(local)], axis=0
            )
        for u in chunk:
            if u % 2:
                reduce.send_on(0, u)
    for j in range(1, shards):
        copy = pltpu.make_async_remote_copy(
            src_ref=dgs.at[(me + j) % shards], dst_ref=dgr.at[me], send_sem=dss.at[j - 1], recv_sem=dsr.at[j - 1],
            device_id=peer(j), device_id_type=MESH,
        )
        copy.start()
        dg_sends.append(copy)
    dgr[me] = dgs[me]
    gown_out[...] = gown[...]
    for step in range(1, reduce.steps):
        reduce.advance(step)
    reduce.last(back_out)
    for copy in dg_sends:
        copy.wait()
    dg_out[...] = dgr[...]
    if spread:
        cots.end(2)
        cots.got_straight(0)
        cots.got_straight(1)
        cots.sent_straight()
    reduce.finish()
    for copy in mixes:
        copy.wait()
    near.sent()
    for copy in gate_sends:
        copy.wait_send()
    for sends in far:
        sends.finish()
    if spread:
        gcol_out[...] = gcol[...]


def moe_own(x, gates, c, ccol, wg, wu, wd, spread, nb=4):
    count, width = x.shape
    local, _, hidden = wg.shape
    shards, reps = lax.axis_size("shard"), lax.axis_size("rep")
    experts = local * shards
    v = pl.BlockSpec(memory_space=pltpu.VMEM)
    any_ = pl.BlockSpec(memory_space=pl.ANY)
    sds = jax.ShapeDtypeStruct
    n = PlaneGather.copies(shards)
    rows = nb * CAP
    half = shards // 2
    dma = lambda *k: pltpu.SemaphoreType.DMA(k)
    return pl.pallas_call(
        functools.partial(own_kernel, spread, nb),
        out_shape=[
            sds((shards, count, width), bf16), sds((reps, count, width), bf16), sds((shards, experts, count), f32),
            sds((reps, experts, count), f32), sds((count, width), f32), sds((shards, local, count), f32),
            sds((shards, count, width), bf16), sds((max(reps - 1, 1), shards, count, width) if spread else (1, 1, 16, LANES), bf16),
        ],
        in_specs=[v, v, any_, any_, any_, any_, any_],
        out_specs=[any_, any_, v, v, v, v, any_, any_],
        scratch_shapes=[
            pltpu.VMEM(wg.shape, bf16), pltpu.VMEM(wu.shape, bf16), pltpu.VMEM(wd.shape, bf16),
            pltpu.VMEM((2, count, width), bf16), pltpu.VMEM((2, count, width), bf16),
            pltpu.VMEM((local, rows, width), bf16), pltpu.VMEM((local, rows, width), bf16), pltpu.VMEM((local, rows, 1), f32),
            pltpu.VMEM((nb, local * CAP, 2 * width), bf16), pltpu.VMEM((local, rows, 1), f32),
            *[pltpu.VMEM((k, count, width), bf16) for k in (half, half)], pltpu.VMEM((2, half, count, width), bf16),
            *[pltpu.VMEM((k, count, width), bf16) for k in (half, half - 1)],
            pltpu.VMEM((shards, experts, count), f32), pltpu.VMEM((reps, experts, count), f32),
            pltpu.VMEM((shards, local, count), f32), pltpu.VMEM((shards, local, count), f32),
            dma(n), dma(n), dma(reps), dma(reps), dma(reps), dma(reps), dma(shards), dma(shards), dma(shards), dma(shards),
            dma(half), dma(half), dma(half), dma(half), dma(3), dma(2, 2), pltpu.SemaphoreType.DMA, dma(2, half),
            *Spread.semaphores(shards, reps),
        ],
        compiler_params=pltpu.CompilerParams(vmem_limit_bytes=60 << 20, has_side_effects=True, collective_id=2),
        name="own_experts",
    )(x, gates, c, ccol, wg, wu, wd)

def norm_backward(rows, scaling, gain, upstream):
    weighted = upstream * gain
    inner_mean = jnp.mean(weighted * rows, axis=-1, keepdims=True)
    gradient = scaling * weighted - rows * (scaling * scaling * scaling) * inner_mean
    return gradient, jnp.sum(upstream * rows * scaling, axis=0, keepdims=True)


def back_kernel(prefix_ref, tok_ref, cot_ref, cos_ref, sin_ref, w_ref, q_ref, k_ref, v_ref, att_ref, n1_ref, x_ref,
                hid_ref, gates_ref, dg_ref, back_ref, dtok_out, shares_out, dqkv_ref, datt_ref, dproj_ref):
    count, width = tok_ref.shape
    kv_width = k_ref.shape[1]
    experts = gates_ref.shape[0]
    shards, depth, total = w_ref.shape
    rows = shards * depth
    cut = [0, width, width + kv_width, width + 2 * kv_width, 2 * width + 2 * kv_width]
    small = w_ref[:, :, cut[4]:].reshape(rows, total - cut[4])
    wide = small.astype(f32).T
    gain_one, gain_two = wide[experts:experts + 1], wide[experts + 1:experts + 2]
    hidden = hid_ref[...]
    gates, d_gates = gates_ref[...], dg_ref[...]
    d_logits = gates * (d_gates - jnp.sum(gates * d_gates, axis=0, keepdims=True))
    none = jnp.zeros((LANES - experts, count), f32)
    d_logits = jnp.concatenate([d_logits, none], axis=0).T.astype(bf16)
    d_normed_two = back_ref[...] + dot(d_logits, small, ((1,), (1,)))
    d_hidden, d_gain_two = norm_backward(hidden, norm_scale(hidden), gain_two, d_normed_two)
    d_hidden = d_hidden + cot_ref[...].astype(f32)
    dtok_out[...] = d_hidden
    dproj_ref[...] = (branch_scale * d_hidden).astype(bf16)
    tile = 2 * LANES

    def out_tile(j, carry):
        grad = dot(att_ref[...], dproj_ref[:, lanes(j, 2)], ((0,), (0,))).astype(bf16)
        at = pl.ds(pl.multiple_of(cut[3] + j * tile, LANES), tile)
        shares_out[:, :, at] = grad.reshape(shards, depth, tile)
        return carry
    lax.fori_loop(0, width // tile, out_tile, 0)
    datt_ref[...] = dot(dproj_ref[...], w_ref[:, :, cut[3]:cut[4]].reshape(rows, width), ((1,), (1,))).astype(bf16)
    cosine, sine = cos_ref[...], sin_ref[...]
    prefix_len = prefix_ref[0]
    low = lax.broadcasted_iota(jnp.int32, (count, LANES), 1) < HEAD_SIZE

    def pair(p, carry):
        at_k = pl.ds(pl.multiple_of(cut[1] + p * LANES, LANES), LANES)
        at_v = pl.ds(pl.multiple_of(cut[2] + p * LANES, LANES), LANES)
        d_keys, d_values = [], []
        for odd in range(2):
            j = 2 * p + odd
            keys = one_head_twice(k_ref[:, lanes(p)], odd)
            values = one_head_twice(v_ref[:, lanes(p)], odd)
            query2, d_att2 = two_heads(q_ref[:, lanes(j)]), two_heads(datt_ref[:, lanes(j)])
            prob = probabilities(query2, keys, prefix_len)
            d_value = dot(prob.astype(bf16), d_att2, ((0,), (0,)))
            d_prob = dot(d_att2, values, ((1,), (1,)))
            weighted = jnp.sum(prob * d_prob, axis=-1, keepdims=True)
            d_score = (prob * (d_prob - weighted) * score_scale).astype(bf16)
            d_query = dot(d_score, keys)
            d_query = jnp.where(low, d_query[:count], d_query[count:])
            dqkv_ref[:, lanes(j)] = rotate(d_query, cosine, sine, -1.0).astype(bf16)
            d_key = dot(d_score, query2, ((0,), (0,)))
            d_keys.append(d_key + pltpu.roll(d_key, HEAD_SIZE, 1))
            d_values.append(d_value + pltpu.roll(d_value, HEAD_SIZE, 1))
        dqkv_ref[:, at_k] = rotate(jnp.where(low, *d_keys), cosine, sine, -1.0).astype(bf16)
        dqkv_ref[:, at_v] = jnp.where(low, *d_values).astype(bf16)
        return carry
    lax.fori_loop(0, KEY_VALUE_HEADS // 2, pair, 0)

    def in_tile(j, carry):
        grad = dot(n1_ref[...], dqkv_ref[:, lanes(j, 2)], ((0,), (0,))).astype(bf16)
        shares_out[:, :, lanes(j, 2)] = grad.reshape(shards, depth, tile)
        return carry
    lax.fori_loop(0, cut[3] // tile, in_tile, 0)
    d_normed_one = dot(dqkv_ref[...], w_ref[:, :, :cut[3]].reshape(rows, cut[3]), ((1,), (1,)))
    inputs = tok_ref[...].astype(f32)
    d_inputs, d_gain_one = norm_backward(inputs, norm_scale(inputs), gain_one, d_normed_one)
    dtok_out[...] += d_inputs
    row = lax.broadcasted_iota(jnp.int32, (LANES, rows), 0)
    gains = jnp.where(row == experts, d_gain_one, jnp.where(row == experts + 1, d_gain_two, 0.0)).T
    d_small = (dot(x_ref[...], d_logits, ((0,), (0,))) + gains).astype(bf16)
    shares_out[:, :, cut[4]:] = d_small.reshape(shards, depth, total - cut[4])


def attention_back(prefix, tokens, cot, cosine, sine, packed, query, keys, values, attended, n1, x, hidden, gates, d_gates, back):
    count, width = tokens.shape
    v = pl.BlockSpec(memory_space=pltpu.VMEM)
    sds = jax.ShapeDtypeStruct
    return pl.pallas_call(
        back_kernel,
        out_shape=[sds((count, width), f32), sds(packed.shape, bf16)],
        in_specs=[pl.BlockSpec(memory_space=pltpu.SMEM)] + [v] * 15,
        out_specs=[v] * 2,
        scratch_shapes=[
            pltpu.VMEM((count, width + 2 * keys.shape[1]), bf16), pltpu.VMEM((count, width), bf16), pltpu.VMEM((count, width), bf16),
        ],
        compiler_params=pltpu.CompilerParams(vmem_limit_bytes=60 << 20),
        name="attention_back",
    )(prefix, tokens, cot, cosine, sine, packed, query, keys, values, attended, n1, x, hidden, gates, d_gates, back)

def spread_kernel(nb, xown_hbm, cown_hbm, xcol_hbm, ccol_hbm, gown_ref, gcol_ref, wg_hbm, wu_hbm, wd_hbm, coth_in,
                  xoth_hbm, coth_hbm, og_hbm, ou_hbm, od_hbm, glast_ref,
                  xbuf, cbuf, wg, wu, wd, ag, au, ad, xg_ref, cg_ref, sg_ref, goth, send, recv, bsem, wsem, *sems):
    xsems, csems = sems[:7], sems[7:]
    local = wg.shape[0]
    shards = gown_ref.shape[0]
    rep, me = lax.axis_index("rep"), lax.axis_index("shard")
    reps = lax.axis_size("rep")
    first = me * local
    chunks = shards // nb

    xs = Spread(xoth_hbm, xcol_hbm, xown_hbm, *xsems)
    cs = Spread(coth_hbm, ccol_hbm, cown_hbm, *csems)
    both = (xs, cs)

    def each(act, j):
        for one in both:
            act(one, j)

    def gate_gathers():
        return [PlaneGather(goth.at[j - 1], gcol_ref.at[(rep + j) % reps], send.at[j - 1], recv.at[j - 1]) for j in range(1, reps)]

    def fetch(x, c, q, slot):
        return (pltpu.make_async_copy(x.at[pl.ds(q * nb, nb)], xbuf.at[slot], bsem.at[0, slot]),
                pltpu.make_async_copy(c.at[pl.ds(q * nb, nb)], cbuf.at[slot], bsem.at[1, slot]))

    def replica(x, c, g, midway, last):
        for copy in fetch(x, c, 0, 0):
            copy.start()

        def chunk(q, carry):
            slot = lax.rem(q, 2)

            @pl.when(q + 1 < chunks)
            def _():
                for copy in fetch(x, c, q + 1, 1 - slot):
                    copy.start()
            for copy in fetch(x, c, q, slot):
                copy.wait()

            def block(b, carry):
                gather_block(xbuf[slot, b], cbuf[slot, b], g[q * nb + b], first, local, xg_ref, cg_ref, sg_ref,
                             pl.multiple_of(b * CAP, CAP))
                return carry
            lax.fori_loop(0, nb, block, 0)

            def expert(l, carry):
                add_expert(l, xg_ref, cg_ref, sg_ref, wg, wu, wd, ag, au, ad)

                @pl.when((q == chunks // 2) & (l == 0))
                def _():
                    midway()
                return carry
            lax.fori_loop(0, local, expert, 0)
            return carry
        lax.fori_loop(0, chunks, chunk, 0)
        last()

    greet(True)
    xs.begin(2)
    for j in range(1, reps):
        goth[j - 1, me] = gcol_ref[(rep + j) % reps]
    for gather in gate_gathers():
        gather.start()
    xs.start_straight()
    for up in (0, 1):
        cs.start_across(up)
    weights = [pltpu.make_async_copy(a, b, wsem.at[i]) for i, (a, b) in enumerate(((wg_hbm, wg), (wu_hbm, wu), (wd_hbm, wd)))]
    for copy in weights:
        copy.start()
    ag[...] = jnp.zeros_like(ag)
    au[...] = jnp.zeros_like(au)
    ad[...] = jnp.zeros_like(ad)
    for copy in weights:
        copy.wait()

    def midway_own():
        xs.forward(2)
        for gather in gate_gathers():
            gather.forward(0)
        on_ends(lambda: each(Spread.begin, reps - 1), lambda: each(Spread.begin, 1))

    def last_own():
        xs.end(2)
        for gather in gate_gathers():
            for step in range(1, gather.steps):
                gather.forward(step)
        for gather in gate_gathers():
            gather.finish()
        for up in (0, 1):
            cs.end_across(up)

    def midway_two():
        on_ends(lambda: each(Spread.forward, reps - 1), lambda: each(Spread.forward, 1))
        xs.got_straight(1)
        xs.start_across(1)

        @pl.when(rep == 0)
        def _():
            xs.got_straight(0)
            xs.start_across(0)

    def last_two():
        xs.end_across(1)
        pl.when(rep == 0)(lambda: xs.end_across(0))

    def midway_three():
        @pl.when(rep > 0)
        def _():
            xs.got_straight(0)
            xs.start_across(0)

    def last_three():
        on_ends(lambda: each(Spread.end, reps - 1), lambda: each(Spread.end, 1))
        pl.when(rep > 0)(lambda: xs.end_across(0))

    replica(xown_hbm, cown_hbm, gown_ref, midway_own, last_own)
    replica(xoth_hbm.at[1], coth_hbm.at[1], goth.at[1], midway_two, last_two)
    third, left = late_places(rep, reps)
    replica(xoth_hbm.at[third], coth_hbm.at[third], goth.at[third], midway_three, last_three)
    xs.sent_straight()
    glast_ref[...] = goth[left]
    outs = [pltpu.make_async_copy(a, b, wsem.at[i]) for i, (a, b) in enumerate(((ag, og_hbm), (au, ou_hbm), (ad, od_hbm)))]
    for copy in outs:
        copy.start()
    for copy in outs:
        copy.wait()


def moe_spread_sums(xown, cown, xcol, ccol, coth, gown, gcol, wg, wu, wd, nb=4):
    shards, count, width = xown.shape
    reps = xcol.shape[0]
    local, _, hidden = wg.shape
    any_ = pl.BlockSpec(memory_space=pl.ANY)
    v = pl.BlockSpec(memory_space=pltpu.VMEM)
    rows = nb * CAP
    n = PlaneGather.copies(shards)
    slots = reps * shards * local * CAP
    outs = pl.pallas_call(
        functools.partial(spread_kernel, nb),
        out_shape=[jax.ShapeDtypeStruct((reps - 1, shards, count, width), bf16)] * 2
        + [jax.ShapeDtypeStruct(w.shape, f32) for w in (wg, wu, wd)] + [jax.ShapeDtypeStruct(gown.shape, f32)],
        in_specs=[any_, any_, any_, any_, v, v, any_, any_, any_, any_],
        input_output_aliases={9: 1},
        out_specs=[any_] * 5 + [v],
        scratch_shapes=[
            pltpu.VMEM((2, nb, count, width), bf16), pltpu.VMEM((2, nb, count, width), bf16),
            pltpu.VMEM(wg.shape, bf16), pltpu.VMEM(wu.shape, bf16), pltpu.VMEM(wd.shape, bf16),
            pltpu.VMEM(wg.shape, f32), pltpu.VMEM(wu.shape, f32), pltpu.VMEM(wd.shape, f32),
            pltpu.VMEM((local, rows, width), bf16), pltpu.VMEM((local, rows, width), bf16), pltpu.VMEM((local, rows, 1), f32),
            pltpu.VMEM((reps - 1, shards, *gown.shape[1:]), f32),
            pltpu.SemaphoreType.DMA((reps - 1, n)), pltpu.SemaphoreType.DMA((reps - 1, n)),
            pltpu.SemaphoreType.DMA((2, 2)), pltpu.SemaphoreType.DMA((3,)),
            *Spread.semaphores(shards, reps), *Spread.semaphores(shards, reps),
        ],
        compiler_params=pltpu.CompilerParams(vmem_limit_bytes=60 << 20, has_side_effects=True, collective_id=3),
        cost_estimate=pl.CostEstimate(
            flops=12 * slots * width * hidden, transcendentals=slots * hidden, bytes_accessed=4 * reps * shards * count * width
        ),
        name="spread_expert_sums",
    )(xown, cown, xcol, ccol, gown, gcol, wg, wu, wd, coth)
    return outs[0], outs[1], outs[5], outs[2:5]

def rotary_tables(count):
    half = HEAD_SIZE // 2
    inverse = np.exp(np.arange(half) * (-2.0 * math.log(10000.0) / HEAD_SIZE))
    angles = np.tile(np.arange(count)[:, None] * inverse[None, :], (1, LANES // half))
    return np.cos(angles).astype(np.float32), np.sin(angles).astype(np.float32)


def pack_small(w_router, norm_attn, norm_moe):
    small = jnp.concatenate([w_router, norm_attn[:, None], norm_moe[:, None]], axis=1)
    return jnp.pad(small, ((0, 0), (0, LANES - small.shape[1])))


def body(
    tokens, prefix, routes, cotangent, w_query, key_weight, value_weight, w_out,
    norm_attn, norm_moe, w_router, w_gate, w_up, w_down,
):
    count, width = tokens.shape
    local = w_gate.shape[0]
    shards, reps = lax.axis_size("shard"), lax.axis_size("rep")
    experts = local * shards
    kv_width = key_weight.shape[1]
    spread = reps == GATHERED_REPLICAS
    cosine, sine = rotary_tables(count)
    packed_own = (w_query, key_weight, value_weight, w_out, pack_small(w_router, norm_attn, norm_moe))
    packed, cot_own, cot_col, query, keys, values, attended, hidden_one, normed_two, gates, normed_one = front(
        tokens, prefix, routes.T, packed_own, cotangent, cosine, sine, experts, kv_width, spread
    )
    x_own, x_col, gates_own, gates_col, back, d_gates, mixture, cot_oth = moe_own(
        normed_two, gates, cot_own, cot_col, w_gate, w_up, w_down, spread
    )
    mixture = lax.psum_scatter(mixture.reshape(-1, width), "shard", scatter_dimension=0, tiled=True)
    d_tokens, shares = attention_back(
        prefix, tokens, cotangent, cosine, sine, packed, query, keys, values, attended, normed_one, normed_two, hidden_one,
        gates, d_gates.reshape(experts, count), back,
    )
    shares = shares.reshape(width, -1)
    if spread:
        x_own, shares = lax.optimization_barrier((x_own, shares))
        x_oth, cot_oth, gates_oth, sums = moe_spread_sums(
            x_own, cot_own, x_col, cot_col, cot_oth, gates_own, gates_col, w_gate, w_up, w_down
        )
        shares = lax.psum_scatter(shares, "shard", scatter_dimension=0, tiled=True)
        shares, gates_oth = lax.optimization_barrier((shares, gates_oth))
        sums = moe_sums(x_oth, cot_oth, gates_oth, w_gate, w_up, w_down, sums)
    else:
        sums = moe_sums(x_own, cot_own, gates_own, w_gate, w_up, w_down)
        sums = [lax.psum(a.astype(bf16), "rep").astype(f32) for a in sums]
        shares = lax.psum_scatter(shares, "shard", scatter_dimension=0, tiled=True)
    d_w_gate, d_w_up, d_w_down = sums
    totals = lax.psum(shares, "rep").astype(f32)
    cuts = [width, width + kv_width, width + 2 * kv_width, 2 * width + 2 * kv_width]
    d_wq, d_wk, d_wv, d_wo, small = jnp.split(totals, cuts, axis=1)
    result = (hidden_one + mixture.astype(f32)).astype(bf16)
    return (
        result, d_tokens, d_wq, d_wk, d_wv, d_wo, small[:, experts], small[:, experts + 1],
        small[:, :experts], d_w_gate, d_w_up, d_w_down,
    )


def solution(mesh):
    rows = P(("rep", "shard"), None)
    one, two, three = P("shard"), P("shard", None), P("shard", None, None)
    return jax.shard_map(
        body,
        mesh=mesh,
        in_specs=(rows, P(("rep", "shard")), rows, rows, two, two, two, two, one, one, two, three, three, three),
        out_specs=(rows, rows, two, two, two, two, one, one, two, three, three, three),
        check_vma=False,
    )
```

```python
import functools
import math

import jax
import jax.numpy as jnp
import numpy as np
from jax import lax
from jax.experimental import pallas as pl
from jax.experimental.pallas import tpu as pltpu
from jax.sharding import PartitionSpec as P

QUERY_HEADS = 16
KEY_VALUE_HEADS = 8
HEAD_SIZE = 64
CAP = 96
LANES = 128
GATHERED_REPLICAS = 4

epsilon = 1e-06
score_scale = 0.015625
branch_scale = 0.22
masked_value = -1e30

f32 = jnp.float32
bf16 = jnp.bfloat16
MESH = pl.DeviceIdType.MESH


def dot(left, right, contract=((1,), (0,))):
    return lax.dot_general(left, right, (contract, ((), ())), preferred_element_type=f32)

def slot_ranks(gates):
    tokens = gates.shape[1]
    named = gates > 0
    before = lax.broadcasted_iota(jnp.int32, (tokens, tokens), 0) < lax.broadcasted_iota(jnp.int32, (tokens, tokens), 1)
    rank = dot(named.astype(f32).astype(bf16), before.astype(f32).astype(bf16))
    return jnp.where(named, rank, -1.0)

def pick_row(table, row):
    here = lax.broadcasted_iota(jnp.int32, table.shape, 0) == row
    return jnp.sum(jnp.where(here, table, 0.0), axis=0, keepdims=True)

def slot_one_hot(ranks, first, local):
    tokens = ranks.shape[1]
    slot = lax.broadcasted_iota(jnp.int32, (CAP, tokens), 0).astype(f32)
    return [jnp.where(pick_row(ranks, first + l) == slot, 1.0, 0.0) for l in range(local)]

def gather_block(x, c, gates, first, local, xg_ref, cg_ref, sg_ref, at):
    ranks = slot_ranks(gates)
    parts = slot_one_hot(ranks, first, local)
    table = jnp.concatenate(parts, axis=0).astype(bf16)
    xg = dot(table, x).astype(bf16)
    cg = dot(table, c).astype(bf16)
    for l in range(local):
        rows = slice(l * CAP, (l + 1) * CAP)
        xg_ref[l, pl.ds(at, CAP), :] = xg[rows]
        cg_ref[l, pl.ds(at, CAP), :] = cg[rows]
        gate = jnp.sum(parts[l] * pick_row(gates, first + l), axis=1, keepdims=True)
        sg_ref[l, pl.ds(at, CAP), :] = branch_scale * gate
    return parts

def expert_parts(xg, cg, scale, wg, wu, wd):
    gate_part = dot(xg, wg)
    up_part = dot(xg, wu)
    raw = dot(cg, wd, ((1,), (1,)))
    sigma = 1.0 / (1.0 + jnp.exp(-gate_part))
    act = gate_part * sigma
    inner = act * up_part
    d_inner = raw * scale
    d_gate = (d_inner * up_part * (sigma + act * (1.0 - sigma))).astype(bf16)
    d_up = (d_inner * act).astype(bf16)
    scaled = (inner * scale).astype(bf16)
    return inner, raw, d_gate, d_up, scaled

def add_expert(l, xg_ref, cg_ref, sg_ref, wg, wu, wd, ag, au, ad):
    xg, cg = xg_ref[l], cg_ref[l]
    _, _, d_gate, d_up, scaled = expert_parts(xg, cg, sg_ref[l], wg[l], wu[l], wd[l])
    ag[l] += dot(xg, d_gate, ((0,), (0,)))
    au[l] += dot(xg, d_up, ((0,), (0,)))
    ad[l] += dot(scaled, cg, ((0,), (0,)))

def late_places(rep, reps):
    later = (rep + reps - 1) // reps
    return later * (reps - 2), (1 - later) * (reps - 2)

def sums_kernel(nb, more, x_hbm, c_hbm, g_ref, wg_hbm, wu_hbm, wd_hbm, *rest):
    if len(x_hbm.shape) == 4:
        _, left = late_places(lax.axis_index("rep"), lax.axis_size("rep"))
        x_hbm, c_hbm = x_hbm.at[left], c_hbm.at[left]
    starts, (og_hbm, ou_hbm, od_hbm, *scratch) = rest[:3 * more], rest[3 * more:]
    sums_body(nb, starts, x_hbm, c_hbm, g_ref, wg_hbm, wu_hbm, wd_hbm, og_hbm, ou_hbm, od_hbm, *scratch)

def sums_body(nb, starts, x_hbm, c_hbm, g_ref, wg_hbm, wu_hbm, wd_hbm, og_hbm, ou_hbm, od_hbm,
                xbuf, cbuf, wg, wu, wd, ag, au, ad, xg_ref, cg_ref, sg_ref, sem, wsem, asem):
    local = wg.shape[0]
    blocks = x_hbm.shape[0]
    chunks = blocks // nb
    first = lax.axis_index("shard") * local
    def fetch(i, slot):
        return (pltpu.make_async_copy(x_hbm.at[pl.ds(i * nb, nb)], xbuf.at[slot], sem.at[0, slot]),
                pltpu.make_async_copy(c_hbm.at[pl.ds(i * nb, nb)], cbuf.at[slot], sem.at[1, slot]))
    for cp in fetch(0, 0):
        cp.start()
    weights = [pltpu.make_async_copy(a, b, wsem.at[i]) for i, (a, b) in enumerate(((wg_hbm, wg), (wu_hbm, wu), (wd_hbm, wd)))]
    for cp in weights:
        cp.start()
    loads = [
        pltpu.make_async_copy(a.at[l], b.at[l], asem.at[i, l])
        for l in range(local) for i, (a, b) in enumerate(zip(starts, (ag, au, ad)))
    ]
    for cp in loads:
        cp.start()
    if not starts:
        ag[...] = jnp.zeros_like(ag)
        au[...] = jnp.zeros_like(au)
        ad[...] = jnp.zeros_like(ad)
    for cp in weights:
        cp.wait()

    def chunk(i, carry):
        slot = lax.rem(i, 2)
        @pl.when(i + 1 < chunks)
        def _():
            for cp in fetch(i + 1, 1 - slot):
                cp.start()
        for cp in fetch(i, slot):
            cp.wait()
        def block(b, carry):
            gather_block(xbuf[slot, b], cbuf[slot, b], g_ref[i * nb + b], first, local, xg_ref, cg_ref, sg_ref,
                         pl.multiple_of(b * CAP, CAP))
            return carry
        lax.fori_loop(0, nb, block, 0)
        def expert(l, carry):
            if starts:
                @pl.when(i == 0)
                def _():
                    for k, (a, b) in enumerate(zip(starts, (ag, au, ad))):
                        pltpu.make_async_copy(a.at[l], b.at[l], asem.at[k, l]).wait()
            add_expert(l, xg_ref, cg_ref, sg_ref, wg, wu, wd, ag, au, ad)

            @pl.when(i == chunks - 1)
            def _():
                for k, (a, b) in enumerate(((ag, og_hbm), (au, ou_hbm), (ad, od_hbm))):
                    pltpu.make_async_copy(a.at[l], b.at[l], asem.at[k, l]).start()
            return carry
        lax.fori_loop(0, local, expert, 0)
        return carry
    lax.fori_loop(0, chunks, chunk, 0)
    for l in range(local):
        for k, (a, b) in enumerate(((ag, og_hbm), (au, ou_hbm), (ad, od_hbm))):
            pltpu.make_async_copy(a.at[l], b.at[l], asem.at[k, l]).wait()

def moe_sums(x, c, gates, wg, wu, wd, starts=(), nb=4):
    blocks, tokens, width = x.shape[-3:]
    local, _, hidden = wg.shape
    any_ = pl.BlockSpec(memory_space=pl.ANY)
    rows = nb * CAP
    return pl.pallas_call(
        functools.partial(sums_kernel, nb, bool(starts)),
        out_shape=[jax.ShapeDtypeStruct(w.shape, f32) for w in (wg, wu, wd)],
        in_specs=[any_, any_, pl.BlockSpec(memory_space=pltpu.VMEM), any_, any_, any_] + [any_] * len(starts),
        out_specs=[any_] * 3,
        scratch_shapes=[
            pltpu.VMEM((2, nb, tokens, width), bf16), pltpu.VMEM((2, nb, tokens, width), bf16),
            pltpu.VMEM(wg.shape, bf16), pltpu.VMEM(wu.shape, bf16), pltpu.VMEM(wd.shape, bf16),
            pltpu.VMEM(wg.shape, f32), pltpu.VMEM(wu.shape, f32), pltpu.VMEM(wd.shape, f32),
            pltpu.VMEM((local, rows, width), bf16), pltpu.VMEM((local, rows, width), bf16), pltpu.VMEM((local, rows, 1), f32),
            pltpu.SemaphoreType.DMA((2, 2)), pltpu.SemaphoreType.DMA((3,)), pltpu.SemaphoreType.DMA((3, local)),
        ],
        compiler_params=pltpu.CompilerParams(vmem_limit_bytes=60 << 20),
        cost_estimate=pl.CostEstimate(
            flops=12 * blocks * local * CAP * width * hidden, transcendentals=blocks * local * CAP * hidden,
            bytes_accessed=4 * blocks * tokens * width + 24 * wg.size,
        ),
        name="expert_sums",
    )(x, c, gates, wg, wu, wd, *starts)


def norm_scale(rows):
    return lax.rsqrt(jnp.mean(rows * rows, axis=-1, keepdims=True) + epsilon)

def flip(index, bit):
    return index + bit - 2 * bit * ((index // bit) % 2)

def turned(index, core, step, bits):
    return (1 - core) * flip(index, bits[step]) + core * flip(index, bits[-1 - step])

def greet(spread):
    rep, me = lax.axis_index("rep"), lax.axis_index("shard")
    shards, reps = lax.axis_size("shard"), lax.axis_size("rep")
    peers = [(rep, (me + j) % shards) for j in range(1, shards)]
    if spread:
        peers += [((rep + j) % reps, me) for j in range(1, reps)]
    barrier = pltpu.get_barrier_semaphore()
    for peer in peers:
        pl.semaphore_signal(barrier, inc=1, device_id=peer, device_id_type=MESH)
    pl.semaphore_wait(barrier, len(peers))


class PlaneGather:
    def __init__(self, buf, own, send, recv, base=0):
        self.buf, self.own, self.send, self.recv, self.base = buf, own, send, recv, base
        self.rep, self.me = lax.axis_index("rep"), lax.axis_index("shard")
        self.core = self.me % 2
        shards = lax.axis_size("shard")
        self.bits = [1 << i for i in range(1, shards.bit_length() - 1)]
        self.steps = len(self.bits)

    @staticmethod
    def copies(shards):
        return (shards // 2 - 1) + shards // 2

    def owner(self, of, subset):
        for step in range(self.steps):
            if subset >> step & 1:
                of = turned(of, self.core, step, self.bits)
        return of

    def copy(self, number, subset, target):
        owner = self.owner(self.me, subset)
        return pltpu.make_async_remote_copy(
            src_ref=self.buf.at[owner] if subset else self.own, dst_ref=self.buf.at[owner],
            send_sem=self.send.at[self.base + number], recv_sem=self.recv.at[self.base + number],
            device_id=(self.rep, target), device_id_type=MESH,
        )

    def chip_copy(self, step, subset):
        return self.copy((1 << step) - 1 + subset, subset, turned(self.me, self.core, step, self.bits))

    def core_copy(self, subset):
        return self.copy((1 << self.steps) - 1 + subset, subset, flip(self.me, 1))

    def start(self):
        for step in range(self.steps):
            self.chip_copy(step, 0).start()
        self.core_copy(0).start()

    def forward(self, step):
        for subset in range(1 << step):
            self.chip_copy(step, subset).wait_recv()
            whole = subset + (1 << step)
            for later in range(step + 1, self.steps):
                self.chip_copy(later, whole).start()
            self.core_copy(whole).start()

    def finish(self):
        for subset in range(1 << self.steps):
            self.core_copy(subset).wait_recv()
        self.sent()

    def sent(self):
        for step in range(self.steps):
            for subset in range(1 << step):
                self.chip_copy(step, subset).wait_send()
        for subset in range(1 << self.steps):
            self.core_copy(subset).wait_send()

class RepSends:
    def __init__(self, buf, own, send, recv, neighbours):
        rep, me, reps = lax.axis_index("rep"), lax.axis_index("shard"), lax.axis_size("rep")
        self.rep, self.reps, self.neighbours = rep, reps, neighbours
        self.copies = [
            pltpu.make_async_remote_copy(
                src_ref=own, dst_ref=buf.at[rep], send_sem=send.at[j - 1], recv_sem=recv.at[j - 1],
                device_id=((rep + j) % reps, me), device_id_type=MESH,
            )
            for j in range(1, reps)
        ]

    def each(self, sent, act):
        for j, copy in enumerate(self.copies, 1):
            if self.neighbours or j not in (1, self.reps - 1):
                act(copy)
            else:
                end = self.reps - 1 if (j == 1) == sent else 0

                @pl.when(self.rep == end)
                def _(copy=copy):
                    act(copy)

    def start(self):
        self.each(True, lambda copy: copy.start())

    def finish(self):
        self.each(True, lambda copy: copy.wait_send())
        self.each(False, lambda copy: copy.wait_recv())


def on_ends(low, high):
    pl.when(lax.axis_index("rep") == 0)(low)
    pl.when(lax.axis_index("rep") == lax.axis_size("rep") - 1)(high)


class Spread:
    def __init__(self, oth, col, own, send, recv, psend, precv, asend, arecv, lsem):
        self.oth, self.col, self.own, self.send, self.recv = oth, col, own, send, recv
        self.psend, self.precv, self.asend, self.arecv, self.lsem = psend, precv, asend, arecv, lsem
        self.rep, self.me, self.reps = lax.axis_index("rep"), lax.axis_index("shard"), lax.axis_size("rep")
        self.core = self.me % 2
        self.blocks = range(lax.axis_size("shard") // 2)

    @staticmethod
    def semaphores(shards, reps):
        n = PlaneGather.copies(shards)
        dma = lambda *k: pltpu.SemaphoreType.DMA(k)
        return [dma(reps - 1, n), dma(reps - 1, n), *[dma(2, shards // 2)] * 4, dma(reps - 1)]

    def gather(self, j):
        return PlaneGather(self.oth.at[j - 1], self.col.at[(self.rep + j) % self.reps], self.send.at[j - 1], self.recv.at[j - 1])

    def own_copy(self, j):
        return pltpu.make_async_copy(self.col.at[(self.rep + j) % self.reps], self.oth.at[j - 1, self.me], self.lsem.at[j - 1])

    def begin(self, j):
        self.gather(j).start()
        self.own_copy(j).start()

    def forward(self, j):
        self.gather(j).forward(0)

    def end(self, j):
        gather = self.gather(j)
        for step in range(1, gather.steps):
            gather.forward(step)
        gather.finish()
        self.own_copy(j).wait()

    def straight(self, up, b):
        at, way = 2 * b + self.core, self.reps - 2 if up else 0
        return pltpu.make_async_remote_copy(
            src_ref=self.own.at[at], dst_ref=self.oth.at[way, at], send_sem=self.psend.at[up, b], recv_sem=self.precv.at[up, b],
            device_id=((self.rep + (1 if up else self.reps - 1)) % self.reps, self.me), device_id_type=MESH,
        )

    def across(self, up, b):
        at, way = 2 * b + self.core, self.reps - 2 if up else 0
        return pltpu.make_async_remote_copy(
            src_ref=self.oth.at[way, at], dst_ref=self.oth.at[way, at], send_sem=self.asend.at[up, b], recv_sem=self.arecv.at[up, b],
            device_id=(self.rep, flip(self.me, 1)), device_id_type=MESH,
        )

    def sends(self, up):
        return self.rep < self.reps - 1 if up else self.rep > 0

    def gets(self, up):
        return self.rep > 0 if up else self.rep < self.reps - 1

    def start_straight(self):
        for up in (0, 1):
            @pl.when(self.sends(up))
            def _(up=up):
                for b in self.blocks:
                    self.straight(up, b).start()

    def sent_straight(self):
        for up in (0, 1):
            @pl.when(self.sends(up))
            def _(up=up):
                for b in self.blocks:
                    self.straight(up, b).wait_send()

    def got_straight(self, up):
        @pl.when(self.gets(up))
        def _():
            for b in self.blocks:
                self.straight(up, b).wait_recv()

    def start_across(self, up):
        @pl.when(self.gets(up))
        def _():
            for b in self.blocks:
                self.across(up, b).start()

    def end_across(self, up):
        @pl.when(self.gets(up))
        def _():
            for b in self.blocks:
                self.across(up, b).wait()


def rotate(v, cosine, sine, sign):
    lane = lax.broadcasted_iota(jnp.int32, v.shape, 1) % HEAD_SIZE
    half = HEAD_SIZE // 2
    low = lane < half
    other = jnp.where(low, -pltpu.roll(v, LANES - half, 1), pltpu.roll(v, half, 1))
    return v * cosine + sign * other * sine

def two_heads(v):
    low = lax.broadcasted_iota(jnp.int32, v.shape, 1) < HEAD_SIZE
    zero = jnp.zeros_like(v)
    return jnp.concatenate([jnp.where(low, v, zero), jnp.where(low, zero, v)], axis=0)

def one_head_twice(pair, odd):
    high = lax.broadcasted_iota(jnp.int32, pair.shape, 1) // HEAD_SIZE
    wide = pair.astype(f32)
    return jnp.where(high == odd, wide, pltpu.roll(wide, HEAD_SIZE, 1)).astype(pair.dtype)

def probabilities(query2, keys, prefix_len):
    rows = query2.shape[0] // 2
    raw = dot(query2, keys, ((1,), (1,)))
    row = lax.broadcasted_iota(jnp.int32, raw.shape, 0) % rows
    col = lax.broadcasted_iota(jnp.int32, raw.shape, 1)
    scores = jnp.where((col <= row) | (col < prefix_len), raw * score_scale, masked_value)
    weights = jnp.exp(scores - jnp.max(scores, axis=-1, keepdims=True))
    return weights / jnp.sum(weights, axis=-1, keepdims=True)

def lanes(j, count=1):
    return pl.ds(pl.multiple_of(j * LANES * count, LANES), LANES * count)

def front_kernel(spread, prefix_ref, tok_ref, routes_ref, cos_ref, sin_ref, wq_hbm, wk_hbm, wv_hbm, wo_hbm, ws_hbm, cot_ref,
                 wall_out, cown_out, ccol_out, q_out, k_out, v_out, att_out, hid_out, x_out, gates_out, n1_out,
                 wbuf, qkv_ref, send, recv, csend, crecv, zsend, zrecv, lsem, osem):
    count, width = tok_ref.shape
    kv_width = k_out.shape[1]
    experts = gates_out.shape[0]
    shards, depth, total = wbuf.shape
    me = lax.axis_index("shard")
    own, at = [], 0
    for i, part in enumerate((wq_hbm, wk_hbm, wv_hbm, wo_hbm, ws_hbm)):
        own.append(pltpu.make_async_copy(part, wbuf.at[me, :, at:at + part.shape[1]], osem.at[i]))
        own[-1].start()
        at += part.shape[1]
    greet(spread)
    gather = PlaneGather(wbuf, wbuf.at[me], send, recv)
    for copy in own:
        copy.wait()
    gather.start()
    far = RepSends(ccol_out, cot_ref, zsend, zrecv, False)
    if spread:
        far.start()
    near = PlaneGather(cown_out, cot_ref, csend, crecv)
    own_cot = pltpu.make_async_copy(cot_ref, cown_out.at[me], lsem.at[2])
    own_cot.start()
    inputs = tok_ref[...].astype(f32)
    scaled = inputs * norm_scale(inputs)
    for step in range(gather.steps):
        gather.forward(step)
    near.start()
    gather.finish()
    keep = pltpu.make_async_copy(wbuf, wall_out, lsem.at[1])
    keep.start()
    cut = [0, width, width + kv_width, width + 2 * kv_width, 2 * width + 2 * kv_width]
    small = wbuf[:, :, cut[4]:].reshape(shards * depth, total - cut[4])
    wide = small.astype(f32).T
    gain_one, gain_two = wide[experts:experts + 1], wide[experts + 1:experts + 2]
    n1_out[...] = (scaled * gain_one).astype(bf16)

    def project(j, carry):
        w = wbuf[:, :, lanes(j, 2)].reshape(shards * depth, 2 * LANES)
        qkv_ref[:, lanes(j, 2)] = dot(n1_out[...], w)
        return carry
    lax.fori_loop(0, cut[3] // (2 * LANES), project, 0)
    cosine, sine = cos_ref[...], sin_ref[...]
    for j in range(width // LANES):
        q_out[:, j * LANES:(j + 1) * LANES] = rotate(qkv_ref[:, j * LANES:(j + 1) * LANES], cosine, sine, 1.0).astype(bf16)
    for j in range(kv_width // LANES):
        at = slice(cut[1] + j * LANES, cut[1] + (j + 1) * LANES)
        k_out[:, j * LANES:(j + 1) * LANES] = rotate(qkv_ref[:, at], cosine, sine, 1.0).astype(bf16)
    v_out[...] = qkv_ref[:, cut[2]:cut[3]].astype(bf16)
    prefix_len = prefix_ref[0]


    def head(j, carry):
        keys = one_head_twice(k_out[:, lanes(j // 2)], j % 2)
        values = one_head_twice(v_out[:, lanes(j // 2)], j % 2)
        prob = probabilities(two_heads(q_out[:, lanes(j)]), keys, prefix_len)
        both = dot(prob.astype(bf16), values)
        low = lax.broadcasted_iota(jnp.int32, (count, LANES), 1) < HEAD_SIZE
        att_out[:, lanes(j)] = jnp.where(low, both[:count], both[count:]).astype(bf16)

        @pl.when(j == 2)
        def _():
            near.forward(0)
        return carry
    lax.fori_loop(0, KEY_VALUE_HEADS, head, 0)
    for step in range(1, near.steps):
        near.forward(step)

    def project_out(j, carry):
        w = wbuf[:, :, pl.ds(pl.multiple_of(cut[3] + j * 2 * LANES, LANES), 2 * LANES)].reshape(shards * depth, 2 * LANES)
        qkv_ref[:, lanes(j, 2)] = dot(att_out[...], w)
        return carry
    lax.fori_loop(0, width // (2 * LANES), project_out, 0)
    hidden = inputs + branch_scale * qkv_ref[:, :width]
    hid_out[...] = hidden
    x = (hidden * norm_scale(hidden) * gain_two).astype(bf16)
    x_out[...] = x
    logits = dot(x, small).T[:experts]
    expert = lax.broadcasted_iota(jnp.int32, (experts, count), 0)
    named = expert < 0
    for k in range(routes_ref.shape[0]):
        named = named | (routes_ref[k:k + 1, :] == expert)
    top = jnp.max(jnp.where(named, logits, masked_value), axis=0, keepdims=True)
    weights = jnp.where(named, jnp.exp(jnp.where(named, logits - top, 0.0)), 0.0)
    gates_out[...] = weights / jnp.sum(weights, axis=0, keepdims=True)
    keep.wait()
    near.finish()
    own_cot.wait()
    if spread:
        far.finish()

def front(tokens, prefix, routes, mine, cot, cosine, sine, experts, kv_width, spread):
    count, width = tokens.shape
    shards, reps = lax.axis_size("shard"), lax.axis_size("rep")
    depth, total = tokens.shape[1] // shards, sum(part.shape[1] for part in mine)
    v = pl.BlockSpec(memory_space=pltpu.VMEM)
    any_ = pl.BlockSpec(memory_space=pl.ANY)
    sds = jax.ShapeDtypeStruct
    n = PlaneGather.copies(shards)
    return pl.pallas_call(
        functools.partial(front_kernel, spread),
        out_shape=[
            sds((shards, depth, total), bf16), sds((shards, count, width), bf16), sds((reps, count, width), bf16), sds((count, width), bf16), sds((count, kv_width), bf16), sds((count, kv_width), bf16),
            sds((count, width), bf16), sds((count, width), f32), sds((count, width), bf16), sds((experts, count), f32), sds((count, width), bf16),
        ],
        in_specs=[pl.BlockSpec(memory_space=pltpu.SMEM), v, v, v, v] + [any_] * 6,
        out_specs=[any_] * 3 + [v] * 8,
        scratch_shapes=[
            pltpu.VMEM((shards, depth, total), bf16), pltpu.VMEM((count, width + 2 * kv_width), f32),
            *[pltpu.SemaphoreType.DMA((k,)) for k in (n, n, n, n, reps, reps, 3, 5)],
        ],
        compiler_params=pltpu.CompilerParams(vmem_limit_bytes=60 << 20, has_side_effects=True, collective_id=1),
        name="front",
    )(prefix, tokens, routes, cosine, sine, *mine, cot)

class PlaneReduce:
    def __init__(self, mine, theirs, from_core, from_chip, csend, crecv, send, recv):
        self.mine, self.theirs, self.from_core, self.from_chip = mine, theirs, from_core, from_chip
        self.csend, self.crecv, self.send, self.recv = csend, crecv, send, recv
        self.rep, self.me = lax.axis_index("rep"), lax.axis_index("shard")
        self.core = self.me % 2
        self.bits = [1 << i for i in range(1, lax.axis_size("shard").bit_length() - 1)]
        self.steps = len(self.bits)

    def owner(self, core, u):
        at = flip(self.me, 1) if core else self.me
        of = (1 - self.core) if core else self.core
        for step in range(self.steps):
            if u >> step & 1:
                at = turned(at, of, step, self.bits)
        return at

    def core_copy(self, u):
        return pltpu.make_async_remote_copy(
            src_ref=self.theirs.at[u], dst_ref=self.from_core.at[u], send_sem=self.csend.at[u], recv_sem=self.crecv.at[u],
            device_id=(self.rep, flip(self.me, 1)), device_id_type=MESH,
        )

    def slot(self, step, u):
        return (1 << self.steps) - (1 << (self.steps - step)) + (u >> (step + 1))

    def chip_copy(self, step, u):
        slot = self.slot(step, u)
        return pltpu.make_async_remote_copy(
            src_ref=self.mine.at[u], dst_ref=self.from_chip.at[slot], send_sem=self.send.at[slot], recv_sem=self.recv.at[slot],
            device_id=(self.rep, turned(self.me, self.core, step, self.bits)), device_id_type=MESH,
        )

    def total(self, u, before, rows):
        whole = self.mine[u, rows].astype(f32) + self.from_core[u, rows].astype(f32)
        for step in range(before):
            whole = whole + self.from_chip[self.slot(step, u), rows].astype(f32)
        return whole

    def send_on(self, step, u):
        self.core_copy(u).wait_recv()
        count = self.mine.shape[1]
        piece = 32

        def add(i, carry):
            rows = pl.ds(pl.multiple_of(i * piece, piece), piece)
            self.mine[u, rows] = self.total(u, step, rows).astype(bf16)
            return carry
        lax.fori_loop(0, count // piece, add, 0)
        self.chip_copy(step, u).start()

    def group(self, step):
        return [u for u in range(1 << self.steps) if u % (2 << step) == 1 << step]

    def arrive(self, step):
        for u in self.group(step):
            self.chip_copy(step, u).wait_recv()

    def advance(self, step):
        if step < self.steps:
            if step:
                self.arrive(step - 1)
            for u in self.group(step):
                self.send_on(step, u)

    def last(self, out, plus=None):
        self.arrive(self.steps - 1)
        self.core_copy(0).wait_recv()
        count = self.mine.shape[1]
        piece = 32

        def add(i, carry):
            rows = pl.ds(pl.multiple_of(i * piece, piece), piece)
            whole = self.total(0, self.steps, rows)
            out[rows] = (whole if plus is None else whole + plus[rows]).astype(out.dtype)
            return carry
        lax.fori_loop(0, count // piece, add, 0)

    def finish(self):
        for u in range(1 << self.steps):
            self.core_copy(u).wait_send()
        for step in range(self.steps):
            for u in self.group(step):
                self.chip_copy(step, u).wait_send()


def own_kernel(spread, nb, x_ref, gates_ref, c_hbm, ccol_hbm, wg_hbm, wu_hbm, wd_hbm,
               xown_out, xcol_out, gown_out, gcol_out, back_out, dg_out, mix_out, coth_out,
               wg, wu, wd, xb, cb, xg_ref, cg_ref, sg_ref, y_ref, ds_ref, mine, theirs, mix, from_core, from_chip,
               gown, gcol, dgs, dgr,
               xs, xr, zxs, zxr, zgs, zgr, gs, gr, dss, dsr, css, csr, hs, hr, wsem, bsem, lsem, msem, *csems):
    count, width = x_ref.shape
    local, _, hidden = wg.shape
    rep, me = lax.axis_index("rep"), lax.axis_index("shard")
    shards = lax.axis_size("shard")
    first = me * local
    greet(spread)
    near = PlaneGather(xown_out, x_ref, xs, xr)
    near.start()
    gown[me] = gates_ref[...]

    def peer(j):
        return (rep, (me + j) % shards)

    gate_sends = [
        pltpu.make_async_remote_copy(
            src_ref=gates_ref, dst_ref=gown.at[me], send_sem=gs.at[j - 1], recv_sem=gr.at[j - 1],
            device_id=peer(j), device_id_type=MESH,
        )
        for j in range(1, shards)
    ]
    for copy in gate_sends:
        copy.start()
    far = [RepSends(xcol_out, x_ref, zxs, zxr, False), RepSends(gcol, gates_ref, zgs, zgr, True)] if spread else []
    for sends in far:
        sends.start()
    cots = Spread(coth_out, ccol_hbm, c_hbm, *csems)
    reps = lax.axis_size("rep")
    if spread:
        cots.start_straight()
    own_x = pltpu.make_async_copy(x_ref, xown_out.at[me], lsem)
    own_x.start()
    weights = [pltpu.make_async_copy(a, b, wsem.at[i]) for i, (a, b) in enumerate(((wg_hbm, wg), (wu_hbm, wu), (wd_hbm, wd)))]
    for copy in weights:
        copy.start()
    reduce = PlaneReduce(mine, theirs, from_core, from_chip, css, csr, hs, hr)
    for copy in gate_sends:
        copy.wait_recv()
    order = list(range(1 << reduce.steps))
    half = nb // 2
    dg_sends, mixes = [], []

    def fetch(at, slot):
        return (pltpu.make_async_copy(xown_out.at[at], xb.at[slot], bsem.at[0, slot]),
                pltpu.make_async_copy(c_hbm.at[at], cb.at[slot], bsem.at[1, slot]))

    chunks = [order[q:q + half] for q in range(0, len(order), half)]
    forwarded = 0
    for q, chunk in enumerate(chunks):
        plan = [(core, u) for u in chunk for core in (0, 1)]
        owners = [reduce.owner(core, u) for core, u in plan]
        while forwarded < chunk[-1].bit_length():
            near.forward(forwarded)
            forwarded += 1
        if not q:
            own_x.wait()
        for u in chunk:
            near.core_copy(u).wait_recv()
        for copy in fetch(owners[0], 0):
            copy.start()
        for b in range(nb):
            if b + 1 < nb:
                for copy in fetch(owners[b + 1], (b + 1) % 2):
                    copy.start()
            for copy in fetch(owners[b], b % 2):
                copy.wait()
            gather_block(xb[b % 2], cb[b % 2], gown[owners[b]], first, local, xg_ref, cg_ref, sg_ref, b * CAP)
        if not q:
            for copy in weights:
                copy.wait()

        def expert(l, carry):
            inner, raw, d_gate, d_up, scaled = expert_parts(xg_ref[l], cg_ref[l], sg_ref[l], wg[l], wu[l], wd[l])
            ds_ref[l] = branch_scale * jnp.sum(inner * raw, axis=1, keepdims=True)
            rows = pl.ds(pl.multiple_of(l * CAP, CAP), CAP)
            out = dot(scaled, wd[l]).astype(bf16)
            d_in = (dot(d_gate, wg[l], ((1,), (1,))) + dot(d_up, wu[l], ((1,), (1,)))).astype(bf16)
            for b in range(nb):
                y_ref[b, rows, :width] = out[b * CAP:(b + 1) * CAP]
                y_ref[b, rows, width:] = d_in[b * CAP:(b + 1) * CAP]
            return carry
        lax.fori_loop(0, local, expert, 0)
        if q + 1 < len(chunks):
            while forwarded < chunks[q + 1][-1].bit_length():
                near.forward(forwarded)
                forwarded += 1
        if spread:
            if not q:
                cots.begin(2)
            else:
                cots.forward(2)
        for b in range(nb):
            core, u = plan[b]
            parts = slot_one_hot(slot_ranks(gown[owners[b]]), first, local)
            table = jnp.concatenate(parts, axis=0).astype(bf16)
            both = dot(table, y_ref[b], ((0,), (0,))).astype(bf16)
            mix[core, u] = both[:, :width]
            mixes.append(pltpu.make_async_copy(mix.at[core, u], mix_out.at[owners[b]], msem.at[core, u]))
            mixes[-1].start()
            (theirs if core else mine)[u] = both[:, width:]
            if core:
                reduce.core_copy(u).start()
            dgs[owners[b]] = jnp.concatenate(
                [jnp.sum(parts[l] * ds_ref[l, b * CAP:(b + 1) * CAP], axis=0, keepdims=True) for l in range(local)], axis=0
            )
        for u in chunk:
            if u % 2:
                reduce.send_on(0, u)
    for j in range(1, shards):
        copy = pltpu.make_async_remote_copy(
            src_ref=dgs.at[(me + j) % shards], dst_ref=dgr.at[me], send_sem=dss.at[j - 1], recv_sem=dsr.at[j - 1],
            device_id=peer(j), device_id_type=MESH,
        )
        copy.start()
        dg_sends.append(copy)
    dgr[me] = dgs[me]
    gown_out[...] = gown[...]
    for step in range(1, reduce.steps):
        reduce.advance(step)
    reduce.last(back_out)
    for copy in dg_sends:
        copy.wait()
    dg_out[...] = dgr[...]
    if spread:
        cots.end(2)
        cots.got_straight(0)
        cots.got_straight(1)
        cots.sent_straight()
    reduce.finish()
    for copy in mixes:
        copy.wait()
    near.sent()
    for copy in gate_sends:
        copy.wait_send()
    for sends in far:
        sends.finish()
    if spread:
        gcol_out[...] = gcol[...]


def moe_own(x, gates, c, ccol, wg, wu, wd, spread, nb=4):
    count, width = x.shape
    local, _, hidden = wg.shape
    shards, reps = lax.axis_size("shard"), lax.axis_size("rep")
    experts = local * shards
    v = pl.BlockSpec(memory_space=pltpu.VMEM)
    any_ = pl.BlockSpec(memory_space=pl.ANY)
    sds = jax.ShapeDtypeStruct
    n = PlaneGather.copies(shards)
    rows = nb * CAP
    half = shards // 2
    dma = lambda *k: pltpu.SemaphoreType.DMA(k)
    return pl.pallas_call(
        functools.partial(own_kernel, spread, nb),
        out_shape=[
            sds((shards, count, width), bf16), sds((reps, count, width), bf16), sds((shards, experts, count), f32),
            sds((reps, experts, count), f32), sds((count, width), f32), sds((shards, local, count), f32),
            sds((shards, count, width), bf16), sds((max(reps - 1, 1), shards, count, width) if spread else (1, 1, 16, LANES), bf16),
        ],
        in_specs=[v, v, any_, any_, any_, any_, any_],
        out_specs=[any_, any_, v, v, v, v, any_, any_],
        scratch_shapes=[
            pltpu.VMEM(wg.shape, bf16), pltpu.VMEM(wu.shape, bf16), pltpu.VMEM(wd.shape, bf16),
            pltpu.VMEM((2, count, width), bf16), pltpu.VMEM((2, count, width), bf16),
            pltpu.VMEM((local, rows, width), bf16), pltpu.VMEM((local, rows, width), bf16), pltpu.VMEM((local, rows, 1), f32),
            pltpu.VMEM((nb, local * CAP, 2 * width), bf16), pltpu.VMEM((local, rows, 1), f32),
            *[pltpu.VMEM((k, count, width), bf16) for k in (half, half)], pltpu.VMEM((2, half, count, width), bf16),
            *[pltpu.VMEM((k, count, width), bf16) for k in (half, half - 1)],
            pltpu.VMEM((shards, experts, count), f32), pltpu.VMEM((reps, experts, count), f32),
            pltpu.VMEM((shards, local, count), f32), pltpu.VMEM((shards, local, count), f32),
            dma(n), dma(n), dma(reps), dma(reps), dma(reps), dma(reps), dma(shards), dma(shards), dma(shards), dma(shards),
            dma(half), dma(half), dma(half), dma(half), dma(3), dma(2, 2), pltpu.SemaphoreType.DMA, dma(2, half),
            *Spread.semaphores(shards, reps),
        ],
        compiler_params=pltpu.CompilerParams(vmem_limit_bytes=60 << 20, has_side_effects=True, collective_id=2),
        name="own_experts",
    )(x, gates, c, ccol, wg, wu, wd)

def norm_backward(rows, scaling, gain, upstream):
    weighted = upstream * gain
    inner_mean = jnp.mean(weighted * rows, axis=-1, keepdims=True)
    gradient = scaling * weighted - rows * (scaling * scaling * scaling) * inner_mean
    return gradient, jnp.sum(upstream * rows * scaling, axis=0, keepdims=True)


def back_kernel(prefix_ref, tok_ref, cot_ref, cos_ref, sin_ref, w_ref, q_ref, k_ref, v_ref, att_ref, n1_ref, x_ref,
                hid_ref, gates_ref, dg_ref, back_ref, dtok_out, shares_out, dqkv_ref, datt_ref, dproj_ref):
    count, width = tok_ref.shape
    kv_width = k_ref.shape[1]
    experts = gates_ref.shape[0]
    shards, depth, total = w_ref.shape
    rows = shards * depth
    cut = [0, width, width + kv_width, width + 2 * kv_width, 2 * width + 2 * kv_width]
    small = w_ref[:, :, cut[4]:].reshape(rows, total - cut[4])
    wide = small.astype(f32).T
    gain_one, gain_two = wide[experts:experts + 1], wide[experts + 1:experts + 2]
    hidden = hid_ref[...]
    gates, d_gates = gates_ref[...], dg_ref[...]
    d_logits = gates * (d_gates - jnp.sum(gates * d_gates, axis=0, keepdims=True))
    none = jnp.zeros((LANES - experts, count), f32)
    d_logits = jnp.concatenate([d_logits, none], axis=0).T.astype(bf16)
    d_normed_two = back_ref[...] + dot(d_logits, small, ((1,), (1,)))
    d_hidden, d_gain_two = norm_backward(hidden, norm_scale(hidden), gain_two, d_normed_two)
    d_hidden = d_hidden + cot_ref[...].astype(f32)
    dtok_out[...] = d_hidden
    dproj_ref[...] = (branch_scale * d_hidden).astype(bf16)
    tile = 2 * LANES

    def out_tile(j, carry):
        grad = dot(att_ref[...], dproj_ref[:, lanes(j, 2)], ((0,), (0,))).astype(bf16)
        at = pl.ds(pl.multiple_of(cut[3] + j * tile, LANES), tile)
        shares_out[:, :, at] = grad.reshape(shards, depth, tile)
        return carry
    lax.fori_loop(0, width // tile, out_tile, 0)
    datt_ref[...] = dot(dproj_ref[...], w_ref[:, :, cut[3]:cut[4]].reshape(rows, width), ((1,), (1,))).astype(bf16)
    cosine, sine = cos_ref[...], sin_ref[...]
    prefix_len = prefix_ref[0]
    low = lax.broadcasted_iota(jnp.int32, (count, LANES), 1) < HEAD_SIZE

    def pair(p, carry):
        at_k = pl.ds(pl.multiple_of(cut[1] + p * LANES, LANES), LANES)
        at_v = pl.ds(pl.multiple_of(cut[2] + p * LANES, LANES), LANES)
        d_keys, d_values = [], []
        for odd in range(2):
            j = 2 * p + odd
            keys = one_head_twice(k_ref[:, lanes(p)], odd)
            values = one_head_twice(v_ref[:, lanes(p)], odd)
            query2, d_att2 = two_heads(q_ref[:, lanes(j)]), two_heads(datt_ref[:, lanes(j)])
            prob = probabilities(query2, keys, prefix_len)
            d_value = dot(prob.astype(bf16), d_att2, ((0,), (0,)))
            d_prob = dot(d_att2, values, ((1,), (1,)))
            weighted = jnp.sum(prob * d_prob, axis=-1, keepdims=True)
            d_score = (prob * (d_prob - weighted) * score_scale).astype(bf16)
            d_query = dot(d_score, keys)
            d_query = jnp.where(low, d_query[:count], d_query[count:])
            dqkv_ref[:, lanes(j)] = rotate(d_query, cosine, sine, -1.0).astype(bf16)
            d_key = dot(d_score, query2, ((0,), (0,)))
            d_keys.append(d_key + pltpu.roll(d_key, HEAD_SIZE, 1))
            d_values.append(d_value + pltpu.roll(d_value, HEAD_SIZE, 1))
        dqkv_ref[:, at_k] = rotate(jnp.where(low, *d_keys), cosine, sine, -1.0).astype(bf16)
        dqkv_ref[:, at_v] = jnp.where(low, *d_values).astype(bf16)
        return carry
    lax.fori_loop(0, KEY_VALUE_HEADS // 2, pair, 0)

    def in_tile(j, carry):
        grad = dot(n1_ref[...], dqkv_ref[:, lanes(j, 2)], ((0,), (0,))).astype(bf16)
        shares_out[:, :, lanes(j, 2)] = grad.reshape(shards, depth, tile)
        return carry
    lax.fori_loop(0, cut[3] // tile, in_tile, 0)
    d_normed_one = dot(dqkv_ref[...], w_ref[:, :, :cut[3]].reshape(rows, cut[3]), ((1,), (1,)))
    inputs = tok_ref[...].astype(f32)
    d_inputs, d_gain_one = norm_backward(inputs, norm_scale(inputs), gain_one, d_normed_one)
    dtok_out[...] += d_inputs
    row = lax.broadcasted_iota(jnp.int32, (LANES, rows), 0)
    gains = jnp.where(row == experts, d_gain_one, jnp.where(row == experts + 1, d_gain_two, 0.0)).T
    d_small = (dot(x_ref[...], d_logits, ((0,), (0,))) + gains).astype(bf16)
    shares_out[:, :, cut[4]:] = d_small.reshape(shards, depth, total - cut[4])


def attention_back(prefix, tokens, cot, cosine, sine, packed, query, keys, values, attended, n1, x, hidden, gates, d_gates, back):
    count, width = tokens.shape
    v = pl.BlockSpec(memory_space=pltpu.VMEM)
    sds = jax.ShapeDtypeStruct
    return pl.pallas_call(
        back_kernel,
        out_shape=[sds((count, width), f32), sds(packed.shape, bf16)],
        in_specs=[pl.BlockSpec(memory_space=pltpu.SMEM)] + [v] * 15,
        out_specs=[v] * 2,
        scratch_shapes=[
            pltpu.VMEM((count, width + 2 * keys.shape[1]), bf16), pltpu.VMEM((count, width), bf16), pltpu.VMEM((count, width), bf16),
        ],
        compiler_params=pltpu.CompilerParams(vmem_limit_bytes=60 << 20),
        name="attention_back",
    )(prefix, tokens, cot, cosine, sine, packed, query, keys, values, attended, n1, x, hidden, gates, d_gates, back)

def spread_kernel(nb, xown_hbm, cown_hbm, xcol_hbm, ccol_hbm, gown_ref, gcol_ref, wg_hbm, wu_hbm, wd_hbm, coth_in,
                  xoth_hbm, coth_hbm, og_hbm, ou_hbm, od_hbm, glast_ref,
                  xbuf, cbuf, wg, wu, wd, ag, au, ad, xg_ref, cg_ref, sg_ref, goth, send, recv, bsem, wsem, osem, *sems):
    xsems, csems = sems[:7], sems[7:]
    local = wg.shape[0]
    shards = gown_ref.shape[0]
    rep, me = lax.axis_index("rep"), lax.axis_index("shard")
    reps = lax.axis_size("rep")
    first = me * local
    chunks = shards // nb

    xs = Spread(xoth_hbm, xcol_hbm, xown_hbm, *xsems)
    cs = Spread(coth_hbm, ccol_hbm, cown_hbm, *csems)
    both = (xs, cs)

    def each(act, j):
        for one in both:
            act(one, j)

    def gate_gathers():
        return [PlaneGather(goth.at[j - 1], gcol_ref.at[(rep + j) % reps], send.at[j - 1], recv.at[j - 1]) for j in range(1, reps)]

    def fetch(x, c, q, slot):
        return (pltpu.make_async_copy(x.at[pl.ds(q * nb, nb)], xbuf.at[slot], bsem.at[0, slot]),
                pltpu.make_async_copy(c.at[pl.ds(q * nb, nb)], cbuf.at[slot], bsem.at[1, slot]))

    def out_copies(l):
        return [pltpu.make_async_copy(a.at[l], b.at[l], osem.at[i, l]) for i, (a, b) in enumerate(((ag, og_hbm), (au, ou_hbm), (ad, od_hbm)))]

    def replica(x, c, g, midway, last, final=False):
        for copy in fetch(x, c, 0, 0):
            copy.start()

        def chunk(q, carry):
            slot = lax.rem(q, 2)

            @pl.when(q + 1 < chunks)
            def _():
                for copy in fetch(x, c, q + 1, 1 - slot):
                    copy.start()
            for copy in fetch(x, c, q, slot):
                copy.wait()

            def block(b, carry):
                gather_block(xbuf[slot, b], cbuf[slot, b], g[q * nb + b], first, local, xg_ref, cg_ref, sg_ref,
                             pl.multiple_of(b * CAP, CAP))
                return carry
            lax.fori_loop(0, nb, block, 0)

            def expert(l, carry):
                add_expert(l, xg_ref, cg_ref, sg_ref, wg, wu, wd, ag, au, ad)

                @pl.when((q == chunks // 2) & (l == 0))
                def _():
                    midway()

                if final:
                    @pl.when(q == chunks - 1)
                    def _():
                        for copy in out_copies(l):
                            copy.start()
                return carry
            lax.fori_loop(0, local, expert, 0)
            return carry
        lax.fori_loop(0, chunks, chunk, 0)
        last()

    greet(True)
    xs.begin(2)
    for j in range(1, reps):
        goth[j - 1, me] = gcol_ref[(rep + j) % reps]
    for gather in gate_gathers():
        gather.start()
    xs.start_straight()
    for up in (0, 1):
        cs.start_across(up)
    weights = [pltpu.make_async_copy(a, b, wsem.at[i]) for i, (a, b) in enumerate(((wg_hbm, wg), (wu_hbm, wu), (wd_hbm, wd)))]
    for copy in weights:
        copy.start()
    ag[...] = jnp.zeros_like(ag)
    au[...] = jnp.zeros_like(au)
    ad[...] = jnp.zeros_like(ad)
    for copy in weights:
        copy.wait()

    def midway_own():
        xs.forward(2)
        for gather in gate_gathers():
            gather.forward(0)
        on_ends(lambda: each(Spread.begin, reps - 1), lambda: each(Spread.begin, 1))

    def last_own():
        xs.end(2)
        for gather in gate_gathers():
            for step in range(1, gather.steps):
                gather.forward(step)
        for gather in gate_gathers():
            gather.finish()
        for up in (0, 1):
            cs.end_across(up)

    def midway_two():
        on_ends(lambda: each(Spread.forward, reps - 1), lambda: each(Spread.forward, 1))
        xs.got_straight(1)
        xs.start_across(1)

        @pl.when(rep == 0)
        def _():
            xs.got_straight(0)
            xs.start_across(0)

    def last_two():
        xs.end_across(1)
        pl.when(rep == 0)(lambda: xs.end_across(0))

    def midway_three():
        @pl.when(rep > 0)
        def _():
            xs.got_straight(0)
            xs.start_across(0)

    def last_three():
        on_ends(lambda: each(Spread.end, reps - 1), lambda: each(Spread.end, 1))
        pl.when(rep > 0)(lambda: xs.end_across(0))

    replica(xown_hbm, cown_hbm, gown_ref, midway_own, last_own)
    replica(xoth_hbm.at[1], coth_hbm.at[1], goth.at[1], midway_two, last_two)
    third, left = late_places(rep, reps)
    replica(xoth_hbm.at[third], coth_hbm.at[third], goth.at[third], midway_three, last_three, True)
    xs.sent_straight()
    glast_ref[...] = goth[left]
    for l in range(local):
        for copy in out_copies(l):
            copy.wait()


def moe_spread_sums(xown, cown, xcol, ccol, coth, gown, gcol, wg, wu, wd, nb=4):
    shards, count, width = xown.shape
    reps = xcol.shape[0]
    local, _, hidden = wg.shape
    any_ = pl.BlockSpec(memory_space=pl.ANY)
    v = pl.BlockSpec(memory_space=pltpu.VMEM)
    rows = nb * CAP
    n = PlaneGather.copies(shards)
    slots = reps * shards * local * CAP
    outs = pl.pallas_call(
        functools.partial(spread_kernel, nb),
        out_shape=[jax.ShapeDtypeStruct((reps - 1, shards, count, width), bf16)] * 2
        + [jax.ShapeDtypeStruct(w.shape, f32) for w in (wg, wu, wd)] + [jax.ShapeDtypeStruct(gown.shape, f32)],
        in_specs=[any_, any_, any_, any_, v, v, any_, any_, any_, any_],
        input_output_aliases={9: 1},
        out_specs=[any_] * 5 + [v],
        scratch_shapes=[
            pltpu.VMEM((2, nb, count, width), bf16), pltpu.VMEM((2, nb, count, width), bf16),
            pltpu.VMEM(wg.shape, bf16), pltpu.VMEM(wu.shape, bf16), pltpu.VMEM(wd.shape, bf16),
            pltpu.VMEM(wg.shape, f32), pltpu.VMEM(wu.shape, f32), pltpu.VMEM(wd.shape, f32),
            pltpu.VMEM((local, rows, width), bf16), pltpu.VMEM((local, rows, width), bf16), pltpu.VMEM((local, rows, 1), f32),
            pltpu.VMEM((reps - 1, shards, *gown.shape[1:]), f32),
            pltpu.SemaphoreType.DMA((reps - 1, n)), pltpu.SemaphoreType.DMA((reps - 1, n)),
            pltpu.SemaphoreType.DMA((2, 2)), pltpu.SemaphoreType.DMA((3,)), pltpu.SemaphoreType.DMA((3, local)),
            *Spread.semaphores(shards, reps), *Spread.semaphores(shards, reps),
        ],
        compiler_params=pltpu.CompilerParams(vmem_limit_bytes=60 << 20, has_side_effects=True, collective_id=3),
        cost_estimate=pl.CostEstimate(
            flops=12 * slots * width * hidden, transcendentals=slots * hidden, bytes_accessed=4 * reps * shards * count * width
        ),
        name="spread_expert_sums",
    )(xown, cown, xcol, ccol, gown, gcol, wg, wu, wd, coth)
    return outs[0], outs[1], outs[5], outs[2:5]

def rotary_tables(count):
    half = HEAD_SIZE // 2
    inverse = np.exp(np.arange(half) * (-2.0 * math.log(10000.0) / HEAD_SIZE))
    angles = np.tile(np.arange(count)[:, None] * inverse[None, :], (1, LANES // half))
    return np.cos(angles).astype(np.float32), np.sin(angles).astype(np.float32)


def pack_small(w_router, norm_attn, norm_moe):
    small = jnp.concatenate([w_router, norm_attn[:, None], norm_moe[:, None]], axis=1)
    return jnp.pad(small, ((0, 0), (0, LANES - small.shape[1])))


def body(
    tokens, prefix, routes, cotangent, w_query, key_weight, value_weight, w_out,
    norm_attn, norm_moe, w_router, w_gate, w_up, w_down,
):
    count, width = tokens.shape
    local = w_gate.shape[0]
    shards, reps = lax.axis_size("shard"), lax.axis_size("rep")
    experts = local * shards
    kv_width = key_weight.shape[1]
    spread = reps == GATHERED_REPLICAS
    cosine, sine = rotary_tables(count)
    packed_own = (w_query, key_weight, value_weight, w_out, pack_small(w_router, norm_attn, norm_moe))
    packed, cot_own, cot_col, query, keys, values, attended, hidden_one, normed_two, gates, normed_one = front(
        tokens, prefix, routes.T, packed_own, cotangent, cosine, sine, experts, kv_width, spread
    )
    x_own, x_col, gates_own, gates_col, back, d_gates, mixture, cot_oth = moe_own(
        normed_two, gates, cot_own, cot_col, w_gate, w_up, w_down, spread
    )
    mixture = lax.psum_scatter(mixture.reshape(-1, width), "shard", scatter_dimension=0, tiled=True)
    d_tokens, shares = attention_back(
        prefix, tokens, cotangent, cosine, sine, packed, query, keys, values, attended, normed_one, normed_two, hidden_one,
        gates, d_gates.reshape(experts, count), back,
    )
    shares = shares.reshape(width, -1)
    if spread:
        x_own, shares = lax.optimization_barrier((x_own, shares))
        x_oth, cot_oth, gates_oth, sums = moe_spread_sums(
            x_own, cot_own, x_col, cot_col, cot_oth, gates_own, gates_col, w_gate, w_up, w_down
        )
        shares = lax.psum_scatter(shares, "shard", scatter_dimension=0, tiled=True)
        shares, gates_oth = lax.optimization_barrier((shares, gates_oth))
        sums = moe_sums(x_oth, cot_oth, gates_oth, w_gate, w_up, w_down, sums)
    else:
        sums = moe_sums(x_own, cot_own, gates_own, w_gate, w_up, w_down)
        sums = [lax.psum(a.astype(bf16), "rep").astype(f32) for a in sums]
        shares = lax.psum_scatter(shares, "shard", scatter_dimension=0, tiled=True)
    d_w_gate, d_w_up, d_w_down = sums
    totals = lax.psum(shares, "rep").astype(f32)
    cuts = [width, width + kv_width, width + 2 * kv_width, 2 * width + 2 * kv_width]
    d_wq, d_wk, d_wv, d_wo, small = jnp.split(totals, cuts, axis=1)
    result = (hidden_one + mixture.astype(f32)).astype(bf16)
    return (
        result, d_tokens, d_wq, d_wk, d_wv, d_wo, small[:, experts], small[:, experts + 1],
        small[:, :experts], d_w_gate, d_w_up, d_w_down,
    )


def solution(mesh):
    rows = P(("rep", "shard"), None)
    one, two, three = P("shard"), P("shard", None), P("shard", None, None)
    return jax.shard_map(
        body,
        mesh=mesh,
        in_specs=(rows, P(("rep", "shard")), rows, rows, two, two, two, two, one, one, two, three, three, three),
        out_specs=(rows, rows, two, two, two, two, one, one, two, three, three, three),
        check_vma=False,
    )
```

```python
import functools
import math

import jax
import jax.numpy as jnp
import numpy as np
from jax import lax
from jax.experimental import pallas as pl
from jax.experimental.pallas import tpu as pltpu
from jax.sharding import PartitionSpec as P

QUERY_HEADS = 16
KEY_VALUE_HEADS = 8
HEAD_SIZE = 64
CAP = 96
LANES = 128
GATHERED_REPLICAS = 4

epsilon = 1e-06
score_scale = 0.015625
branch_scale = 0.22
masked_value = -1e30

f32 = jnp.float32
bf16 = jnp.bfloat16
MESH = pl.DeviceIdType.MESH


def dot(left, right, contract=((1,), (0,))):
    return lax.dot_general(left, right, (contract, ((), ())), preferred_element_type=f32)

def slot_ranks(gates):
    tokens = gates.shape[1]
    named = gates > 0
    before = lax.broadcasted_iota(jnp.int32, (tokens, tokens), 0) < lax.broadcasted_iota(jnp.int32, (tokens, tokens), 1)
    rank = dot(named.astype(f32).astype(bf16), before.astype(f32).astype(bf16))
    return jnp.where(named, rank, -1.0)

def pick_row(table, row):
    here = lax.broadcasted_iota(jnp.int32, table.shape, 0) == row
    return jnp.sum(jnp.where(here, table, 0.0), axis=0, keepdims=True)

def slot_one_hot(ranks, first, local):
    tokens = ranks.shape[1]
    slot = lax.broadcasted_iota(jnp.int32, (CAP, tokens), 0).astype(f32)
    return [jnp.where(pick_row(ranks, first + l) == slot, 1.0, 0.0) for l in range(local)]

def gather_block(x, c, gates, first, local, xg_ref, cg_ref, sg_ref, at):
    ranks = slot_ranks(gates)
    parts = slot_one_hot(ranks, first, local)
    table = jnp.concatenate(parts, axis=0).astype(bf16)
    xg = dot(table, x).astype(bf16)
    cg = dot(table, c).astype(bf16)
    for l in range(local):
        rows = slice(l * CAP, (l + 1) * CAP)
        xg_ref[l, pl.ds(at, CAP), :] = xg[rows]
        cg_ref[l, pl.ds(at, CAP), :] = cg[rows]
        gate = jnp.sum(parts[l] * pick_row(gates, first + l), axis=1, keepdims=True)
        sg_ref[l, pl.ds(at, CAP), :] = branch_scale * gate
    return parts

def expert_parts(xg, cg, scale, wg, wu, wd):
    gate_part = dot(xg, wg)
    up_part = dot(xg, wu)
    raw = dot(cg, wd, ((1,), (1,)))
    sigma = 1.0 / (1.0 + jnp.exp(-gate_part))
    act = gate_part * sigma
    inner = act * up_part
    d_inner = raw * scale
    d_gate = (d_inner * up_part * (sigma + act * (1.0 - sigma))).astype(bf16)
    d_up = (d_inner * act).astype(bf16)
    scaled = (inner * scale).astype(bf16)
    return inner, raw, d_gate, d_up, scaled

def add_expert(l, xg_ref, cg_ref, sg_ref, wg, wu, wd, ag, au, ad):
    xg, cg = xg_ref[l], cg_ref[l]
    _, _, d_gate, d_up, scaled = expert_parts(xg, cg, sg_ref[l], wg[l], wu[l], wd[l])
    ag[l] += dot(xg, d_gate, ((0,), (0,)))
    au[l] += dot(xg, d_up, ((0,), (0,)))
    ad[l] += dot(scaled, cg, ((0,), (0,)))

def late_places(rep, reps):
    later = (rep + reps - 1) // reps
    return later * (reps - 2), (1 - later) * (reps - 2)

def sums_kernel(nb, more, x_hbm, c_hbm, g_ref, wg_hbm, wu_hbm, wd_hbm, *rest):
    if len(x_hbm.shape) == 4:
        _, left = late_places(lax.axis_index("rep"), lax.axis_size("rep"))
        x_hbm, c_hbm = x_hbm.at[left], c_hbm.at[left]
    starts, (og_hbm, ou_hbm, od_hbm, *scratch) = rest[:3 * more], rest[3 * more:]
    sums_body(nb, starts, x_hbm, c_hbm, g_ref, wg_hbm, wu_hbm, wd_hbm, og_hbm, ou_hbm, od_hbm, *scratch)

def sums_body(nb, starts, x_hbm, c_hbm, g_ref, wg_hbm, wu_hbm, wd_hbm, og_hbm, ou_hbm, od_hbm,
                xbuf, cbuf, wg, wu, wd, ag, au, ad, xg_ref, cg_ref, sg_ref, sem, wsem, asem):
    local = wg.shape[0]
    blocks = x_hbm.shape[0]
    chunks = blocks // nb
    first = lax.axis_index("shard") * local
    def fetch(i, slot):
        return (pltpu.make_async_copy(x_hbm.at[pl.ds(i * nb, nb)], xbuf.at[slot], sem.at[0, slot]),
                pltpu.make_async_copy(c_hbm.at[pl.ds(i * nb, nb)], cbuf.at[slot], sem.at[1, slot]))
    for cp in fetch(0, 0):
        cp.start()
    weights = [pltpu.make_async_copy(a, b, wsem.at[i]) for i, (a, b) in enumerate(((wg_hbm, wg), (wu_hbm, wu), (wd_hbm, wd)))]
    for cp in weights:
        cp.start()
    loads = [
        pltpu.make_async_copy(a.at[l], b.at[l], asem.at[i, l])
        for l in range(local) for i, (a, b) in enumerate(zip(starts, (ag, au, ad)))
    ]
    for cp in loads:
        cp.start()
    if not starts:
        ag[...] = jnp.zeros_like(ag)
        au[...] = jnp.zeros_like(au)
        ad[...] = jnp.zeros_like(ad)

    def chunk(i, carry):
        slot = lax.rem(i, 2)
        @pl.when(i + 1 < chunks)
        def _():
            for cp in fetch(i + 1, 1 - slot):
                cp.start()
        for cp in fetch(i, slot):
            cp.wait()
        def block(b, carry):
            gather_block(xbuf[slot, b], cbuf[slot, b], g_ref[i * nb + b], first, local, xg_ref, cg_ref, sg_ref,
                         pl.multiple_of(b * CAP, CAP))
            return carry
        lax.fori_loop(0, nb, block, 0)

        @pl.when(i == 0)
        def _():
            for cp in weights:
                cp.wait()

        def expert(l, carry):
            if starts:
                @pl.when(i == 0)
                def _():
                    for k, (a, b) in enumerate(zip(starts, (ag, au, ad))):
                        pltpu.make_async_copy(a.at[l], b.at[l], asem.at[k, l]).wait()
            add_expert(l, xg_ref, cg_ref, sg_ref, wg, wu, wd, ag, au, ad)

            @pl.when(i == chunks - 1)
            def _():
                for k, (a, b) in enumerate(((ag, og_hbm), (au, ou_hbm), (ad, od_hbm))):
                    pltpu.make_async_copy(a.at[l], b.at[l], asem.at[k, l]).start()
            return carry
        lax.fori_loop(0, local, expert, 0)
        return carry
    lax.fori_loop(0, chunks, chunk, 0)
    for l in range(local):
        for k, (a, b) in enumerate(((ag, og_hbm), (au, ou_hbm), (ad, od_hbm))):
            pltpu.make_async_copy(a.at[l], b.at[l], asem.at[k, l]).wait()

def moe_sums(x, c, gates, wg, wu, wd, starts=(), nb=4):
    blocks, tokens, width = x.shape[-3:]
    local, _, hidden = wg.shape
    any_ = pl.BlockSpec(memory_space=pl.ANY)
    rows = nb * CAP
    return pl.pallas_call(
        functools.partial(sums_kernel, nb, bool(starts)),
        out_shape=[jax.ShapeDtypeStruct(w.shape, f32) for w in (wg, wu, wd)],
        in_specs=[any_, any_, pl.BlockSpec(memory_space=pltpu.VMEM), any_, any_, any_] + [any_] * len(starts),
        out_specs=[any_] * 3,
        scratch_shapes=[
            pltpu.VMEM((2, nb, tokens, width), bf16), pltpu.VMEM((2, nb, tokens, width), bf16),
            pltpu.VMEM(wg.shape, bf16), pltpu.VMEM(wu.shape, bf16), pltpu.VMEM(wd.shape, bf16),
            pltpu.VMEM(wg.shape, f32), pltpu.VMEM(wu.shape, f32), pltpu.VMEM(wd.shape, f32),
            pltpu.VMEM((local, rows, width), bf16), pltpu.VMEM((local, rows, width), bf16), pltpu.VMEM((local, rows, 1), f32),
            pltpu.SemaphoreType.DMA((2, 2)), pltpu.SemaphoreType.DMA((3,)), pltpu.SemaphoreType.DMA((3, local)),
        ],
        compiler_params=pltpu.CompilerParams(vmem_limit_bytes=60 << 20),
        cost_estimate=pl.CostEstimate(
            flops=12 * blocks * local * CAP * width * hidden, transcendentals=blocks * local * CAP * hidden,
            bytes_accessed=4 * blocks * tokens * width + 24 * wg.size,
        ),
        name="expert_sums",
    )(x, c, gates, wg, wu, wd, *starts)


def norm_scale(rows):
    return lax.rsqrt(jnp.mean(rows * rows, axis=-1, keepdims=True) + epsilon)

def flip(index, bit):
    return index + bit - 2 * bit * ((index // bit) % 2)

def turned(index, core, step, bits):
    return (1 - core) * flip(index, bits[step]) + core * flip(index, bits[-1 - step])

def greet(spread):
    rep, me = lax.axis_index("rep"), lax.axis_index("shard")
    shards, reps = lax.axis_size("shard"), lax.axis_size("rep")
    peers = [(rep, (me + j) % shards) for j in range(1, shards)]
    if spread:
        peers += [((rep + j) % reps, me) for j in range(1, reps)]
    barrier = pltpu.get_barrier_semaphore()
    for peer in peers:
        pl.semaphore_signal(barrier, inc=1, device_id=peer, device_id_type=MESH)
    pl.semaphore_wait(barrier, len(peers))


class PlaneGather:
    def __init__(self, buf, own, send, recv, base=0):
        self.buf, self.own, self.send, self.recv, self.base = buf, own, send, recv, base
        self.rep, self.me = lax.axis_index("rep"), lax.axis_index("shard")
        self.core = self.me % 2
        shards = lax.axis_size("shard")
        self.bits = [1 << i for i in range(1, shards.bit_length() - 1)]
        self.steps = len(self.bits)

    @staticmethod
    def copies(shards):
        return (shards // 2 - 1) + shards // 2

    def owner(self, of, subset):
        for step in range(self.steps):
            if subset >> step & 1:
                of = turned(of, self.core, step, self.bits)
        return of

    def copy(self, number, subset, target):
        owner = self.owner(self.me, subset)
        return pltpu.make_async_remote_copy(
            src_ref=self.buf.at[owner] if subset else self.own, dst_ref=self.buf.at[owner],
            send_sem=self.send.at[self.base + number], recv_sem=self.recv.at[self.base + number],
            device_id=(self.rep, target), device_id_type=MESH,
        )

    def chip_copy(self, step, subset):
        return self.copy((1 << step) - 1 + subset, subset, turned(self.me, self.core, step, self.bits))

    def core_copy(self, subset):
        return self.copy((1 << self.steps) - 1 + subset, subset, flip(self.me, 1))

    def start(self):
        for step in range(self.steps):
            self.chip_copy(step, 0).start()
        self.core_copy(0).start()

    def forward(self, step):
        for subset in range(1 << step):
            self.chip_copy(step, subset).wait_recv()
            whole = subset + (1 << step)
            for later in range(step + 1, self.steps):
                self.chip_copy(later, whole).start()
            self.core_copy(whole).start()

    def finish(self):
        for subset in range(1 << self.steps):
            self.core_copy(subset).wait_recv()
        self.sent()

    def sent(self):
        for step in range(self.steps):
            for subset in range(1 << step):
                self.chip_copy(step, subset).wait_send()
        for subset in range(1 << self.steps):
            self.core_copy(subset).wait_send()

class RepSends:
    def __init__(self, buf, own, send, recv, neighbours):
        rep, me, reps = lax.axis_index("rep"), lax.axis_index("shard"), lax.axis_size("rep")
        self.rep, self.reps, self.neighbours = rep, reps, neighbours
        self.copies = [
            pltpu.make_async_remote_copy(
                src_ref=own, dst_ref=buf.at[rep], send_sem=send.at[j - 1], recv_sem=recv.at[j - 1],
                device_id=((rep + j) % reps, me), device_id_type=MESH,
            )
            for j in range(1, reps)
        ]

    def each(self, sent, act):
        for j, copy in enumerate(self.copies, 1):
            if self.neighbours or j not in (1, self.reps - 1):
                act(copy)
            else:
                end = self.reps - 1 if (j == 1) == sent else 0

                @pl.when(self.rep == end)
                def _(copy=copy):
                    act(copy)

    def start(self):
        self.each(True, lambda copy: copy.start())

    def finish(self):
        self.each(True, lambda copy: copy.wait_send())
        self.each(False, lambda copy: copy.wait_recv())


def on_ends(low, high):
    pl.when(lax.axis_index("rep") == 0)(low)
    pl.when(lax.axis_index("rep") == lax.axis_size("rep") - 1)(high)


class Spread:
    def __init__(self, oth, col, own, send, recv, psend, precv, asend, arecv, lsem):
        self.oth, self.col, self.own, self.send, self.recv = oth, col, own, send, recv
        self.psend, self.precv, self.asend, self.arecv, self.lsem = psend, precv, asend, arecv, lsem
        self.rep, self.me, self.reps = lax.axis_index("rep"), lax.axis_index("shard"), lax.axis_size("rep")
        self.core = self.me % 2
        self.blocks = range(lax.axis_size("shard") // 2)

    @staticmethod
    def semaphores(shards, reps):
        n = PlaneGather.copies(shards)
        dma = lambda *k: pltpu.SemaphoreType.DMA(k)
        return [dma(reps - 1, n), dma(reps - 1, n), *[dma(2, shards // 2)] * 4, dma(reps - 1)]

    def gather(self, j):
        return PlaneGather(self.oth.at[j - 1], self.col.at[(self.rep + j) % self.reps], self.send.at[j - 1], self.recv.at[j - 1])

    def own_copy(self, j):
        return pltpu.make_async_copy(self.col.at[(self.rep + j) % self.reps], self.oth.at[j - 1, self.me], self.lsem.at[j - 1])

    def begin(self, j):
        self.gather(j).start()
        self.own_copy(j).start()

    def forward(self, j):
        self.gather(j).forward(0)

    def end(self, j):
        gather = self.gather(j)
        for step in range(1, gather.steps):
            gather.forward(step)
        gather.finish()
        self.own_copy(j).wait()

    def straight(self, up, b):
        at, way = 2 * b + self.core, self.reps - 2 if up else 0
        return pltpu.make_async_remote_copy(
            src_ref=self.own.at[at], dst_ref=self.oth.at[way, at], send_sem=self.psend.at[up, b], recv_sem=self.precv.at[up, b],
            device_id=((self.rep + (1 if up else self.reps - 1)) % self.reps, self.me), device_id_type=MESH,
        )

    def across(self, up, b):
        at, way = 2 * b + self.core, self.reps - 2 if up else 0
        return pltpu.make_async_remote_copy(
            src_ref=self.oth.at[way, at], dst_ref=self.oth.at[way, at], send_sem=self.asend.at[up, b], recv_sem=self.arecv.at[up, b],
            device_id=(self.rep, flip(self.me, 1)), device_id_type=MESH,
        )

    def sends(self, up):
        return self.rep < self.reps - 1 if up else self.rep > 0

    def gets(self, up):
        return self.rep > 0 if up else self.rep < self.reps - 1

    def start_straight(self):
        for up in (0, 1):
            @pl.when(self.sends(up))
            def _(up=up):
                for b in self.blocks:
                    self.straight(up, b).start()

    def sent_straight(self):
        for up in (0, 1):
            @pl.when(self.sends(up))
            def _(up=up):
                for b in self.blocks:
                    self.straight(up, b).wait_send()

    def got_straight(self, up):
        @pl.when(self.gets(up))
        def _():
            for b in self.blocks:
                self.straight(up, b).wait_recv()

    def start_across(self, up):
        @pl.when(self.gets(up))
        def _():
            for b in self.blocks:
                self.across(up, b).start()

    def end_across(self, up):
        @pl.when(self.gets(up))
        def _():
            for b in self.blocks:
                self.across(up, b).wait()


def rotate(v, cosine, sine, sign):
    lane = lax.broadcasted_iota(jnp.int32, v.shape, 1) % HEAD_SIZE
    half = HEAD_SIZE // 2
    low = lane < half
    other = jnp.where(low, -pltpu.roll(v, LANES - half, 1), pltpu.roll(v, half, 1))
    return v * cosine + sign * other * sine

def two_heads(v):
    low = lax.broadcasted_iota(jnp.int32, v.shape, 1) < HEAD_SIZE
    zero = jnp.zeros_like(v)
    return jnp.concatenate([jnp.where(low, v, zero), jnp.where(low, zero, v)], axis=0)

def one_head_twice(pair, odd):
    high = lax.broadcasted_iota(jnp.int32, pair.shape, 1) // HEAD_SIZE
    wide = pair.astype(f32)
    return jnp.where(high == odd, wide, pltpu.roll(wide, HEAD_SIZE, 1)).astype(pair.dtype)

def probabilities(query2, keys, prefix_len):
    rows = query2.shape[0] // 2
    raw = dot(query2, keys, ((1,), (1,)))
    row = lax.broadcasted_iota(jnp.int32, raw.shape, 0) % rows
    col = lax.broadcasted_iota(jnp.int32, raw.shape, 1)
    scores = jnp.where((col <= row) | (col < prefix_len), raw * score_scale, masked_value)
    weights = jnp.exp(scores - jnp.max(scores, axis=-1, keepdims=True))
    return weights / jnp.sum(weights, axis=-1, keepdims=True)

def lanes(j, count=1):
    return pl.ds(pl.multiple_of(j * LANES * count, LANES), LANES * count)

def front_kernel(spread, prefix_ref, tok_ref, routes_ref, cos_ref, sin_ref, wq_hbm, wk_hbm, wv_hbm, wo_hbm, ws_hbm, cot_ref,
                 wall_out, cown_out, ccol_out, q_out, k_out, v_out, att_out, hid_out, x_out, gates_out, n1_out,
                 wbuf, qkv_ref, send, recv, csend, crecv, zsend, zrecv, lsem, osem):
    count, width = tok_ref.shape
    kv_width = k_out.shape[1]
    experts = gates_out.shape[0]
    shards, depth, total = wbuf.shape
    me = lax.axis_index("shard")
    own, at = [], 0
    for i, part in enumerate((wq_hbm, wk_hbm, wv_hbm, wo_hbm, ws_hbm)):
        own.append(pltpu.make_async_copy(part, wbuf.at[me, :, at:at + part.shape[1]], osem.at[i]))
        own[-1].start()
        at += part.shape[1]
    greet(spread)
    gather = PlaneGather(wbuf, wbuf.at[me], send, recv)
    for copy in own:
        copy.wait()
    gather.start()
    far = RepSends(ccol_out, cot_ref, zsend, zrecv, False)
    if spread:
        far.start()
    near = PlaneGather(cown_out, cot_ref, csend, crecv)
    own_cot = pltpu.make_async_copy(cot_ref, cown_out.at[me], lsem.at[2])
    own_cot.start()
    inputs = tok_ref[...].astype(f32)
    scaled = inputs * norm_scale(inputs)
    for step in range(gather.steps):
        gather.forward(step)
    near.start()
    gather.finish()
    keep = pltpu.make_async_copy(wbuf, wall_out, lsem.at[1])
    keep.start()
    cut = [0, width, width + kv_width, width + 2 * kv_width, 2 * width + 2 * kv_width]
    small = wbuf[:, :, cut[4]:].reshape(shards * depth, total - cut[4])
    wide = small.astype(f32).T
    gain_one, gain_two = wide[experts:experts + 1], wide[experts + 1:experts + 2]
    n1_out[...] = (scaled * gain_one).astype(bf16)

    def project(j, carry):
        w = wbuf[:, :, lanes(j, 2)].reshape(shards * depth, 2 * LANES)
        qkv_ref[:, lanes(j, 2)] = dot(n1_out[...], w)
        return carry
    lax.fori_loop(0, cut[3] // (2 * LANES), project, 0)
    cosine, sine = cos_ref[...], sin_ref[...]
    for j in range(width // LANES):
        q_out[:, j * LANES:(j + 1) * LANES] = rotate(qkv_ref[:, j * LANES:(j + 1) * LANES], cosine, sine, 1.0).astype(bf16)
    for j in range(kv_width // LANES):
        at = slice(cut[1] + j * LANES, cut[1] + (j + 1) * LANES)
        k_out[:, j * LANES:(j + 1) * LANES] = rotate(qkv_ref[:, at], cosine, sine, 1.0).astype(bf16)
    v_out[...] = qkv_ref[:, cut[2]:cut[3]].astype(bf16)
    prefix_len = prefix_ref[0]


    def head(j, carry):
        keys = one_head_twice(k_out[:, lanes(j // 2)], j % 2)
        values = one_head_twice(v_out[:, lanes(j // 2)], j % 2)
        prob = probabilities(two_heads(q_out[:, lanes(j)]), keys, prefix_len)
        both = dot(prob.astype(bf16), values)
        low = lax.broadcasted_iota(jnp.int32, (count, LANES), 1) < HEAD_SIZE
        att_out[:, lanes(j)] = jnp.where(low, both[:count], both[count:]).astype(bf16)

        @pl.when(j == 2)
        def _():
            near.forward(0)
        return carry
    lax.fori_loop(0, KEY_VALUE_HEADS, head, 0)
    for step in range(1, near.steps):
        near.forward(step)

    def project_out(j, carry):
        w = wbuf[:, :, pl.ds(pl.multiple_of(cut[3] + j * 2 * LANES, LANES), 2 * LANES)].reshape(shards * depth, 2 * LANES)
        qkv_ref[:, lanes(j, 2)] = dot(att_out[...], w)
        return carry
    lax.fori_loop(0, width // (2 * LANES), project_out, 0)
    hidden = inputs + branch_scale * qkv_ref[:, :width]
    hid_out[...] = hidden
    x = (hidden * norm_scale(hidden) * gain_two).astype(bf16)
    x_out[...] = x
    logits = dot(x, small).T[:experts]
    expert = lax.broadcasted_iota(jnp.int32, (experts, count), 0)
    named = expert < 0
    for k in range(routes_ref.shape[0]):
        named = named | (routes_ref[k:k + 1, :] == expert)
    top = jnp.max(jnp.where(named, logits, masked_value), axis=0, keepdims=True)
    weights = jnp.where(named, jnp.exp(jnp.where(named, logits - top, 0.0)), 0.0)
    gates_out[...] = weights / jnp.sum(weights, axis=0, keepdims=True)
    keep.wait()
    near.finish()
    own_cot.wait()
    if spread:
        far.finish()

def front(tokens, prefix, routes, mine, cot, cosine, sine, experts, kv_width, spread):
    count, width = tokens.shape
    shards, reps = lax.axis_size("shard"), lax.axis_size("rep")
    depth, total = tokens.shape[1] // shards, sum(part.shape[1] for part in mine)
    v = pl.BlockSpec(memory_space=pltpu.VMEM)
    any_ = pl.BlockSpec(memory_space=pl.ANY)
    sds = jax.ShapeDtypeStruct
    n = PlaneGather.copies(shards)
    return pl.pallas_call(
        functools.partial(front_kernel, spread),
        out_shape=[
            sds((shards, depth, total), bf16), sds((shards, count, width), bf16), sds((reps, count, width), bf16), sds((count, width), bf16), sds((count, kv_width), bf16), sds((count, kv_width), bf16),
            sds((count, width), bf16), sds((count, width), f32), sds((count, width), bf16), sds((experts, count), f32), sds((count, width), bf16),
        ],
        in_specs=[pl.BlockSpec(memory_space=pltpu.SMEM), v, v, v, v] + [any_] * 6,
        out_specs=[any_] * 3 + [v] * 8,
        scratch_shapes=[
            pltpu.VMEM((shards, depth, total), bf16), pltpu.VMEM((count, width + 2 * kv_width), f32),
            *[pltpu.SemaphoreType.DMA((k,)) for k in (n, n, n, n, reps, reps, 3, 5)],
        ],
        compiler_params=pltpu.CompilerParams(vmem_limit_bytes=60 << 20, has_side_effects=True, collective_id=1),
        name="front",
    )(prefix, tokens, routes, cosine, sine, *mine, cot)

class PlaneReduce:
    def __init__(self, mine, theirs, from_core, from_chip, csend, crecv, send, recv):
        self.mine, self.theirs, self.from_core, self.from_chip = mine, theirs, from_core, from_chip
        self.csend, self.crecv, self.send, self.recv = csend, crecv, send, recv
        self.rep, self.me = lax.axis_index("rep"), lax.axis_index("shard")
        self.core = self.me % 2
        self.bits = [1 << i for i in range(1, lax.axis_size("shard").bit_length() - 1)]
        self.steps = len(self.bits)

    def owner(self, core, u):
        at = flip(self.me, 1) if core else self.me
        of = (1 - self.core) if core else self.core
        for step in range(self.steps):
            if u >> step & 1:
                at = turned(at, of, step, self.bits)
        return at

    def core_copy(self, u):
        return pltpu.make_async_remote_copy(
            src_ref=self.theirs.at[u], dst_ref=self.from_core.at[u], send_sem=self.csend.at[u], recv_sem=self.crecv.at[u],
            device_id=(self.rep, flip(self.me, 1)), device_id_type=MESH,
        )

    def slot(self, step, u):
        return (1 << self.steps) - (1 << (self.steps - step)) + (u >> (step + 1))

    def chip_copy(self, step, u):
        slot = self.slot(step, u)
        return pltpu.make_async_remote_copy(
            src_ref=self.mine.at[u], dst_ref=self.from_chip.at[slot], send_sem=self.send.at[slot], recv_sem=self.recv.at[slot],
            device_id=(self.rep, turned(self.me, self.core, step, self.bits)), device_id_type=MESH,
        )

    def total(self, u, before, rows):
        whole = self.mine[u, rows].astype(f32) + self.from_core[u, rows].astype(f32)
        for step in range(before):
            whole = whole + self.from_chip[self.slot(step, u), rows].astype(f32)
        return whole

    def send_on(self, step, u):
        self.core_copy(u).wait_recv()
        count = self.mine.shape[1]
        piece = 32

        def add(i, carry):
            rows = pl.ds(pl.multiple_of(i * piece, piece), piece)
            self.mine[u, rows] = self.total(u, step, rows).astype(bf16)
            return carry
        lax.fori_loop(0, count // piece, add, 0)
        self.chip_copy(step, u).start()

    def group(self, step):
        return [u for u in range(1 << self.steps) if u % (2 << step) == 1 << step]

    def arrive(self, step):
        for u in self.group(step):
            self.chip_copy(step, u).wait_recv()

    def advance(self, step):
        if step < self.steps:
            if step:
                self.arrive(step - 1)
            for u in self.group(step):
                self.send_on(step, u)

    def last(self, out, plus=None):
        self.arrive(self.steps - 1)
        self.core_copy(0).wait_recv()
        count = self.mine.shape[1]
        piece = 32

        def add(i, carry):
            rows = pl.ds(pl.multiple_of(i * piece, piece), piece)
            whole = self.total(0, self.steps, rows)
            out[rows] = (whole if plus is None else whole + plus[rows]).astype(out.dtype)
            return carry
        lax.fori_loop(0, count // piece, add, 0)

    def finish(self):
        for u in range(1 << self.steps):
            self.core_copy(u).wait_send()
        for step in range(self.steps):
            for u in self.group(step):
                self.chip_copy(step, u).wait_send()


def own_kernel(spread, nb, x_ref, gates_ref, c_hbm, ccol_hbm, wg_hbm, wu_hbm, wd_hbm,
               xown_out, xcol_out, gown_out, gcol_out, back_out, dg_out, mix_out, coth_out,
               wg, wu, wd, xb, cb, xg_ref, cg_ref, sg_ref, y_ref, ds_ref, mine, theirs, mix, from_core, from_chip,
               gown, gcol, dgs, dgr,
               xs, xr, zxs, zxr, zgs, zgr, gs, gr, dss, dsr, css, csr, hs, hr, wsem, bsem, lsem, msem, *csems):
    count, width = x_ref.shape
    local, _, hidden = wg.shape
    rep, me = lax.axis_index("rep"), lax.axis_index("shard")
    shards = lax.axis_size("shard")
    first = me * local
    greet(spread)
    near = PlaneGather(xown_out, x_ref, xs, xr)
    near.start()
    gown[me] = gates_ref[...]

    def peer(j):
        return (rep, (me + j) % shards)

    gate_sends = [
        pltpu.make_async_remote_copy(
            src_ref=gates_ref, dst_ref=gown.at[me], send_sem=gs.at[j - 1], recv_sem=gr.at[j - 1],
            device_id=peer(j), device_id_type=MESH,
        )
        for j in range(1, shards)
    ]
    for copy in gate_sends:
        copy.start()
    far = [RepSends(xcol_out, x_ref, zxs, zxr, False), RepSends(gcol, gates_ref, zgs, zgr, True)] if spread else []
    for sends in far:
        sends.start()
    cots = Spread(coth_out, ccol_hbm, c_hbm, *csems)
    reps = lax.axis_size("rep")
    if spread:
        cots.start_straight()
    own_x = pltpu.make_async_copy(x_ref, xown_out.at[me], lsem)
    own_x.start()
    weights = [pltpu.make_async_copy(a, b, wsem.at[i]) for i, (a, b) in enumerate(((wg_hbm, wg), (wu_hbm, wu), (wd_hbm, wd)))]
    for copy in weights:
        copy.start()
    reduce = PlaneReduce(mine, theirs, from_core, from_chip, css, csr, hs, hr)
    for copy in gate_sends:
        copy.wait_recv()
    order = list(range(1 << reduce.steps))
    half = nb // 2
    dg_sends, mixes = [], []

    def fetch(at, slot):
        return (pltpu.make_async_copy(xown_out.at[at], xb.at[slot], bsem.at[0, slot]),
                pltpu.make_async_copy(c_hbm.at[at], cb.at[slot], bsem.at[1, slot]))

    chunks = [order[q:q + half] for q in range(0, len(order), half)]
    forwarded = 0
    for q, chunk in enumerate(chunks):
        plan = [(core, u) for u in chunk for core in (0, 1)]
        owners = [reduce.owner(core, u) for core, u in plan]
        while forwarded < chunk[-1].bit_length():
            near.forward(forwarded)
            forwarded += 1
        if not q:
            own_x.wait()
        for u in chunk:
            near.core_copy(u).wait_recv()
        for copy in fetch(owners[0], 0):
            copy.start()
        for b in range(nb):
            if b + 1 < nb:
                for copy in fetch(owners[b + 1], (b + 1) % 2):
                    copy.start()
            for copy in fetch(owners[b], b % 2):
                copy.wait()
            gather_block(xb[b % 2], cb[b % 2], gown[owners[b]], first, local, xg_ref, cg_ref, sg_ref, b * CAP)
        if not q:
            for copy in weights:
                copy.wait()

        def expert(l, carry):
            inner, raw, d_gate, d_up, scaled = expert_parts(xg_ref[l], cg_ref[l], sg_ref[l], wg[l], wu[l], wd[l])
            ds_ref[l] = branch_scale * jnp.sum(inner * raw, axis=1, keepdims=True)
            rows = pl.ds(pl.multiple_of(l * CAP, CAP), CAP)
            out = dot(scaled, wd[l]).astype(bf16)
            d_in = (dot(d_gate, wg[l], ((1,), (1,))) + dot(d_up, wu[l], ((1,), (1,)))).astype(bf16)
            for b in range(nb):
                y_ref[b, rows, :width] = out[b * CAP:(b + 1) * CAP]
                y_ref[b, rows, width:] = d_in[b * CAP:(b + 1) * CAP]
            return carry
        lax.fori_loop(0, local, expert, 0)
        if q + 1 < len(chunks):
            while forwarded < chunks[q + 1][-1].bit_length():
                near.forward(forwarded)
                forwarded += 1
        if spread:
            if not q:
                cots.begin(2)
            else:
                cots.forward(2)
        for b in range(nb):
            core, u = plan[b]
            parts = slot_one_hot(slot_ranks(gown[owners[b]]), first, local)
            table = jnp.concatenate(parts, axis=0).astype(bf16)
            both = dot(table, y_ref[b], ((0,), (0,))).astype(bf16)
            mix[core, u] = both[:, :width]
            mixes.append(pltpu.make_async_copy(mix.at[core, u], mix_out.at[owners[b]], msem.at[core, u]))
            mixes[-1].start()
            (theirs if core else mine)[u] = both[:, width:]
            if core:
                reduce.core_copy(u).start()
            dgs[owners[b]] = jnp.concatenate(
                [jnp.sum(parts[l] * ds_ref[l, b * CAP:(b + 1) * CAP], axis=0, keepdims=True) for l in range(local)], axis=0
            )
        for u in chunk:
            if u % 2:
                reduce.send_on(0, u)
    for j in range(1, shards):
        copy = pltpu.make_async_remote_copy(
            src_ref=dgs.at[(me + j) % shards], dst_ref=dgr.at[me], send_sem=dss.at[j - 1], recv_sem=dsr.at[j - 1],
            device_id=peer(j), device_id_type=MESH,
        )
        copy.start()
        dg_sends.append(copy)
    dgr[me] = dgs[me]
    gown_out[...] = gown[...]
    for step in range(1, reduce.steps):
        reduce.advance(step)
    reduce.last(back_out)
    for copy in dg_sends:
        copy.wait()
    dg_out[...] = dgr[...]
    if spread:
        cots.end(2)
        cots.got_straight(0)
        cots.got_straight(1)
        cots.sent_straight()
    reduce.finish()
    for copy in mixes:
        copy.wait()
    near.sent()
    for copy in gate_sends:
        copy.wait_send()
    for sends in far:
        sends.finish()
    if spread:
        gcol_out[...] = gcol[...]


def moe_own(x, gates, c, ccol, wg, wu, wd, spread, nb=4):
    count, width = x.shape
    local, _, hidden = wg.shape
    shards, reps = lax.axis_size("shard"), lax.axis_size("rep")
    experts = local * shards
    v = pl.BlockSpec(memory_space=pltpu.VMEM)
    any_ = pl.BlockSpec(memory_space=pl.ANY)
    sds = jax.ShapeDtypeStruct
    n = PlaneGather.copies(shards)
    rows = nb * CAP
    half = shards // 2
    dma = lambda *k: pltpu.SemaphoreType.DMA(k)
    return pl.pallas_call(
        functools.partial(own_kernel, spread, nb),
        out_shape=[
            sds((shards, count, width), bf16), sds((reps, count, width), bf16), sds((shards, experts, count), f32),
            sds((reps, experts, count), f32), sds((count, width), f32), sds((shards, local, count), f32),
            sds((shards, count, width), bf16), sds((max(reps - 1, 1), shards, count, width) if spread else (1, 1, 16, LANES), bf16),
        ],
        in_specs=[v, v, any_, any_, any_, any_, any_],
        out_specs=[any_, any_, v, v, v, v, any_, any_],
        scratch_shapes=[
            pltpu.VMEM(wg.shape, bf16), pltpu.VMEM(wu.shape, bf16), pltpu.VMEM(wd.shape, bf16),
            pltpu.VMEM((2, count, width), bf16), pltpu.VMEM((2, count, width), bf16),
            pltpu.VMEM((local, rows, width), bf16), pltpu.VMEM((local, rows, width), bf16), pltpu.VMEM((local, rows, 1), f32),
            pltpu.VMEM((nb, local * CAP, 2 * width), bf16), pltpu.VMEM((local, rows, 1), f32),
            *[pltpu.VMEM((k, count, width), bf16) for k in (half, half)], pltpu.VMEM((2, half, count, width), bf16),
            *[pltpu.VMEM((k, count, width), bf16) for k in (half, half - 1)],
            pltpu.VMEM((shards, experts, count), f32), pltpu.VMEM((reps, experts, count), f32),
            pltpu.VMEM((shards, local, count), f32), pltpu.VMEM((shards, local, count), f32),
            dma(n), dma(n), dma(reps), dma(reps), dma(reps), dma(reps), dma(shards), dma(shards), dma(shards), dma(shards),
            dma(half), dma(half), dma(half), dma(half), dma(3), dma(2, 2), pltpu.SemaphoreType.DMA, dma(2, half),
            *Spread.semaphores(shards, reps),
        ],
        compiler_params=pltpu.CompilerParams(vmem_limit_bytes=60 << 20, has_side_effects=True, collective_id=2),
        name="own_experts",
    )(x, gates, c, ccol, wg, wu, wd)

def norm_backward(rows, scaling, gain, upstream):
    weighted = upstream * gain
    inner_mean = jnp.mean(weighted * rows, axis=-1, keepdims=True)
    gradient = scaling * weighted - rows * (scaling * scaling * scaling) * inner_mean
    return gradient, jnp.sum(upstream * rows * scaling, axis=0, keepdims=True)


def back_kernel(prefix_ref, tok_ref, cot_ref, cos_ref, sin_ref, w_ref, q_ref, k_ref, v_ref, att_ref, n1_ref, x_ref,
                hid_ref, gates_ref, dg_ref, back_ref, dtok_out, shares_out, dqkv_ref, datt_ref, dproj_ref):
    count, width = tok_ref.shape
    kv_width = k_ref.shape[1]
    experts = gates_ref.shape[0]
    shards, depth, total = w_ref.shape
    rows = shards * depth
    cut = [0, width, width + kv_width, width + 2 * kv_width, 2 * width + 2 * kv_width]
    small = w_ref[:, :, cut[4]:].reshape(rows, total - cut[4])
    wide = small.astype(f32).T
    gain_one, gain_two = wide[experts:experts + 1], wide[experts + 1:experts + 2]
    hidden = hid_ref[...]
    gates, d_gates = gates_ref[...], dg_ref[...]
    d_logits = gates * (d_gates - jnp.sum(gates * d_gates, axis=0, keepdims=True))
    none = jnp.zeros((LANES - experts, count), f32)
    d_logits = jnp.concatenate([d_logits, none], axis=0).T.astype(bf16)
    d_normed_two = back_ref[...] + dot(d_logits, small, ((1,), (1,)))
    d_hidden, d_gain_two = norm_backward(hidden, norm_scale(hidden), gain_two, d_normed_two)
    d_hidden = d_hidden + cot_ref[...].astype(f32)
    dtok_out[...] = d_hidden
    dproj_ref[...] = (branch_scale * d_hidden).astype(bf16)
    tile = 2 * LANES

    def out_tile(j, carry):
        grad = dot(att_ref[...], dproj_ref[:, lanes(j, 2)], ((0,), (0,))).astype(bf16)
        at = pl.ds(pl.multiple_of(cut[3] + j * tile, LANES), tile)
        shares_out[:, :, at] = grad.reshape(shards, depth, tile)
        return carry
    lax.fori_loop(0, width // tile, out_tile, 0)
    datt_ref[...] = dot(dproj_ref[...], w_ref[:, :, cut[3]:cut[4]].reshape(rows, width), ((1,), (1,))).astype(bf16)
    cosine, sine = cos_ref[...], sin_ref[...]
    prefix_len = prefix_ref[0]
    low = lax.broadcasted_iota(jnp.int32, (count, LANES), 1) < HEAD_SIZE

    def pair(p, carry):
        at_k = pl.ds(pl.multiple_of(cut[1] + p * LANES, LANES), LANES)
        at_v = pl.ds(pl.multiple_of(cut[2] + p * LANES, LANES), LANES)
        d_keys, d_values = [], []
        for odd in range(2):
            j = 2 * p + odd
            keys = one_head_twice(k_ref[:, lanes(p)], odd)
            values = one_head_twice(v_ref[:, lanes(p)], odd)
            query2, d_att2 = two_heads(q_ref[:, lanes(j)]), two_heads(datt_ref[:, lanes(j)])
            prob = probabilities(query2, keys, prefix_len)
            d_value = dot(prob.astype(bf16), d_att2, ((0,), (0,)))
            d_prob = dot(d_att2, values, ((1,), (1,)))
            weighted = jnp.sum(prob * d_prob, axis=-1, keepdims=True)
            d_score = (prob * (d_prob - weighted) * score_scale).astype(bf16)
            d_query = dot(d_score, keys)
            d_query = jnp.where(low, d_query[:count], d_query[count:])
            dqkv_ref[:, lanes(j)] = rotate(d_query, cosine, sine, -1.0).astype(bf16)
            d_key = dot(d_score, query2, ((0,), (0,)))
            d_keys.append(d_key + pltpu.roll(d_key, HEAD_SIZE, 1))
            d_values.append(d_value + pltpu.roll(d_value, HEAD_SIZE, 1))
        dqkv_ref[:, at_k] = rotate(jnp.where(low, *d_keys), cosine, sine, -1.0).astype(bf16)
        dqkv_ref[:, at_v] = jnp.where(low, *d_values).astype(bf16)
        return carry
    lax.fori_loop(0, KEY_VALUE_HEADS // 2, pair, 0)

    def in_tile(j, carry):
        grad = dot(n1_ref[...], dqkv_ref[:, lanes(j, 2)], ((0,), (0,))).astype(bf16)
        shares_out[:, :, lanes(j, 2)] = grad.reshape(shards, depth, tile)
        return carry
    lax.fori_loop(0, cut[3] // tile, in_tile, 0)
    d_normed_one = dot(dqkv_ref[...], w_ref[:, :, :cut[3]].reshape(rows, cut[3]), ((1,), (1,)))
    inputs = tok_ref[...].astype(f32)
    d_inputs, d_gain_one = norm_backward(inputs, norm_scale(inputs), gain_one, d_normed_one)
    dtok_out[...] += d_inputs
    row = lax.broadcasted_iota(jnp.int32, (LANES, rows), 0)
    gains = jnp.where(row == experts, d_gain_one, jnp.where(row == experts + 1, d_gain_two, 0.0)).T
    d_small = (dot(x_ref[...], d_logits, ((0,), (0,))) + gains).astype(bf16)
    shares_out[:, :, cut[4]:] = d_small.reshape(shards, depth, total - cut[4])


def attention_back(prefix, tokens, cot, cosine, sine, packed, query, keys, values, attended, n1, x, hidden, gates, d_gates, back):
    count, width = tokens.shape
    v = pl.BlockSpec(memory_space=pltpu.VMEM)
    sds = jax.ShapeDtypeStruct
    return pl.pallas_call(
        back_kernel,
        out_shape=[sds((count, width), f32), sds(packed.shape, bf16)],
        in_specs=[pl.BlockSpec(memory_space=pltpu.SMEM)] + [v] * 15,
        out_specs=[v] * 2,
        scratch_shapes=[
            pltpu.VMEM((count, width + 2 * keys.shape[1]), bf16), pltpu.VMEM((count, width), bf16), pltpu.VMEM((count, width), bf16),
        ],
        compiler_params=pltpu.CompilerParams(vmem_limit_bytes=60 << 20),
        name="attention_back",
    )(prefix, tokens, cot, cosine, sine, packed, query, keys, values, attended, n1, x, hidden, gates, d_gates, back)

def spread_kernel(nb, xown_hbm, cown_hbm, xcol_hbm, ccol_hbm, gown_ref, gcol_ref, wg_hbm, wu_hbm, wd_hbm, coth_in,
                  xoth_hbm, coth_hbm, og_hbm, ou_hbm, od_hbm, glast_ref,
                  xbuf, cbuf, wg, wu, wd, ag, au, ad, xg_ref, cg_ref, sg_ref, goth, send, recv, bsem, wsem, osem, *sems):
    xsems, csems = sems[:7], sems[7:]
    local = wg.shape[0]
    shards = gown_ref.shape[0]
    rep, me = lax.axis_index("rep"), lax.axis_index("shard")
    reps = lax.axis_size("rep")
    first = me * local
    chunks = shards // nb

    xs = Spread(xoth_hbm, xcol_hbm, xown_hbm, *xsems)
    cs = Spread(coth_hbm, ccol_hbm, cown_hbm, *csems)
    both = (xs, cs)

    def each(act, j):
        for one in both:
            act(one, j)

    def gate_gathers():
        return [PlaneGather(goth.at[j - 1], gcol_ref.at[(rep + j) % reps], send.at[j - 1], recv.at[j - 1]) for j in range(1, reps)]

    def fetch(x, c, q, slot):
        return (pltpu.make_async_copy(x.at[pl.ds(q * nb, nb)], xbuf.at[slot], bsem.at[0, slot]),
                pltpu.make_async_copy(c.at[pl.ds(q * nb, nb)], cbuf.at[slot], bsem.at[1, slot]))

    def out_copies(l):
        return [pltpu.make_async_copy(a.at[l], b.at[l], osem.at[i, l]) for i, (a, b) in enumerate(((ag, og_hbm), (au, ou_hbm), (ad, od_hbm)))]

    def replica(x, c, g, midway, last, opening=False, final=False):
        for copy in fetch(x, c, 0, 0):
            copy.start()

        def chunk(q, carry):
            slot = lax.rem(q, 2)

            @pl.when(q + 1 < chunks)
            def _():
                for copy in fetch(x, c, q + 1, 1 - slot):
                    copy.start()
            for copy in fetch(x, c, q, slot):
                copy.wait()

            def block(b, carry):
                gather_block(xbuf[slot, b], cbuf[slot, b], g[q * nb + b], first, local, xg_ref, cg_ref, sg_ref,
                             pl.multiple_of(b * CAP, CAP))
                return carry
            lax.fori_loop(0, nb, block, 0)
            if opening:
                @pl.when(q == 0)
                def _():
                    for copy in weights:
                        copy.wait()

            def expert(l, carry):
                add_expert(l, xg_ref, cg_ref, sg_ref, wg, wu, wd, ag, au, ad)

                @pl.when((q == chunks // 2) & (l == 0))
                def _():
                    midway()

                if final:
                    @pl.when(q == chunks - 1)
                    def _():
                        for copy in out_copies(l):
                            copy.start()
                return carry
            lax.fori_loop(0, local, expert, 0)
            return carry
        lax.fori_loop(0, chunks, chunk, 0)
        last()

    greet(True)
    xs.begin(2)
    for j in range(1, reps):
        goth[j - 1, me] = gcol_ref[(rep + j) % reps]
    for gather in gate_gathers():
        gather.start()
    xs.start_straight()
    for up in (0, 1):
        cs.start_across(up)
    weights = [pltpu.make_async_copy(a, b, wsem.at[i]) for i, (a, b) in enumerate(((wg_hbm, wg), (wu_hbm, wu), (wd_hbm, wd)))]
    for copy in weights:
        copy.start()
    ag[...] = jnp.zeros_like(ag)
    au[...] = jnp.zeros_like(au)
    ad[...] = jnp.zeros_like(ad)

    def midway_own():
        xs.forward(2)
        for gather in gate_gathers():
            gather.forward(0)
        on_ends(lambda: each(Spread.begin, reps - 1), lambda: each(Spread.begin, 1))

    def last_own():
        xs.end(2)
        for gather in gate_gathers():
            for step in range(1, gather.steps):
                gather.forward(step)
        for gather in gate_gathers():
            gather.finish()
        for up in (0, 1):
            cs.end_across(up)

    def midway_two():
        on_ends(lambda: each(Spread.forward, reps - 1), lambda: each(Spread.forward, 1))
        xs.got_straight(1)
        xs.start_across(1)

        @pl.when(rep == 0)
        def _():
            xs.got_straight(0)
            xs.start_across(0)

    def last_two():
        xs.end_across(1)
        pl.when(rep == 0)(lambda: xs.end_across(0))

    def midway_three():
        @pl.when(rep > 0)
        def _():
            xs.got_straight(0)
            xs.start_across(0)

    def last_three():
        on_ends(lambda: each(Spread.end, reps - 1), lambda: each(Spread.end, 1))
        pl.when(rep > 0)(lambda: xs.end_across(0))

    replica(xown_hbm, cown_hbm, gown_ref, midway_own, last_own, opening=True)
    replica(xoth_hbm.at[1], coth_hbm.at[1], goth.at[1], midway_two, last_two)
    third, left = late_places(rep, reps)
    replica(xoth_hbm.at[third], coth_hbm.at[third], goth.at[third], midway_three, last_three, final=True)
    xs.sent_straight()
    glast_ref[...] = goth[left]
    for l in range(local):
        for copy in out_copies(l):
            copy.wait()


def moe_spread_sums(xown, cown, xcol, ccol, coth, gown, gcol, wg, wu, wd, nb=4):
    shards, count, width = xown.shape
    reps = xcol.shape[0]
    local, _, hidden = wg.shape
    any_ = pl.BlockSpec(memory_space=pl.ANY)
    v = pl.BlockSpec(memory_space=pltpu.VMEM)
    rows = nb * CAP
    n = PlaneGather.copies(shards)
    slots = reps * shards * local * CAP
    outs = pl.pallas_call(
        functools.partial(spread_kernel, nb),
        out_shape=[jax.ShapeDtypeStruct((reps - 1, shards, count, width), bf16)] * 2
        + [jax.ShapeDtypeStruct(w.shape, f32) for w in (wg, wu, wd)] + [jax.ShapeDtypeStruct(gown.shape, f32)],
        in_specs=[any_, any_, any_, any_, v, v, any_, any_, any_, any_],
        input_output_aliases={9: 1},
        out_specs=[any_] * 5 + [v],
        scratch_shapes=[
            pltpu.VMEM((2, nb, count, width), bf16), pltpu.VMEM((2, nb, count, width), bf16),
            pltpu.VMEM(wg.shape, bf16), pltpu.VMEM(wu.shape, bf16), pltpu.VMEM(wd.shape, bf16),
            pltpu.VMEM(wg.shape, f32), pltpu.VMEM(wu.shape, f32), pltpu.VMEM(wd.shape, f32),
            pltpu.VMEM((local, rows, width), bf16), pltpu.VMEM((local, rows, width), bf16), pltpu.VMEM((local, rows, 1), f32),
            pltpu.VMEM((reps - 1, shards, *gown.shape[1:]), f32),
            pltpu.SemaphoreType.DMA((reps - 1, n)), pltpu.SemaphoreType.DMA((reps - 1, n)),
            pltpu.SemaphoreType.DMA((2, 2)), pltpu.SemaphoreType.DMA((3,)), pltpu.SemaphoreType.DMA((3, local)),
            *Spread.semaphores(shards, reps), *Spread.semaphores(shards, reps),
        ],
        compiler_params=pltpu.CompilerParams(vmem_limit_bytes=60 << 20, has_side_effects=True, collective_id=3),
        cost_estimate=pl.CostEstimate(
            flops=12 * slots * width * hidden, transcendentals=slots * hidden, bytes_accessed=4 * reps * shards * count * width
        ),
        name="spread_expert_sums",
    )(xown, cown, xcol, ccol, gown, gcol, wg, wu, wd, coth)
    return outs[0], outs[1], outs[5], outs[2:5]

def rotary_tables(count):
    half = HEAD_SIZE // 2
    inverse = np.exp(np.arange(half) * (-2.0 * math.log(10000.0) / HEAD_SIZE))
    angles = np.tile(np.arange(count)[:, None] * inverse[None, :], (1, LANES // half))
    return np.cos(angles).astype(np.float32), np.sin(angles).astype(np.float32)


def pack_small(w_router, norm_attn, norm_moe):
    small = jnp.concatenate([w_router, norm_attn[:, None], norm_moe[:, None]], axis=1)
    return jnp.pad(small, ((0, 0), (0, LANES - small.shape[1])))


def body(
    tokens, prefix, routes, cotangent, w_query, key_weight, value_weight, w_out,
    norm_attn, norm_moe, w_router, w_gate, w_up, w_down,
):
    count, width = tokens.shape
    local = w_gate.shape[0]
    shards, reps = lax.axis_size("shard"), lax.axis_size("rep")
    experts = local * shards
    kv_width = key_weight.shape[1]
    spread = reps == GATHERED_REPLICAS
    cosine, sine = rotary_tables(count)
    packed_own = (w_query, key_weight, value_weight, w_out, pack_small(w_router, norm_attn, norm_moe))
    packed, cot_own, cot_col, query, keys, values, attended, hidden_one, normed_two, gates, normed_one = front(
        tokens, prefix, routes.T, packed_own, cotangent, cosine, sine, experts, kv_width, spread
    )
    x_own, x_col, gates_own, gates_col, back, d_gates, mixture, cot_oth = moe_own(
        normed_two, gates, cot_own, cot_col, w_gate, w_up, w_down, spread
    )
    mixture = lax.psum_scatter(mixture.reshape(-1, width), "shard", scatter_dimension=0, tiled=True)
    d_tokens, shares = attention_back(
        prefix, tokens, cotangent, cosine, sine, packed, query, keys, values, attended, normed_one, normed_two, hidden_one,
        gates, d_gates.reshape(experts, count), back,
    )
    shares = shares.reshape(width, -1)
    if spread:
        x_own, shares = lax.optimization_barrier((x_own, shares))
        x_oth, cot_oth, gates_oth, sums = moe_spread_sums(
            x_own, cot_own, x_col, cot_col, cot_oth, gates_own, gates_col, w_gate, w_up, w_down
        )
        shares = lax.psum_scatter(shares, "shard", scatter_dimension=0, tiled=True)
        shares, gates_oth = lax.optimization_barrier((shares, gates_oth))
        sums = moe_sums(x_oth, cot_oth, gates_oth, w_gate, w_up, w_down, sums)
    else:
        sums = moe_sums(x_own, cot_own, gates_own, w_gate, w_up, w_down)
        sums = [lax.psum(a.astype(bf16), "rep").astype(f32) for a in sums]
        shares = lax.psum_scatter(shares, "shard", scatter_dimension=0, tiled=True)
    d_w_gate, d_w_up, d_w_down = sums
    totals = lax.psum(shares, "rep").astype(f32)
    cuts = [width, width + kv_width, width + 2 * kv_width, 2 * width + 2 * kv_width]
    d_wq, d_wk, d_wv, d_wo, small = jnp.split(totals, cuts, axis=1)
    result = (hidden_one + mixture.astype(f32)).astype(bf16)
    return (
        result, d_tokens, d_wq, d_wk, d_wv, d_wo, small[:, experts], small[:, experts + 1],
        small[:, :experts], d_w_gate, d_w_up, d_w_down,
    )


def solution(mesh):
    rows = P(("rep", "shard"), None)
    one, two, three = P("shard"), P("shard", None), P("shard", None, None)
    return jax.shard_map(
        body,
        mesh=mesh,
        in_specs=(rows, P(("rep", "shard")), rows, rows, two, two, two, two, one, one, two, three, three, three),
        out_specs=(rows, rows, two, two, two, two, one, one, two, three, three, three),
        check_vma=False,
    )
```
